256 devices in a mesh: dom: 64 (over y, z, core), rep: 4 (over x).
Axes of the slice: x: 4, y: 4, z: 8, core: 2. Of those that a mesh axis runs over, the one named last changes fastest.
Arguments:
- feats: bfloat16 [256, 262144], P('rep', 'dom'), may hold values from -6 to 6
- w_self: bfloat16 [256, 256], P(None, 'rep'), may hold values from -0.375 to 0.375
- w_neigh: bfloat16 [256, 256], P(None, 'rep'), may hold values from -3 to 3
- local_cols: int32 [2048, 2], P('dom'), may hold values from 0 to 31
- local_tiles: bfloat16 [2048, 2, 128, 128], P('dom'), may hold values from 0 to 3, as said below
- send_list: int32 [64, 64, 2], P('dom'), may hold values from 0 to 31
- remote_rows: int32 [64, 64, 2], P('dom'), may hold values from 0 to 31
- remote_tiles: bfloat16 [64, 64, 2, 128, 128], P('dom'), may hold values from 0 to 3, as said below
- cotangent: bfloat16 [256, 262144], P('rep', 'dom'), may hold values from -6 to 6
Outputs:
- output: bfloat16 [256, 262144], P('rep', 'dom')
- grad_feats: bfloat16 [256, 262144], P('rep', 'dom')
- grad_w_self: float32 [256, 256], P(None, 'rep')
- grad_w_neigh: float32 [256, 256], P(None, 'rep')
The draws below stay inside these ranges and needn't reach their ends.
Inputs may be any that keep to these rules, and one draw needn't show every extreme that they name: `local_tiles`: edge weights: zero where a tile has no edge, positive otherwise. `remote_tiles`: edge weights: zero where a tile has no edge, positive otherwise.
All inputs are finite; a program needn't handle non-finite values.
Results may differ from the reference program's by a relative error of at most 0.0055.
Values may be sent and summed in bfloat16 or wider, within the bound.
No kernel may reach another device: no remote copies, remote signals or barrier semaphores. Data moves between devices by JAX's collectives and lax.ppermute only.
A program may use at most 128 MiB of HBM per device.

```python
import math
import jax
import jax.numpy as jnp
from jax import lax

FEAT = 256
TILE = 128
BLK_DEV = 32
LOC = 2
SLOTS = 2
NODES = 262144
N_DOM = 64


def edge_weights(key, shape, density, low_scale):
    keep_key, value_key, scale_key = jax.random.split(key, 3)
    present = (jax.random.uniform(keep_key, shape, dtype=jnp.float32) < density).astype(jnp.float32)
    values = jax.random.uniform(value_key, shape, dtype=jnp.float32, minval=0.25, maxval=1.0)
    row_shape = tuple(shape[:-1]) + (1,)
    row_scale = jnp.exp(jax.random.uniform(scale_key, row_shape, dtype=jnp.float32, minval=math.log(low_scale), maxval=math.log(3.0)))
    return (present * values * row_scale).astype(jnp.bfloat16)


def draw_local_tiles(key, part):
    shape = (NODES // TILE, LOC, TILE, TILE)
    return edge_weights(jax.random.fold_in(key, 11), shape, 0.2, 0.3)


def draw_remote_tiles(key, part):
    shape = (N_DOM, N_DOM, SLOTS, TILE, TILE)
    return edge_weights(jax.random.fold_in(key, 23), shape, 0.2, 0.3)


def plant(result, own_key, least, largest):
    place = [jax.random.randint(jax.random.fold_in(own_key, axis), (), 0, length) for axis, length in enumerate(result.shape)]
    longest = result.shape.index(max(result.shape))
    next_to = place[:longest] + [(place[longest] + 1) % result.shape[longest]] + place[longest + 1:]
    return result.at[tuple(place)].set(least).at[tuple(next_to)].set(largest)


def level_of(key, shape, cuts, least, top_value):
    loudness = 1.0
    for dim, blocks in cuts:
        heights = jax.random.uniform(jax.random.fold_in(jax.random.fold_in(key, 6), dim), (blocks,), jnp.float32, least / len(cuts), top_value / len(cuts))
        loudness = loudness * jnp.repeat(jnp.exp(heights), shape[dim] // blocks).reshape((-1,) + (1,) * (len(shape) - 1 - dim))
    return loudness


def centred(own_key, shape, width, limit, shards=(), kind=jnp.bfloat16):
    gain = level_of(own_key, shape, shards, -0.22, 0.18) if shards else 1.0
    values = jax.random.normal(own_key, shape, jnp.float32) * width * gain
    return jnp.minimum(jnp.maximum(values, -limit), limit).astype(kind)


def setup_inputs(seed: int = 0) -> dict:
    splits = jax.random.split(jax.random.key(seed), 10)
    feats = centred(splits[0], (FEAT, NODES), 1.0, 6.0, ((0, 4), (1, 64)))
    w_self = centred(splits[1], (FEAT, FEAT), FEAT ** -0.5, 0.375, ((1, 4),))
    w_neigh = centred(splits[2], (FEAT, FEAT), (max(FEAT // 64, 1)) ** -0.5, 3.0, ((1, 4),))
    local_cols = plant(jax.random.randint(splits[3], (NODES // TILE, LOC), 0, BLK_DEV), jax.random.fold_in(splits[3], 1), 0, BLK_DEV - 1).astype(jnp.int32)
    local_tiles = draw_local_tiles(jax.random.fold_in(splits[9], 71), 0)
    send_list = plant(jax.random.randint(splits[5], (N_DOM, N_DOM, SLOTS), 0, BLK_DEV), jax.random.fold_in(splits[5], 1), 0, BLK_DEV - 1).astype(jnp.int32)
    remote_rows = plant(jax.random.randint(splits[6], (N_DOM, N_DOM, SLOTS), 0, BLK_DEV), jax.random.fold_in(splits[6], 1), 0, BLK_DEV - 1).astype(jnp.int32)
    remote_tiles = draw_remote_tiles(jax.random.fold_in(splits[9], 71), 0)
    cotangent = centred(splits[8], (FEAT, NODES), 1.0, 6.0, ((0, 4), (1, 64)))
    return dict(feats=feats, w_self=w_self, w_neigh=w_neigh, local_cols=local_cols, local_tiles=local_tiles, send_list=send_list, remote_rows=remote_rows, remote_tiles=remote_tiles, cotangent=cotangent)


def reference(feats, w_self, w_neigh, local_cols, local_tiles, send_list, remote_rows, remote_tiles, cotangent):
    highest = lax.Precision.HIGHEST
    feat_width, node_count = feats.shape
    block_total = node_count // TILE
    blocked = feats.reshape(feat_width, block_total, TILE)
    block_ids = jnp.arange(BLK_DEV, dtype=jnp.int32)
    local_view = local_tiles.reshape(N_DOM, BLK_DEV, LOC, TILE, TILE)
    col_view = local_cols.reshape(N_DOM, BLK_DEV, LOC)
    sender_base = (jnp.arange(N_DOM, dtype=jnp.int32) * BLK_DEV)[:, None]

    def forward_part(part):
        near_tiles = local_view[part].astype(jnp.float32)
        near_cols = (col_view[part] + part * BLK_DEV).astype(jnp.int32)
        gathered = blocked[:, near_cols].astype(jnp.float32)
        summed = jnp.einsum("fblj,blij->fbi", gathered, near_tiles, precision=highest)
        far_tiles = remote_tiles[part].astype(jnp.float32)
        far_blocks = (sender_base + send_list[:, part, :]).astype(jnp.int32)
        incoming = blocked[:, far_blocks].astype(jnp.float32)
        far_terms = jnp.einsum("fskj,skij->fski", incoming, far_tiles, precision=highest)
        placing = (remote_rows[part][:, :, None] == block_ids).astype(jnp.float32)
        summed = summed + jnp.einsum("fski,skb->fbi", far_terms, placing, precision=highest)
        far_sums = jnp.sum(far_tiles, axis=3)
        divisor = 1.0 + jnp.sum(near_tiles, axis=(1, 3)) + jnp.einsum("ski,skb->bi", far_sums, placing, precision=highest)
        return (summed / divisor).astype(jnp.bfloat16), divisor

    aggregates, divisors = lax.map(forward_part, jnp.arange(N_DOM, dtype=jnp.int32))
    aggregate = aggregates.transpose(1, 0, 2, 3).reshape(feat_width, node_count)
    divisor = divisors.reshape(block_total, TILE)

    preact = jnp.dot(w_self.T, feats, preferred_element_type=jnp.float32)
    preact = preact + jnp.dot(w_neigh.T, aggregate, preferred_element_type=jnp.float32)
    sigmoid_val = jax.nn.sigmoid(preact)
    output = (preact * sigmoid_val).astype(jnp.bfloat16)
    slope = sigmoid_val * (1.0 + preact * (1.0 - sigmoid_val))
    grad_pre = (cotangent.astype(jnp.float32) * slope).astype(jnp.bfloat16)
    grad_w_self = jnp.dot(feats, grad_pre.T, preferred_element_type=jnp.float32)
    grad_w_neigh = jnp.dot(aggregate, grad_pre.T, preferred_element_type=jnp.float32)
    back_self = jnp.dot(w_self, grad_pre, preferred_element_type=jnp.float32)
    back_agg = jnp.dot(w_neigh, grad_pre, preferred_element_type=jnp.float32)
    scaled = (back_agg.reshape(feat_width, block_total, TILE) / divisor).astype(jnp.bfloat16)

    def backward_part(part):
        near_tiles = local_view[part].astype(jnp.float32)
        own_rows = lax.dynamic_slice_in_dim(scaled, (part * BLK_DEV).astype(jnp.int32), BLK_DEV, 1).astype(jnp.float32)
        near_back = jnp.einsum("fbi,blij->fblj", own_rows, near_tiles, precision=highest)
        landing = (col_view[part][:, :, None] == block_ids).astype(jnp.float32)
        collected = jnp.einsum("fblj,blc->fcj", near_back, landing, precision=highest)
        far_rows = (sender_base + remote_rows[:, part, :]).astype(jnp.int32)
        picked = scaled[:, far_rows].astype(jnp.float32)
        far_tiles = remote_tiles[:, part].astype(jnp.float32)
        far_back = jnp.einsum("fdki,dkij->fdkj", picked, far_tiles, precision=highest)
        homing = (send_list[part][:, :, None] == block_ids).astype(jnp.float32)
        return collected + jnp.einsum("fdkj,dkc->fcj", far_back, homing, precision=highest)

    edge_parts = lax.map(backward_part, jnp.arange(N_DOM, dtype=jnp.int32))
    edge_grads = edge_parts.transpose(1, 0, 2, 3).reshape(feat_width, node_count)
    grad_feats = (back_self + edge_grads).astype(jnp.bfloat16)
    return output, grad_feats, grad_w_self, grad_w_neigh
```

```python
import jax
import jax.numpy as jnp
from jax import lax
from jax.experimental import pallas as pl
from jax.experimental.pallas import tpu as pltpu
from jax.sharding import PartitionSpec as P

TILE = 128
STEP = 8
VMEM_BYTES = 40 * 1024 * 1024
F32 = jnp.float32
BF16 = jnp.bfloat16


def whole(shape):
    return pl.BlockSpec(shape, lambda *_: (0,) * len(shape))


def lanes(index, width):
    return pl.ds(pl.multiple_of(index * width, width), width)


def params():
    return pltpu.CompilerParams(vmem_limit_bytes=VMEM_BYTES)


def cost(flops, nbytes):
    return pl.CostEstimate(flops=flops, bytes_accessed=nbytes, transcendentals=0)


def call(body, args, prefetch, grid, in_specs, out_shape, out_specs, scratch=(), aliases=None, flops=0, nbytes=1 << 20):
    return pl.pallas_call(
        body,
        grid_spec=pltpu.PrefetchScalarGridSpec(
            num_scalar_prefetch=prefetch, grid=grid, in_specs=in_specs, out_specs=out_specs, scratch_shapes=scratch
        ),
        out_shape=out_shape,
        input_output_aliases=aliases or {},
        compiler_params=params(),
        cost_estimate=cost(flops, nbytes),
    )(*args)


def shape(dims, kind):
    return jax.ShapeDtypeStruct(dims, kind)


def dot(left, right, left_dim, right_dim):
    return lax.dot_general(left, right, (((left_dim,), (right_dim,)), ((), ())), preferred_element_type=F32)


def pick_body(send_ref, feats_ref, out_ref):
    step = pl.program_id(0)
    chans = feats_ref.shape[0]
    for item in range(STEP):
        for slot in range(2):
            block = send_ref[step * STEP + item, slot]
            out_ref[item, slot * chans : (slot + 1) * chans, :] = feats_ref[:, lanes(block, TILE)]


def chunk_body(rep_ref, feats_ref, cot_ref, *outs):
    reps = len(outs) // 2
    width = outs[0].shape[1]
    for k in range(reps):
        chunk = lax.rem(rep_ref[0] + k, reps)
        outs[k][...] = feats_ref[:, lanes(chunk, width)]
        outs[reps + k][...] = cot_ref[:, lanes(chunk, width)]


def near_body(cols_ref, rows_ref, feats_ref, near_ref, far_ref, acc_ref, div_ref):
    step = pl.program_id(0)
    ones = jnp.ones((8, TILE), BF16)
    near_blocks = near_ref.shape[0]

    @pl.when(step == 0)
    def _():
        div_ref[...] = jnp.ones_like(div_ref)

    for item in range(near_blocks):
        row = step * near_blocks + item
        total = None
        sums = None
        for link in range(2):
            tile = near_ref[item, link]
            block = feats_ref[:, lanes(cols_ref[row, link], TILE)]
            term = dot(block, tile, 1, 1)
            part = dot(ones, tile, 1, 1)
            total = term if total is None else total + term
            sums = part if sums is None else sums + part
        acc_ref[:, lanes(row, TILE)] = total
        div_ref[:, lanes(row, TILE)] += sums
    for item in range(STEP):
        for slot in range(2):
            row = rows_ref[step * STEP + item, slot]
            div_ref[:, lanes(row, TILE)] += dot(ones, far_ref[item, slot], 1, 1)


def far_body(rep_ref, rows_ref, got_ref, far_ref, near_acc_ref, div_ref, *rest):
    outs, acc_ref = rest[:-1], rest[-1]
    step = pl.program_id(0)
    reps = len(outs)
    chans = acc_ref.shape[0]
    width = outs[0].shape[1]

    @pl.when(step == 0)
    def _():
        acc_ref[...] = near_acc_ref[...]

    for item in range(STEP):
        for slot in range(2):
            row = rows_ref[step * STEP + item, slot]
            block = got_ref[item, slot * chans : (slot + 1) * chans, :]
            acc_ref[:, lanes(row, TILE)] += dot(block, far_ref[item, slot], 1, 1)

    @pl.when(step == pl.num_programs(0) - 1)
    def _():
        for k in range(reps):
            chunk = lax.rem(rep_ref[0] + k, reps)
            where = lanes(chunk, width)
            outs[k][...] = (acc_ref[:, where] / div_ref[0:1, where]).astype(BF16)


def gather_rows(ref, pieces, rep):
    reps = len(pieces)
    rows = pieces[0].shape[0]
    for k in range(reps):
        source = lax.rem(rep + reps - k, reps)
        ref[lanes(source, rows), :] = pieces[k][...]


def dense_body(rep_ref, *refs):
    agg, feats, cot, wts = refs[0:4], refs[4:8], refs[8:12], refs[12:16]
    div_ref = refs[16]
    scaled_out, out_out = refs[17:21], refs[21:25]
    grad_ref, back_ref, full_feats, full_agg = refs[25:29]
    rep = rep_ref[0]
    reps = 4
    rows, width = agg[0].shape
    gather_rows(full_feats, feats, rep)
    gather_rows(full_agg, agg, rep)
    for k in range(reps):
        preact = dot(wts[k][0], full_feats[...], 1, 0) + dot(wts[k][1], full_agg[...], 1, 0)
        gate = jax.nn.sigmoid(preact)
        out_out[k][...] = (preact * gate).astype(BF16)
        slope = gate * (1.0 + preact * (1.0 - gate))
        grad_ref[k * rows : (k + 1) * rows, :] = (cot[k][...].astype(F32) * slope).astype(BF16)
    w_neigh = jnp.concatenate([wts[k][1] for k in range(reps)], axis=0)
    back_ref[...] = dot(w_neigh, grad_ref[...], 0, 0)
    div = div_ref[0:1, lanes(rep, width)]
    for k in range(reps):
        target = lax.rem(rep + k, reps)
        scaled_out[k][...] = (back_ref[lanes(target, rows), :] / div).astype(BF16)


def weight_body(rep_ref, *refs):
    agg, feats, wts = refs[0:4], refs[4:8], refs[8:12]
    grad_ref = refs[12]
    back_out = refs[13:17]
    slices_ref, back_ref, full, prod_ref = refs[17:21]
    rep = rep_ref[0]
    reps = 4
    rows = agg[0].shape[0]
    for which, pieces in ((0, feats), (1, agg)):
        gather_rows(full, pieces, rep)
        prod_ref[...] = dot(grad_ref[...], full[...], 1, 1)
        for group in range(rows // 4):
            for half in range(2):
                index = which * 32 + group * 2 + half
                for k in range(reps):
                    start = k * rows + group * 4
                    slices_ref[index, 4 * k : 4 * k + 4, :] = prod_ref[
                        start : start + 4, half * TILE : (half + 1) * TILE
                    ].astype(BF16)
    w_self = jnp.concatenate([wts[k][0] for k in range(reps)], axis=0)
    back_ref[...] = dot(w_self, grad_ref[...], 0, 0)
    for k in range(reps):
        target = lax.rem(rep + k, reps)
        back_out[k][...] = back_ref[lanes(target, rows), :]


def slice_sum_body(got_ref, *outs):
    total = jnp.sum(got_ref[...].astype(F32), axis=0)
    for k in range(len(outs)):
        outs[k][...] = total[4 * k : 4 * k + 4, :]


def slice_send_body(*refs):
    parts, out_ref = refs[:4], refs[-1]
    total = parts[0][...] + parts[1][...] + parts[2][...] + parts[3][...]
    high = total.astype(BF16)
    low = (total - high.astype(F32)).astype(BF16)
    both = jnp.concatenate([high.astype(F32), low.astype(F32)], axis=0).astype(BF16)
    out_ref[...] = jnp.broadcast_to(both[None], out_ref.shape)


def gather_lanes(ref, pieces, rep):
    reps = len(pieces)
    width = pieces[0].shape[1]
    for k in range(reps):
        source = lax.rem(rep + reps - k, reps)
        ref[:, lanes(source, width)] = pieces[k][...]


def far_back_body(rep_ref, rows_ref, s0, s1, s2, s3, far_ref, out_ref, full_ref):
    step = pl.program_id(0)
    chans = full_ref.shape[0]

    @pl.when(step == 0)
    def _():
        gather_lanes(full_ref, (s0, s1, s2, s3), rep_ref[0])

    for item in range(STEP):
        for slot in range(2):
            row = rows_ref[step * STEP + item, slot]
            term = dot(full_ref[:, lanes(row, TILE)], far_ref[item, slot], 1, 0)
            out_ref[item, slot * chans : (slot + 1) * chans, :] = term.astype(BF16)


def near_back_body(rep_ref, cols_ref, *refs):
    scaled, back, outs = refs[0:4], refs[4:8], refs[8:12]
    near_ref, acc_ref, output_ref, full_ref = refs[12:16]
    rep = rep_ref[0]
    reps = 4
    width = scaled[0].shape[1]
    gather_lanes(full_ref, scaled, rep)
    gather_lanes(acc_ref, back, rep)
    for k in range(reps):
        output_ref[:, lanes(lax.rem(rep + k, reps), width)] = outs[k][...]
    for row in range(near_ref.shape[0]):
        for link in range(2):
            term = dot(full_ref[:, row * TILE : (row + 1) * TILE], near_ref[row, link], 1, 0)
            acc_ref[:, lanes(cols_ref[row, link], TILE)] += term


def home_body(send_ref, got_ref, near_acc_ref, grad_ref, weight_ref, acc_ref):
    step = pl.program_id(0)
    chans = acc_ref.shape[0]

    @pl.when(step == 0)
    def _():
        acc_ref[...] = near_acc_ref[...]

    for item in range(STEP):
        for slot in range(2):
            block = send_ref[step * STEP + item, slot]
            acc_ref[:, lanes(block, TILE)] += got_ref[item, slot * chans : (slot + 1) * chans, :].astype(F32)
        both = got_ref[item, 2 * chans : 2 * chans + 8, :].astype(F32)
        group, half = item // 2, item % 2
        weight_ref[4 * group : 4 * group + 4, half * TILE : (half + 1) * TILE] = both[0:4] + both[4:8]

    @pl.when(step == pl.num_programs(0) - 1)
    def _():
        grad_ref[...] = acc_ref[...].astype(BF16)


def local(feats, w_self, w_neigh, local_cols, local_tiles, send_list, remote_rows, remote_tiles, cotangent):
    chans, nodes = feats.shape
    full = w_self.shape[0]
    reps = full // chans
    width = nodes // reps
    parts = remote_tiles.shape[1]
    blocks = local_tiles.shape[0]
    steps = parts // STEP
    far_tiles = remote_tiles[0]
    far_rows = remote_rows[0]
    sends = send_list[0]
    rep = lax.axis_index("rep").astype(jnp.int32).reshape(1)
    piece = shape((chans, width), BF16)
    piece32 = shape((chans, width), F32)
    piece_spec = whole((chans, width))
    wide_spec = whole((chans, nodes))
    tile_spec = pl.BlockSpec((STEP, 2, TILE, TILE), lambda i, *_: (i, 0, 0, 0))
    far_flops = 2 * parts * 2 * chans * TILE * TILE
    far_bytes = far_tiles.size * 2

    def shift(value, by):
        return lax.ppermute(value, "rep", [(i, (i + by) % reps) for i in range(reps)])

    def exchange(pieces, sign=1):
        return [pieces[0]] + [shift(pieces[k], (sign * k) % reps) for k in range(1, reps)]

    with jax.named_scope("pick"):
        outgoing = call(
            pick_body, (sends, feats), 1, (steps,), [wide_spec],
            shape((parts, 2 * chans, TILE), BF16), pl.BlockSpec((STEP, 2 * chans, TILE), lambda i, *_: (i, 0, 0)),
            nbytes=3 << 20,
        )
    incoming = lax.all_to_all(outgoing, "dom", split_axis=0, concat_axis=0, tiled=True)

    with jax.named_scope("chunks"):
        pieces = call(
            chunk_body, (rep, feats, cotangent), 1, (1,), [wide_spec, wide_spec],
            [piece] * (2 * reps), [piece_spec] * (2 * reps), nbytes=2 << 20,
        )
    feats_in = exchange(pieces[:reps])
    cot_in = exchange(pieces[reps:])
    weights = jnp.stack([w_self.T, w_neigh.T])
    weights_in = exchange([weights] * reps)
    weight_spec = whole(weights.shape)

    with jax.named_scope("near"):
        near_acc, div = call(
            near_body, (local_cols, far_rows, feats, local_tiles, far_tiles), 2, (steps,),
            [wide_spec, pl.BlockSpec((blocks // steps, 2, TILE, TILE), lambda i, *_: (i, 0, 0, 0)), tile_spec],
            [shape((chans, nodes), F32), shape((8, nodes), F32)], [wide_spec, whole((8, nodes))],
            flops=far_flops, nbytes=far_bytes * 2,
        )
    with jax.named_scope("far"):
        agg = call(
            far_body, (rep, far_rows, incoming, far_tiles, near_acc, div), 2, (steps,),
            [pl.BlockSpec((STEP, 2 * chans, TILE), lambda i, *_: (i, 0, 0)), tile_spec, wide_spec, whole((8, nodes))],
            [piece] * reps, [piece_spec] * reps, [pltpu.VMEM((chans, nodes), F32)],
            flops=far_flops, nbytes=far_bytes * 2,
        )
    agg_in = exchange(agg)

    with jax.named_scope("dense"):
        dense = call(
            dense_body, (rep, *agg_in, *feats_in, *cot_in, *weights_in, div), 1, (1,),
            [piece_spec] * (3 * reps) + [weight_spec] * reps + [whole((8, nodes))],
            [piece] * (2 * reps) + [shape((full, width), BF16)],
            [piece_spec] * (2 * reps) + [whole((full, width))],
            [pltpu.VMEM((full, width), F32), pltpu.VMEM((full, width), BF16), pltpu.VMEM((full, width), BF16)],
            flops=6 * full * full * width, nbytes=3 << 20,
        )
    scaled, out_pieces, grad_pre = dense[:reps], dense[reps : 2 * reps], dense[2 * reps]
    scaled_in = exchange(scaled)

    with jax.named_scope("weights"):
        weight_out = call(
            weight_body, (rep, *agg_in, *feats_in, *weights_in, grad_pre), 1, (1,),
            [piece_spec] * (2 * reps) + [weight_spec] * reps + [whole((full, width))],
            [piece32] * reps + [shape((parts, 4 * reps, TILE), BF16)],
            [piece_spec] * reps + [whole((parts, 4 * reps, TILE))],
            [pltpu.VMEM((full, width), F32), pltpu.VMEM((full, width), BF16), pltpu.VMEM((full, full), F32)],
            flops=6 * full * full * width, nbytes=3 << 20,
        )
    back_self, slices = weight_out[:reps], weight_out[reps]
    slices_in = lax.all_to_all(slices, "dom", split_axis=0, concat_axis=0, tiled=True)
    with jax.named_scope("slice_sum"):
        sums = call(
            slice_sum_body, (slices_in,), 0, (1,), [whole(slices.shape)],
            [shape((4, TILE), F32)] * reps, [whole((4, TILE))] * reps,
        )
    sums_in = exchange(sums, -1)

    with jax.named_scope("far_back"):
        far_back = call(
            far_back_body, (rep, far_rows, *scaled_in, far_tiles), 2, (steps,),
            [piece_spec] * reps + [tile_spec],
            shape((parts, 2 * chans + 8, TILE), BF16),
            pl.BlockSpec((STEP, 2 * chans + 8, TILE), lambda i, *_: (i, 0, 0)),
            [pltpu.VMEM((chans, nodes), BF16)],
            flops=far_flops, nbytes=far_bytes * 2,
        )
    with jax.named_scope("slice_send"):
        sending = call(
            slice_send_body, (*sums_in, far_back), 0, (1,),
            [whole((4, TILE))] * reps + [pl.BlockSpec(memory_space=pl.ANY)],
            shape(far_back.shape, BF16),
            pl.BlockSpec((parts, 8, TILE), lambda i: (0, 2 * chans // 8, 0)),
            aliases={reps: 0},
        )
    returned = lax.all_to_all(sending, "dom", split_axis=0, concat_axis=0, tiled=True)

    back_in = exchange(back_self)
    out_in = exchange(out_pieces, -1)
    with jax.named_scope("near_back"):
        near_back, output = call(
            near_back_body, (rep, local_cols, *scaled_in, *back_in, *out_in, local_tiles), 2, (1,),
            [piece_spec] * (3 * reps) + [whole(local_tiles.shape)],
            [shape((chans, nodes), F32), shape((chans, nodes), BF16)], [wide_spec, wide_spec],
            [pltpu.VMEM((chans, nodes), BF16)],
            flops=far_flops // 2, nbytes=far_bytes,
        )
    with jax.named_scope("home"):
        grad_feats, weight_grads = call(
            home_body, (sends, returned, near_back), 1, (steps,),
            [pl.BlockSpec((STEP, 2 * chans + 8, TILE), lambda i, *_: (i, 0, 0)), wide_spec],
            [shape((chans, nodes), BF16), shape((2 * chans, full), F32)],
            [wide_spec, pl.BlockSpec((2 * STEP, full), lambda i, *_: (i, 0))],
            [pltpu.VMEM((chans, nodes), F32)],
            nbytes=4 << 20,
        )
    return output, grad_feats, weight_grads[:chans].T, weight_grads[chans:].T


def solution(mesh):
    placed = (
        P("rep", "dom"),
        P(None, "rep"),
        P(None, "rep"),
        P("dom", None),
        P("dom", None, None, None),
        P("dom", None, None),
        P("dom", None, None),
        P("dom", None, None, None, None),
        P("rep", "dom"),
    )
    return jax.shard_map(
        local,
        mesh=mesh,
        in_specs=placed,
        out_specs=(P("rep", "dom"), P("rep", "dom"), P(None, "rep"), P(None, "rep")),
        check_vma=False,
    )
```

```python
import jax
import jax.numpy as jnp
from jax import lax
from jax.experimental import pallas as pl
from jax.experimental.pallas import tpu as pltpu
from jax.sharding import PartitionSpec as P

TILE = 128
STEP = 8
VMEM_BYTES = 12 * 1024 * 1024
F32 = jnp.float32
BF16 = jnp.bfloat16
IN_VMEM = pl.BlockSpec(memory_space=pltpu.VMEM)
IN_SMEM = pl.BlockSpec(memory_space=pltpu.SMEM)
IN_HBM = pl.BlockSpec(memory_space=pltpu.HBM)


def lanes(index, width):
    return pl.ds(pl.multiple_of(index * width, width), width)


def call(body, scalars, args, out_shape, scratch=(), micros=1.0, hbm=(), hbm_out=()):
    many = isinstance(out_shape, list)
    out_specs = [IN_HBM if i in hbm_out else IN_VMEM for i in range(len(out_shape) if many else 1)]
    out_specs = out_specs if many else out_specs[0]
    args = [pinned(arg) if i in hbm else arg for i, arg in enumerate(args)]
    return pl.pallas_call(
        body,
        in_specs=[IN_SMEM] * len(scalars) + [IN_HBM if i in hbm else IN_VMEM for i in range(len(args))],
        out_shape=out_shape,
        out_specs=out_specs,
        scratch_shapes=scratch,
        compiler_params=pltpu.CompilerParams(vmem_limit_bytes=VMEM_BYTES),
        cost_estimate=pl.CostEstimate(flops=int(micros * 1.1e9), bytes_accessed=1 << 16, transcendentals=0),
    )(*scalars, *args)


def shape(dims, kind):
    return jax.ShapeDtypeStruct(dims, kind)


def in_hbm(dims, kind):
    return pltpu.HBM(dims, kind)


def pinned(value):
    return pltpu.with_memory_space_constraint(value, pltpu.HBM)


def dot(left, right, left_dim, right_dim):
    return lax.dot_general(left, right, (((left_dim,), (right_dim,)), ((), ())), preferred_element_type=F32)


def pick_body(send_ref, feats_hbm, out_ref, feats_ref, buf_ref, sems, feats_sem):
    chans = feats_ref.shape[0]
    load = pltpu.make_async_copy(feats_hbm, feats_ref, feats_sem)
    load.start()
    load.wait()
    parts = buf_ref.shape[0]
    for step in range(parts // STEP):
        for item in range(step * STEP, (step + 1) * STEP):
            for slot in range(2):
                block = send_ref[slot, item]
                buf_ref[item, slot * chans : (slot + 1) * chans, :] = feats_ref[:, lanes(block, TILE)]
        rows = pl.ds(step * STEP, STEP)
        pltpu.make_async_copy(buf_ref.at[rows], out_ref.at[rows], sems.at[step]).start()
    for step in range(parts // STEP):
        rows = pl.ds(step * STEP, STEP)
        pltpu.make_async_copy(buf_ref.at[rows], out_ref.at[rows], sems.at[step]).wait()


def tile_copy(far_hbm, far_ref, sems, step):
    rows = pl.ds(step * STEP, STEP)
    return pltpu.make_async_copy(far_hbm.at[rows], far_ref.at[rows], sems.at[step])


def chunk_body(rep_ref, feats_ref, cot_ref, *outs):
    reps = len(outs) // 2
    width = outs[0].shape[1]
    for k in range(reps):
        chunk = lax.rem(rep_ref[0] + k, reps)
        outs[k][...] = feats_ref[:, lanes(chunk, width)]
        outs[reps + k][...] = cot_ref[:, lanes(chunk, width)]


def near_body(cols_ref, rows_ref, feats_ref, near_ref, far_ref, acc_ref, div_ref):
    ones = jnp.ones((8, TILE), BF16)
    div_ref[...] = jnp.ones_like(div_ref)

    @pl.loop(0, near_ref.shape[0] // 4)
    def _(step):
        for item in range(4):
            row = step * 4 + item
            total = None
            sums = None
            for link in range(2):
                tile = near_ref[row, link]
                term = dot(feats_ref[:, lanes(cols_ref[link, row], TILE)], tile, 1, 1)
                part = dot(ones, tile, 1, 1)
                total = term if total is None else total + term
                sums = part if sums is None else sums + part
            acc_ref[:, lanes(row, TILE)] = total
            div_ref[:, lanes(row, TILE)] += sums

    @pl.loop(0, far_ref.shape[0] // STEP)
    def _(step):
        for item in range(STEP):
            for slot in range(2):
                part = step * STEP + item
                row = rows_ref[slot, part]
                div_ref[:, lanes(row, TILE)] += dot(ones, far_ref[part, slot], 1, 1)


def far_body(rep_ref, rows_ref, got_ref, far_hbm, near_acc_hbm, div_hbm, *rest):
    outs = rest[:4]
    acc_ref, far_ref, div_ref, sems, acc_sem, div_sem = rest[4:]
    reps = len(outs)
    chans = acc_ref.shape[0]
    width = outs[0].shape[1]
    load_acc = pltpu.make_async_copy(near_acc_hbm, acc_ref, acc_sem)
    load_div = pltpu.make_async_copy(div_hbm, div_ref, div_sem)
    load_acc.start()
    for step in range(far_ref.shape[0] // STEP):
        tile_copy(far_hbm, far_ref, sems, step).start()
    load_div.start()
    load_acc.wait()

    @pl.loop(0, far_ref.shape[0] // STEP)
    def _(step):
        tile_copy(far_hbm, far_ref, sems, step).wait()
        for item in range(STEP):
            for slot in range(2):
                part = step * STEP + item
                row = rows_ref[slot, part]
                block = got_ref[part, slot * chans : (slot + 1) * chans, :]
                acc_ref[:, lanes(row, TILE)] += dot(block, far_ref[part, slot], 1, 1)

    load_div.wait()
    for k in range(reps):
        where = lanes(lax.rem(rep_ref[0] + k, reps), width)
        outs[k][...] = (acc_ref[:, where] / div_ref[0:1, where]).astype(BF16)


def gather_rows(ref, pieces, rep):
    reps = len(pieces)
    rows = pieces[0].shape[0]
    for k in range(reps):
        source = lax.rem(rep + reps - k, reps)
        ref[lanes(source, rows), :] = pieces[k][...]


def dense_body(rep_ref, *refs):
    agg, feats, cot, wts = refs[0:4], refs[4:8], refs[8:12], refs[12:16]
    div_ref = refs[16]
    scaled_out, out_out, grad_hbm, slices_hbm = refs[17:21], refs[21:25], refs[25], refs[26]
    back_ref, full_feats, full_agg, grad_ref, out_buf, prod_ref, slices_ref = refs[27:34]
    out_sems, grad_sem, slices_sem = refs[34:37]
    rep = rep_ref[0]
    reps = 4
    rows, width = agg[0].shape
    gather_rows(full_feats, feats, rep)
    gather_rows(full_agg, agg, rep)
    copies = []

    def leave(source, target, sem):
        copies.append(pltpu.make_async_copy(source, target, sem))
        copies[-1].start()

    for k in range(reps):
        preact = dot(wts[k][0], full_feats[...], 1, 0) + dot(wts[k][1], full_agg[...], 1, 0)
        gate = jax.nn.sigmoid(preact)
        slope = gate * (1.0 + preact * (1.0 - gate))
        grad_ref[k * rows : (k + 1) * rows, :] = (cot[k][...].astype(F32) * slope).astype(BF16)
        out_buf[k] = (preact * gate).astype(BF16)
        leave(out_buf.at[k], out_out[k], out_sems.at[k])
    leave(grad_ref, grad_hbm, grad_sem)
    for which, full in ((0, full_feats), (1, full_agg)):
        prod_ref[...] = dot(grad_ref[...], full[...], 1, 1)
        for group in range(rows // 4):
            for half in range(2):
                index = which * 32 + group * 2 + half
                for k in range(reps):
                    start = k * rows + group * 4
                    slices_ref[index, 4 * k : 4 * k + 4, :] = prod_ref[
                        start : start + 4, half * TILE : (half + 1) * TILE
                    ].astype(BF16)
    leave(slices_ref, slices_hbm, slices_sem)
    w_neigh = jnp.concatenate([wts[k][1] for k in range(reps)], axis=0)
    back_ref[...] = dot(w_neigh, grad_ref[...], 0, 0)
    div = div_ref[0:1, lanes(rep, width)]
    for k in range(reps):
        target = lax.rem(rep + k, reps)
        scaled_out[k][...] = (back_ref[lanes(target, rows), :] / div).astype(BF16)
    for copy in copies:
        copy.wait()


def back_body(rep_ref, *refs):
    wts, grad_ref, back_out, back_ref = refs[0:4], refs[4], refs[5:9], refs[9]
    rep = rep_ref[0]
    reps = 4
    rows = back_out[0].shape[0]
    w_self = jnp.concatenate([wts[k][0] for k in range(reps)], axis=0)
    back_ref[...] = dot(w_self, grad_ref[...], 0, 0)
    for k in range(reps):
        target = lax.rem(rep + k, reps)
        back_out[k][...] = back_ref[lanes(target, rows), :]


def slice_sum_body(got_ref, *outs):
    total = jnp.sum(got_ref[...].astype(F32), axis=0)
    for k in range(len(outs)):
        outs[k][...] = total[4 * k : 4 * k + 4, :]


def slice_send_body(*refs):
    parts, out_ref = refs[:4], refs[-1]
    total = parts[0][...] + parts[1][...] + parts[2][...] + parts[3][...]
    high = total.astype(BF16)
    low = (total - high.astype(F32)).astype(BF16)
    both = jnp.concatenate([high.astype(F32), low.astype(F32)], axis=0).astype(BF16)
    out_ref[...] = jnp.broadcast_to(both[None], out_ref.shape)


def gather_lanes(ref, pieces, rep):
    reps = len(pieces)
    width = pieces[0].shape[1]
    for k in range(reps):
        source = lax.rem(rep + reps - k, reps)
        ref[:, lanes(source, width)] = pieces[k][...]


def far_back_body(rep_ref, rows_ref, s0, s1, s2, s3, far_hbm, out_ref, full_ref, buf_ref, far_ref, sems, out_sems):
    chans = full_ref.shape[0]
    parts = far_ref.shape[0]
    for step in range(parts // STEP):
        tile_copy(far_hbm, far_ref, sems, step).start()
    gather_lanes(full_ref, (s0, s1, s2, s3), rep_ref[0])

    def copy(step):
        rows = pl.ds(step * STEP, STEP)
        return pltpu.make_async_copy(
            buf_ref.at[rows], out_ref.at[rows, pl.ds(0, 2 * chans)], out_sems.at[step]
        )

    @pl.loop(0, parts // STEP)
    def _(step):
        tile_copy(far_hbm, far_ref, sems, step).wait()
        for item in range(STEP):
            for slot in range(2):
                part = step * STEP + item
                row = rows_ref[slot, part]
                term = dot(full_ref[:, lanes(row, TILE)], far_ref[part, slot], 1, 0)
                buf_ref[part, slot * chans : (slot + 1) * chans, :] = term.astype(BF16)
        copy(step).start()

    for step in range(parts // STEP):
        copy(step).wait()


def near_back_body(rep_ref, cols_ref, *refs):
    scaled, back, outs = refs[0:4], refs[4:8], refs[8:12]
    near_ref, acc_ref, output_ref, full_ref = refs[12:16]
    rep = rep_ref[0]
    reps = 4
    width = scaled[0].shape[1]
    gather_lanes(full_ref, scaled, rep)
    gather_lanes(acc_ref, back, rep)
    for k in range(reps):
        output_ref[:, lanes(lax.rem(rep + k, reps), width)] = outs[k][...]

    @pl.loop(0, near_ref.shape[0] // 4)
    def _(step):
        for item in range(4):
            row = step * 4 + item
            for link in range(2):
                term = dot(full_ref[:, lanes(row, TILE)], near_ref[row, link], 1, 0)
                acc_ref[:, lanes(cols_ref[link, row], TILE)] += term


def home_body(send_ref, got_ref, near_acc_hbm, grad_ref, w_self_ref, w_neigh_ref, acc_ref, near_acc_ref, sem):
    chans = acc_ref.shape[0]
    parts = got_ref.shape[0]
    load = pltpu.make_async_copy(near_acc_hbm, near_acc_ref, sem)
    load.start()
    acc_ref[...] = jnp.zeros_like(acc_ref)
    for item in range(parts):
        for slot in range(2):
            block = send_ref[slot, item]
            acc_ref[:, lanes(block, TILE)] += got_ref[item, slot * chans : (slot + 1) * chans, :].astype(F32)
        both = got_ref[item, 2 * chans : 2 * chans + 8, :].astype(F32)
        weight_ref = (w_self_ref, w_neigh_ref)[item // (parts // 2)]
        group, half = item % (parts // 2) // 2, item % 2
        weight_ref[4 * group : 4 * group + 4, half * TILE : (half + 1) * TILE] = both[0:4] + both[4:8]
    load.wait()
    grad_ref[...] = (near_acc_ref[...] + acc_ref[...]).astype(BF16)


def local(feats, w_self, w_neigh, local_cols, local_tiles, send_list, remote_rows, remote_tiles, cotangent):
    chans, nodes = feats.shape
    full = w_self.shape[0]
    reps = full // chans
    width = nodes // reps
    parts = remote_tiles.shape[1]
    far_tiles = remote_tiles[0]
    rows = remote_rows[0].T
    sends = send_list[0].T
    cols = local_cols.T
    rep = lax.axis_index("rep").astype(jnp.int32).reshape(1)
    piece = shape((chans, width), BF16)
    piece32 = shape((chans, width), F32)
    sems = pltpu.SemaphoreType.DMA((parts // STEP,))
    sem = pltpu.SemaphoreType.DMA(())
    tile_buf = pltpu.VMEM(far_tiles.shape, BF16)
    wide32 = pltpu.VMEM((chans, nodes), F32)

    def shift(value, by):
        return lax.ppermute(value, "rep", [(i, (i + by) % reps) for i in range(reps)])

    def exchange(pieces, sign=1):
        return [pieces[0]] + [shift(pieces[k], (sign * k) % reps) for k in range(1, reps)]

    with jax.named_scope("pick"):
        outgoing = call(
            pick_body, (sends,), (feats,), in_hbm((parts, 2 * chans, TILE), BF16),
            [pltpu.VMEM((chans, nodes), BF16), pltpu.VMEM((parts, 2 * chans, TILE), BF16), sems, sem], 2.0, (0,), (0,),
        )
    incoming = lax.all_to_all(outgoing, "dom", split_axis=0, concat_axis=0, tiled=True)

    with jax.named_scope("chunks"):
        pieces = call(chunk_body, (rep,), (feats, cotangent), [piece] * (2 * reps))
    feats_in = exchange(pieces[:reps])
    cot_in = exchange(pieces[reps:])
    weights_in = exchange([jnp.stack([w_self.T, w_neigh.T])] * reps)
    with jax.named_scope("near"):
        near_acc, div = call(
            near_body, (cols, rows), (feats, local_tiles, far_tiles),
            [shape((chans, nodes), F32), shape((8, nodes), F32)], (), 6.0,
        )
    incoming, feats_in, cot_in, weights_in, near_acc, div = lax.optimization_barrier(
        (incoming, feats_in, cot_in, weights_in, near_acc, div)
    )
    with jax.named_scope("far"):
        agg = call(
            far_body, (rep, rows), (incoming, far_tiles, near_acc, div), [piece] * reps,
            [wide32, tile_buf, pltpu.VMEM((8, nodes), F32), sems, sem, sem], 6.0, (1, 2, 3),
        )
    agg_in = exchange(agg)

    with jax.named_scope("dense"):
        dense = call(
            dense_body, (rep,), (*agg_in, *feats_in, *cot_in, *weights_in, div),
            [piece] * reps
            + [in_hbm((chans, width), BF16)] * reps
            + [in_hbm((full, width), BF16), in_hbm((parts, 4 * reps, TILE), BF16)],
            [
                pltpu.VMEM((full, width), F32), pltpu.VMEM((full, width), BF16), pltpu.VMEM((full, width), BF16),
                pltpu.VMEM((full, width), BF16), pltpu.VMEM((reps, chans, width), BF16), pltpu.VMEM((full, full), F32),
                pltpu.VMEM((parts, 4 * reps, TILE), BF16), pltpu.SemaphoreType.DMA((reps,)), sem, sem,
            ],
            3.0, (), range(reps, 2 * reps + 2),
        )
    scaled, out_pieces, grad_pre, slices = dense[:reps], dense[reps : 2 * reps], dense[2 * reps], dense[2 * reps + 1]
    scaled_in = exchange(scaled)
    slices_in = lax.all_to_all(slices, "dom", split_axis=0, concat_axis=0, tiled=True)
    with jax.named_scope("far_back"):
        far_back = call(
            far_back_body, (rep, rows), (*scaled_in, far_tiles), in_hbm((parts, 2 * chans + 8, TILE), BF16),
            [
                pltpu.VMEM((chans, nodes), BF16), pltpu.VMEM((parts, 2 * chans, TILE), BF16), tile_buf, sems, sems,
            ],
            5.0, (reps,), (0,),
        )
    with jax.named_scope("slice_sum"):
        sums = call(slice_sum_body, (), (slices_in,), [shape((4, TILE), F32)] * reps)
    sums_in = exchange(sums, -1)
    with jax.named_scope("slice_send"):
        sending = pl.pallas_call(
            slice_send_body,
            grid=(1,),
            in_specs=[IN_VMEM] * reps + [IN_HBM],
            out_shape=in_hbm(far_back.shape, BF16),
            out_specs=pl.BlockSpec((parts, 8, TILE), lambda i: (0, 2 * chans // 8, 0)),
            input_output_aliases={reps: 0},
            compiler_params=pltpu.CompilerParams(vmem_limit_bytes=VMEM_BYTES),
        )(*sums_in, pinned(far_back))
    returned = lax.all_to_all(sending, "dom", split_axis=0, concat_axis=0, tiled=True)

    with jax.named_scope("back"):
        back_self = call(
            back_body, (rep,), (*weights_in, grad_pre), [piece32] * reps, [pltpu.VMEM((full, width), F32)], 1.0
        )
    back_in = exchange(back_self)
    out_in = exchange(out_pieces, -1)
    with jax.named_scope("near_back"):
        near_back, output = call(
            near_back_body, (rep, cols), (*scaled_in, *back_in, *out_in, local_tiles),
            [shape((chans, nodes), F32), shape((chans, nodes), BF16)], [pltpu.VMEM((chans, nodes), BF16)], 2.0,
        )
    with jax.named_scope("home"):
        grad_feats, wg_self, wg_neigh = call(
            home_body, (sends,), (returned, near_back),
            [shape((chans, nodes), BF16), shape((chans, full), F32), shape((chans, full), F32)],
            [wide32, wide32, sem], 3.0, (1,),
        )
    return output, grad_feats, wg_self.T, wg_neigh.T


def solution(mesh):
    placed = (
        P("rep", "dom"),
        P(None, "rep"),
        P(None, "rep"),
        P("dom", None),
        P("dom", None, None, None),
        P("dom", None, None),
        P("dom", None, None),
        P("dom", None, None, None, None),
        P("rep", "dom"),
    )
    return jax.shard_map(
        local,
        mesh=mesh,
        in_specs=placed,
        out_specs=(P("rep", "dom"), P("rep", "dom"), P(None, "rep"), P(None, "rep")),
        check_vma=False,
    )
```

```python
import jax
import jax.numpy as jnp
from jax import lax
from jax.experimental import pallas as pl
from jax.experimental.pallas import tpu as pltpu
from jax.sharding import PartitionSpec as P

TILE = 128
STEP = 8
VMEM_BYTES = 12 * 1024 * 1024
F32 = jnp.float32
BF16 = jnp.bfloat16
IN_VMEM = pl.BlockSpec(memory_space=pltpu.VMEM)
IN_SMEM = pl.BlockSpec(memory_space=pltpu.SMEM)
IN_HBM = pl.BlockSpec(memory_space=pltpu.HBM)


def lanes(index, width):
    return pl.ds(pl.multiple_of(index * width, width), width)


def call(body, scalars, args, out_shape, scratch=(), micros=1.0, hbm=(), hbm_out=()):
    many = isinstance(out_shape, list)
    out_specs = [IN_HBM if i in hbm_out else IN_VMEM for i in range(len(out_shape) if many else 1)]
    out_specs = out_specs if many else out_specs[0]
    args = [pinned(arg) if i in hbm else arg for i, arg in enumerate(args)]
    return pl.pallas_call(
        body,
        in_specs=[IN_SMEM] * len(scalars) + [IN_HBM if i in hbm else IN_VMEM for i in range(len(args))],
        out_shape=out_shape,
        out_specs=out_specs,
        scratch_shapes=scratch,
        compiler_params=pltpu.CompilerParams(vmem_limit_bytes=VMEM_BYTES),
        cost_estimate=pl.CostEstimate(flops=int(micros * 1.1e9), bytes_accessed=1 << 16, transcendentals=0),
    )(*scalars, *args)


def shape(dims, kind):
    return jax.ShapeDtypeStruct(dims, kind)


def in_hbm(dims, kind):
    return pltpu.HBM(dims, kind)


def pinned(value):
    return pltpu.with_memory_space_constraint(value, pltpu.HBM)


def dot(left, right, left_dim, right_dim):
    return lax.dot_general(left, right, (((left_dim,), (right_dim,)), ((), ())), preferred_element_type=F32)


def pick_body(send_ref, feats_hbm, out_ref, feats_ref, buf_ref, sems, feats_sem):
    chans = feats_ref.shape[0]
    load = pltpu.make_async_copy(feats_hbm, feats_ref, feats_sem)
    load.start()
    load.wait()
    parts = buf_ref.shape[0]
    for step in range(parts // STEP):
        for item in range(step * STEP, (step + 1) * STEP):
            for slot in range(2):
                block = send_ref[slot, item]
                buf_ref[item, slot * chans : (slot + 1) * chans, :] = feats_ref[:, lanes(block, TILE)]
        rows = pl.ds(step * STEP, STEP)
        pltpu.make_async_copy(buf_ref.at[rows], out_ref.at[rows], sems.at[step]).start()
    for step in range(parts // STEP):
        rows = pl.ds(step * STEP, STEP)
        pltpu.make_async_copy(buf_ref.at[rows], out_ref.at[rows], sems.at[step]).wait()


def tile_copy(far_hbm, far_ref, sems, step):
    rows = pl.ds(step * STEP, STEP)
    return pltpu.make_async_copy(far_hbm.at[rows], far_ref.at[rows], sems.at[step])


def chunk_body(rep_ref, feats_ref, cot_ref, *outs):
    reps = len(outs) // 2
    width = outs[0].shape[1]
    for k in range(reps):
        chunk = lax.rem(rep_ref[0] + k, reps)
        outs[k][...] = feats_ref[:, lanes(chunk, width)]
        outs[reps + k][...] = cot_ref[:, lanes(chunk, width)]


def near_body(cols_ref, rows_ref, feats_ref, near_ref, far_ref, acc_ref, div_ref, turned_hbm, turned_ref, sems):
    ones = jnp.ones((8, TILE), BF16)
    div_ref[...] = jnp.ones_like(div_ref)

    @pl.loop(0, near_ref.shape[0] // 4)
    def _(step):
        for item in range(4):
            row = step * 4 + item
            total = None
            sums = None
            for link in range(2):
                tile = near_ref[row, link]
                term = dot(feats_ref[:, lanes(cols_ref[link, row], TILE)], tile, 1, 1)
                part = dot(ones, tile, 1, 1)
                total = term if total is None else total + term
                sums = part if sums is None else sums + part
            acc_ref[:, lanes(row, TILE)] = total
            div_ref[:, lanes(row, TILE)] += sums

    @pl.loop(0, far_ref.shape[0] // STEP)
    def _(step):
        for item in range(STEP):
            for slot in range(2):
                part = step * STEP + item
                row = rows_ref[slot, part]
                turned = far_ref[part, slot].T
                turned_ref[part, slot] = turned
                div_ref[:, lanes(row, TILE)] += dot(ones, turned, 1, 0)
        tile_copy(turned_ref, turned_hbm, sems, step).start()

    for step in range(far_ref.shape[0] // STEP):
        tile_copy(turned_ref, turned_hbm, sems, step).wait()


def far_body(rep_ref, rows_ref, got_ref, far_hbm, near_acc_hbm, div_hbm, *rest):
    outs = rest[:4]
    acc_ref, near_acc_ref, far_ref, div_ref, sems, acc_sem, div_sem = rest[4:]
    reps = len(outs)
    chans = acc_ref.shape[0]
    width = outs[0].shape[1]
    load_acc = pltpu.make_async_copy(near_acc_hbm, near_acc_ref, acc_sem)
    load_div = pltpu.make_async_copy(div_hbm, div_ref, div_sem)
    for step in range(far_ref.shape[0] // STEP):
        tile_copy(far_hbm, far_ref, sems, step).start()
    load_acc.start()
    load_div.start()
    acc_ref[...] = jnp.zeros_like(acc_ref)

    @pl.loop(0, far_ref.shape[0] // STEP)
    def _(step):
        tile_copy(far_hbm, far_ref, sems, step).wait()
        for item in range(STEP):
            for slot in range(2):
                part = step * STEP + item
                row = rows_ref[slot, part]
                block = got_ref[part, slot * chans : (slot + 1) * chans, :]
                acc_ref[:, lanes(row, TILE)] += dot(block, far_ref[part, slot], 1, 0)

    load_acc.wait()
    load_div.wait()
    for k in range(reps):
        where = lanes(lax.rem(rep_ref[0] + k, reps), width)
        outs[k][...] = ((near_acc_ref[:, where] + acc_ref[:, where]) / div_ref[0:1, where]).astype(BF16)


def gather_rows(ref, pieces, rep):
    reps = len(pieces)
    rows = pieces[0].shape[0]
    for k in range(reps):
        source = lax.rem(rep + reps - k, reps)
        ref[lanes(source, rows), :] = pieces[k][...]


def dense_body(rep_ref, *refs):
    agg, feats, cot, wts = refs[0:4], refs[4:8], refs[8:12], refs[12:16]
    div_ref = refs[16]
    scaled_out, out_out, grad_hbm, slices_hbm = refs[17:21], refs[21:25], refs[25], refs[26]
    back_ref, full_feats, full_agg, grad_ref, out_buf, prod_ref, slices_ref = refs[27:34]
    out_sems, grad_sem, slices_sem = refs[34:37]
    rep = rep_ref[0]
    reps = 4
    rows, width = agg[0].shape
    gather_rows(full_feats, feats, rep)
    gather_rows(full_agg, agg, rep)
    copies = []

    def leave(source, target, sem):
        copies.append(pltpu.make_async_copy(source, target, sem))
        copies[-1].start()

    for k in range(reps):
        preact = dot(wts[k][0], full_feats[...], 1, 0) + dot(wts[k][1], full_agg[...], 1, 0)
        gate = jax.nn.sigmoid(preact)
        slope = gate * (1.0 + preact * (1.0 - gate))
        grad_ref[k * rows : (k + 1) * rows, :] = (cot[k][...].astype(F32) * slope).astype(BF16)
        out_buf[k] = (preact * gate).astype(BF16)
        leave(out_buf.at[k], out_out[k], out_sems.at[k])
    leave(grad_ref, grad_hbm, grad_sem)
    for which, full in ((0, full_feats), (1, full_agg)):
        prod_ref[...] = dot(grad_ref[...], full[...], 1, 1)
        for group in range(rows // 4):
            for half in range(2):
                index = which * 32 + group * 2 + half
                for k in range(reps):
                    start = k * rows + group * 4
                    slices_ref[index, 4 * k : 4 * k + 4, :] = prod_ref[
                        start : start + 4, half * TILE : (half + 1) * TILE
                    ].astype(BF16)
    leave(slices_ref, slices_hbm, slices_sem)
    w_neigh = jnp.concatenate([wts[k][1] for k in range(reps)], axis=0)
    back_ref[...] = dot(w_neigh, grad_ref[...], 0, 0)
    div = div_ref[0:1, lanes(rep, width)]
    for k in range(reps):
        target = lax.rem(rep + k, reps)
        scaled_out[k][...] = (back_ref[lanes(target, rows), :] / div).astype(BF16)
    for copy in copies:
        copy.wait()


def back_body(rep_ref, *refs):
    wts, grad_ref, back_out, back_ref = refs[0:4], refs[4], refs[5:9], refs[9]
    rep = rep_ref[0]
    reps = 4
    rows = back_out[0].shape[0]
    w_self = jnp.concatenate([wts[k][0] for k in range(reps)], axis=0)
    back_ref[...] = dot(w_self, grad_ref[...], 0, 0)
    for k in range(reps):
        target = lax.rem(rep + k, reps)
        back_out[k][...] = back_ref[lanes(target, rows), :]


def slice_sum_body(got_ref, *outs):
    total = jnp.sum(got_ref[...].astype(F32), axis=0)
    for k in range(len(outs)):
        outs[k][...] = total[4 * k : 4 * k + 4, :]


def slice_send_body(*refs):
    parts, out_ref = refs[:4], refs[-1]
    total = parts[0][...] + parts[1][...] + parts[2][...] + parts[3][...]
    high = total.astype(BF16)
    low = (total - high.astype(F32)).astype(BF16)
    both = jnp.concatenate([high.astype(F32), low.astype(F32)], axis=0).astype(BF16)
    out_ref[...] = jnp.broadcast_to(both[None], out_ref.shape)


def gather_lanes(ref, pieces, rep):
    reps = len(pieces)
    width = pieces[0].shape[1]
    for k in range(reps):
        source = lax.rem(rep + reps - k, reps)
        ref[:, lanes(source, width)] = pieces[k][...]


def far_back_body(rep_ref, rows_ref, s0, s1, s2, s3, far_hbm, out_ref, full_ref, buf_ref, far_ref, sems, out_sems):
    chans = full_ref.shape[0]
    parts = far_ref.shape[0]
    for step in range(parts // STEP):
        tile_copy(far_hbm, far_ref, sems, step).start()
    gather_lanes(full_ref, (s0, s1, s2, s3), rep_ref[0])

    def copy(step):
        rows = pl.ds(step * STEP, STEP)
        return pltpu.make_async_copy(
            buf_ref.at[rows], out_ref.at[rows, pl.ds(0, 2 * chans)], out_sems.at[step]
        )

    @pl.loop(0, parts // STEP)
    def _(step):
        tile_copy(far_hbm, far_ref, sems, step).wait()
        for item in range(STEP):
            for slot in range(2):
                part = step * STEP + item
                row = rows_ref[slot, part]
                term = dot(full_ref[:, lanes(row, TILE)], far_ref[part, slot], 1, 0)
                buf_ref[part, slot * chans : (slot + 1) * chans, :] = term.astype(BF16)
        copy(step).start()

    for step in range(parts // STEP):
        copy(step).wait()


def near_back_body(rep_ref, cols_ref, *refs):
    scaled, back, outs = refs[0:4], refs[4:8], refs[8:12]
    near_ref, acc_ref, output_ref, full_ref = refs[12:16]
    rep = rep_ref[0]
    reps = 4
    width = scaled[0].shape[1]
    gather_lanes(full_ref, scaled, rep)
    gather_lanes(acc_ref, back, rep)
    for k in range(reps):
        output_ref[:, lanes(lax.rem(rep + k, reps), width)] = outs[k][...]

    @pl.loop(0, near_ref.shape[0] // 4)
    def _(step):
        for item in range(4):
            row = step * 4 + item
            for link in range(2):
                term = dot(full_ref[:, lanes(row, TILE)], near_ref[row, link], 1, 0)
                acc_ref[:, lanes(cols_ref[link, row], TILE)] += term


def home_body(send_ref, got_ref, near_acc_hbm, grad_ref, w_self_ref, w_neigh_ref, acc_ref, near_acc_ref, sem):
    chans = acc_ref.shape[0]
    parts = got_ref.shape[0]
    load = pltpu.make_async_copy(near_acc_hbm, near_acc_ref, sem)
    load.start()
    acc_ref[...] = jnp.zeros_like(acc_ref)
    for item in range(parts):
        for slot in range(2):
            block = send_ref[slot, item]
            acc_ref[:, lanes(block, TILE)] += got_ref[item, slot * chans : (slot + 1) * chans, :].astype(F32)
        both = got_ref[item, 2 * chans : 2 * chans + 8, :].astype(F32)
        weight_ref = (w_self_ref, w_neigh_ref)[item // (parts // 2)]
        group, half = item % (parts // 2) // 2, item % 2
        weight_ref[4 * group : 4 * group + 4, half * TILE : (half + 1) * TILE] = both[0:4] + both[4:8]
    load.wait()
    grad_ref[...] = (near_acc_ref[...] + acc_ref[...]).astype(BF16)


def local(feats, w_self, w_neigh, local_cols, local_tiles, send_list, remote_rows, remote_tiles, cotangent):
    chans, nodes = feats.shape
    full = w_self.shape[0]
    reps = full // chans
    width = nodes // reps
    parts = remote_tiles.shape[1]
    far_tiles = remote_tiles[0]
    rows = remote_rows[0].T
    sends = send_list[0].T
    cols = local_cols.T
    rep = lax.axis_index("rep").astype(jnp.int32).reshape(1)
    piece = shape((chans, width), BF16)
    piece32 = shape((chans, width), F32)
    sems = pltpu.SemaphoreType.DMA((parts // STEP,))
    sem = pltpu.SemaphoreType.DMA(())
    tile_buf = pltpu.VMEM(far_tiles.shape, BF16)
    wide32 = pltpu.VMEM((chans, nodes), F32)

    def shift(value, by):
        return lax.ppermute(value, "rep", [(i, (i + by) % reps) for i in range(reps)])

    def exchange(pieces, sign=1):
        return [pieces[0]] + [shift(pieces[k], (sign * k) % reps) for k in range(1, reps)]

    with jax.named_scope("pick"):
        outgoing = call(
            pick_body, (sends,), (feats,), in_hbm((parts, 2 * chans, TILE), BF16),
            [pltpu.VMEM((chans, nodes), BF16), pltpu.VMEM((parts, 2 * chans, TILE), BF16), sems, sem], 2.0, (0,), (0,),
        )
    incoming = lax.all_to_all(outgoing, "dom", split_axis=0, concat_axis=0, tiled=True)

    with jax.named_scope("chunks"):
        pieces = call(chunk_body, (rep,), (feats, cotangent), [piece] * (2 * reps))
    feats_in = exchange(pieces[:reps])
    cot_in = exchange(pieces[reps:])
    weights_in = exchange([jnp.stack([w_self.T, w_neigh.T])] * reps)
    with jax.named_scope("near"):
        near_acc, div, turned = call(
            near_body, (cols, rows), (feats, local_tiles, far_tiles),
            [shape((chans, nodes), F32), shape((8, nodes), F32), in_hbm(far_tiles.shape, BF16)],
            [tile_buf, sems], 8.0, (), (2,),
        )
    incoming, feats_in, cot_in, weights_in, near_acc, div, turned = lax.optimization_barrier(
        (incoming, feats_in, cot_in, weights_in, near_acc, div, turned)
    )
    with jax.named_scope("far"):
        agg = call(
            far_body, (rep, rows), (incoming, turned, near_acc, div), [piece] * reps,
            [wide32, wide32, tile_buf, pltpu.VMEM((8, nodes), F32), sems, sem, sem], 6.0, (1, 2, 3),
        )
    agg_in = exchange(agg)

    with jax.named_scope("dense"):
        dense = call(
            dense_body, (rep,), (*agg_in, *feats_in, *cot_in, *weights_in, div),
            [piece] * reps
            + [in_hbm((chans, width), BF16)] * reps
            + [in_hbm((full, width), BF16), in_hbm((parts, 4 * reps, TILE), BF16)],
            [
                pltpu.VMEM((full, width), F32), pltpu.VMEM((full, width), BF16), pltpu.VMEM((full, width), BF16),
                pltpu.VMEM((full, width), BF16), pltpu.VMEM((reps, chans, width), BF16), pltpu.VMEM((full, full), F32),
                pltpu.VMEM((parts, 4 * reps, TILE), BF16), pltpu.SemaphoreType.DMA((reps,)), sem, sem,
            ],
            3.0, (), range(reps, 2 * reps + 2),
        )
    scaled, out_pieces, grad_pre, slices = dense[:reps], dense[reps : 2 * reps], dense[2 * reps], dense[2 * reps + 1]
    scaled_in = exchange(scaled)
    slices_in = lax.all_to_all(slices, "dom", split_axis=0, concat_axis=0, tiled=True)
    with jax.named_scope("far_back"):
        far_back = call(
            far_back_body, (rep, rows), (*scaled_in, far_tiles), in_hbm((parts, 2 * chans + 8, TILE), BF16),
            [
                pltpu.VMEM((chans, nodes), BF16), pltpu.VMEM((parts, 2 * chans, TILE), BF16), tile_buf, sems, sems,
            ],
            2.0, (reps,), (0,),
        )
    slices_in, far_back = lax.optimization_barrier((slices_in, far_back))
    with jax.named_scope("slice_sum"):
        sums = call(slice_sum_body, (), (slices_in,), [shape((4, TILE), F32)] * reps)
    sums_in = exchange(sums, -1)
    with jax.named_scope("slice_send"):
        sending = pl.pallas_call(
            slice_send_body,
            grid=(1,),
            in_specs=[IN_VMEM] * reps + [IN_HBM],
            out_shape=in_hbm(far_back.shape, BF16),
            out_specs=pl.BlockSpec((parts, 8, TILE), lambda i: (0, 2 * chans // 8, 0)),
            input_output_aliases={reps: 0},
            compiler_params=pltpu.CompilerParams(vmem_limit_bytes=VMEM_BYTES),
        )(*sums_in, pinned(far_back))
    returned = lax.all_to_all(sending, "dom", split_axis=0, concat_axis=0, tiled=True)

    with jax.named_scope("back"):
        back_self = call(
            back_body, (rep,), (*weights_in, grad_pre), [piece32] * reps, [pltpu.VMEM((full, width), F32)], 1.0
        )
    back_in = exchange(back_self)
    out_in = exchange(out_pieces, -1)
    with jax.named_scope("near_back"):
        near_back, output = call(
            near_back_body, (rep, cols), (*scaled_in, *back_in, *out_in, local_tiles),
            [shape((chans, nodes), F32), shape((chans, nodes), BF16)], [pltpu.VMEM((chans, nodes), BF16)], 2.0,
        )
    with jax.named_scope("home"):
        grad_feats, wg_self, wg_neigh = call(
            home_body, (sends,), (returned, near_back),
            [shape((chans, nodes), BF16), shape((chans, full), F32), shape((chans, full), F32)],
            [wide32, wide32, sem], 3.0, (1,),
        )
    return output, grad_feats, wg_self.T, wg_neigh.T


def solution(mesh):
    placed = (
        P("rep", "dom"),
        P(None, "rep"),
        P(None, "rep"),
        P("dom", None),
        P("dom", None, None, None),
        P("dom", None, None),
        P("dom", None, None),
        P("dom", None, None, None, None),
        P("rep", "dom"),
    )
    return jax.shard_map(
        local,
        mesh=mesh,
        in_specs=placed,
        out_specs=(P("rep", "dom"), P("rep", "dom"), P(None, "rep"), P(None, "rep")),
        check_vma=False,
    )
```

```python
import jax
import jax.numpy as jnp
from jax import lax
from jax.experimental import pallas as pl
from jax.experimental.pallas import tpu as pltpu
from jax.sharding import PartitionSpec as P

TILE = 128
STEP = 8
VMEM_BYTES = 12 * 1024 * 1024
F32 = jnp.float32
BF16 = jnp.bfloat16
IN_VMEM = pl.BlockSpec(memory_space=pltpu.VMEM)
IN_SMEM = pl.BlockSpec(memory_space=pltpu.SMEM)
IN_HBM = pl.BlockSpec(memory_space=pltpu.HBM)


def lanes(index, width):
    return pl.ds(pl.multiple_of(index * width, width), width)


def call(body, scalars, args, out_shape, scratch=(), micros=1.0, hbm=(), hbm_out=()):
    many = isinstance(out_shape, list)
    out_specs = [IN_HBM if i in hbm_out else IN_VMEM for i in range(len(out_shape) if many else 1)]
    out_specs = out_specs if many else out_specs[0]
    args = [pinned(arg) if i in hbm else arg for i, arg in enumerate(args)]
    return pl.pallas_call(
        body,
        in_specs=[IN_SMEM] * len(scalars) + [IN_HBM if i in hbm else IN_VMEM for i in range(len(args))],
        out_shape=out_shape,
        out_specs=out_specs,
        scratch_shapes=scratch,
        compiler_params=pltpu.CompilerParams(vmem_limit_bytes=VMEM_BYTES),
        cost_estimate=pl.CostEstimate(flops=int(micros * 1.1e9), bytes_accessed=1 << 16, transcendentals=0),
    )(*scalars, *args)


def shape(dims, kind):
    return jax.ShapeDtypeStruct(dims, kind)


def in_hbm(dims, kind):
    return pltpu.HBM(dims, kind)


def pinned(value):
    return pltpu.with_memory_space_constraint(value, pltpu.HBM)


def dot(left, right, left_dim, right_dim):
    return lax.dot_general(left, right, (((left_dim,), (right_dim,)), ((), ())), preferred_element_type=F32)


def pick_body(send_ref, feats_hbm, out_ref, feats_ref, buf_ref, sems, feats_sem):
    chans = feats_ref.shape[0]
    load = pltpu.make_async_copy(feats_hbm, feats_ref, feats_sem)
    load.start()
    load.wait()
    parts = buf_ref.shape[0]
    for step in range(parts // STEP):
        for item in range(step * STEP, (step + 1) * STEP):
            for slot in range(2):
                block = send_ref[slot, item]
                buf_ref[item, slot * chans : (slot + 1) * chans, :] = feats_ref[:, lanes(block, TILE)]
        rows = pl.ds(step * STEP, STEP)
        pltpu.make_async_copy(buf_ref.at[rows], out_ref.at[rows], sems.at[step]).start()
    for step in range(parts // STEP):
        rows = pl.ds(step * STEP, STEP)
        pltpu.make_async_copy(buf_ref.at[rows], out_ref.at[rows], sems.at[step]).wait()


def tile_copy(far_hbm, far_ref, sems, step):
    rows = pl.ds(step * STEP, STEP)
    return pltpu.make_async_copy(far_hbm.at[rows], far_ref.at[rows], sems.at[step])


def chunk_body(rep_ref, feats_ref, cot_ref, *outs):
    reps = len(outs) // 2
    width = outs[0].shape[1]
    for k in range(reps):
        chunk = lax.rem(rep_ref[0] + k, reps)
        outs[k][...] = feats_ref[:, lanes(chunk, width)]
        outs[reps + k][...] = cot_ref[:, lanes(chunk, width)]


def near_body(cols_ref, rows_ref, feats_ref, near_ref, far_ref, acc_ref, div_ref, turned_hbm, turned_ref, sems):
    ones = jnp.ones((8, TILE), BF16)
    div_ref[...] = jnp.ones_like(div_ref)

    @pl.loop(0, near_ref.shape[0] // 4)
    def _(step):
        for item in range(4):
            row = step * 4 + item
            total = None
            sums = None
            for link in range(2):
                tile = near_ref[row, link]
                term = dot(feats_ref[:, lanes(cols_ref[link, row], TILE)], tile, 1, 1)
                part = dot(ones, tile, 1, 1)
                total = term if total is None else total + term
                sums = part if sums is None else sums + part
            acc_ref[:, lanes(row, TILE)] = total
            div_ref[:, lanes(row, TILE)] += sums

    @pl.loop(0, far_ref.shape[0] // STEP)
    def _(step):
        for item in range(STEP):
            for slot in range(2):
                part = step * STEP + item
                row = rows_ref[slot, part]
                turned = far_ref[part, slot].T
                turned_ref[part, slot] = turned
                div_ref[:, lanes(row, TILE)] += dot(ones, turned, 1, 0)
        tile_copy(turned_ref, turned_hbm, sems, step).start()

    for step in range(far_ref.shape[0] // STEP):
        tile_copy(turned_ref, turned_hbm, sems, step).wait()


def far_body(rep_ref, rows_ref, got_ref, far_hbm, near_acc_hbm, div_hbm, *rest):
    outs = rest[:4]
    acc_ref, near_acc_ref, far_ref, div_ref, sems, acc_sem, div_sem = rest[4:]
    reps = len(outs)
    chans = acc_ref.shape[0]
    width = outs[0].shape[1]
    load_acc = pltpu.make_async_copy(near_acc_hbm, near_acc_ref, acc_sem)
    load_div = pltpu.make_async_copy(div_hbm, div_ref, div_sem)
    for step in range(far_ref.shape[0] // STEP):
        tile_copy(far_hbm, far_ref, sems, step).start()
    load_acc.start()
    load_div.start()
    acc_ref[...] = jnp.zeros_like(acc_ref)

    @pl.loop(0, far_ref.shape[0] // STEP)
    def _(step):
        tile_copy(far_hbm, far_ref, sems, step).wait()
        for item in range(STEP):
            for slot in range(2):
                part = step * STEP + item
                row = rows_ref[slot, part]
                block = got_ref[part, slot * chans : (slot + 1) * chans, :]
                acc_ref[:, lanes(row, TILE)] += dot(block, far_ref[part, slot], 1, 0)

    load_acc.wait()
    load_div.wait()
    for k in range(reps):
        where = lanes(lax.rem(rep_ref[0] + k, reps), width)
        outs[k][...] = ((near_acc_ref[:, where] + acc_ref[:, where]) / div_ref[0:1, where]).astype(BF16)


def gather_rows(ref, pieces, rep):
    reps = len(pieces)
    rows = pieces[0].shape[0]
    for k in range(reps):
        source = lax.rem(rep + reps - k, reps)
        ref[lanes(source, rows), :] = pieces[k][...]


def dense_body(rep_ref, *refs):
    agg, feats, cot, wts = refs[0:4], refs[4:8], refs[8:12], refs[12:16]
    div_ref = refs[16]
    leaving, out_out, grad_hbm = refs[17:21], refs[21:25], refs[25]
    back_ref, full_feats, full_agg, grad_ref, out_buf, prod_ref = refs[26:32]
    out_sems, grad_sem = refs[32:34]
    rep = rep_ref[0]
    reps = 4
    rows, width = agg[0].shape
    gather_rows(full_feats, feats, rep)
    gather_rows(full_agg, agg, rep)
    copies = []

    def leave(source, target, sem):
        copies.append(pltpu.make_async_copy(source, target, sem))
        copies[-1].start()

    for k in range(reps):
        preact = dot(wts[k][0], full_feats[...], 1, 0) + dot(wts[k][1], full_agg[...], 1, 0)
        gate = jax.nn.sigmoid(preact)
        slope = gate * (1.0 + preact * (1.0 - gate))
        grad_ref[k * rows : (k + 1) * rows, :] = (cot[k][...].astype(F32) * slope).astype(BF16)
        out_buf[k] = (preact * gate).astype(BF16)
        leave(out_buf.at[k], out_out[k], out_sems.at[k])
    leave(grad_ref, grad_hbm, grad_sem)
    for which, full in ((0, full_feats), (1, full_agg)):
        prod_ref[...] = dot(grad_ref[...], full[...], 1, 1)
        full_width = prod_ref.shape[1]
        for k in range(reps):
            source = (reps - k) % reps
            start = width + which * full_width
            leaving[k][:, start : start + full_width] = prod_ref[source * rows : (source + 1) * rows, :].astype(BF16)
    w_neigh = jnp.concatenate([wts[k][1] for k in range(reps)], axis=0)
    back_ref[...] = dot(w_neigh, grad_ref[...], 0, 0)
    div = div_ref[0:1, lanes(rep, width)]
    for k in range(reps):
        target = lax.rem(rep + k, reps)
        leaving[k][:, :width] = (back_ref[lanes(target, rows), :] / div).astype(BF16)
    for copy in copies:
        copy.wait()


def back_body(rep_ref, *refs):
    wts, grad_ref, back_out, back_ref = refs[0:4], refs[4], refs[5:9], refs[9]
    rep = rep_ref[0]
    reps = 4
    rows = back_out[0].shape[0]
    w_self = jnp.concatenate([wts[k][0] for k in range(reps)], axis=0)
    back_ref[...] = dot(w_self, grad_ref[...], 0, 0)
    for k in range(reps):
        target = lax.rem(rep + k, reps)
        back_out[k][...] = back_ref[lanes(target, rows), :]


def slice_body(*refs):
    pieces, slices_ref = refs[:4], refs[4]
    rows, wide = pieces[0].shape
    full = wide // 6
    first = wide - 2 * full
    total = pieces[0][:, first:].astype(F32)
    for piece in pieces[1:]:
        total = total + piece[:, first:].astype(F32)
    for which in range(2):
        for group in range(rows // 4):
            for half in range(2):
                start = which * full + half * TILE
                slices_ref[which * 32 + group * 2 + half] = total[4 * group : 4 * group + 4, start : start + TILE]


def slice_send_body(got_ref, rest_ref, out_ref):
    total = jnp.sum(got_ref[...], axis=0)
    high = total.astype(BF16)
    low = (total - high.astype(F32)).astype(BF16)
    both = jnp.concatenate([high.astype(F32), low.astype(F32)], axis=0).astype(BF16)
    out_ref[...] = jnp.broadcast_to(both[None], out_ref.shape)


def gather_lanes(ref, pieces, rep):
    reps = len(pieces)
    width = ref.shape[1] // reps
    for k in range(reps):
        source = lax.rem(rep + reps - k, reps)
        ref[:, lanes(source, width)] = pieces[k][:, :width]


def far_back_body(rep_ref, rows_ref, s0, s1, s2, s3, far_hbm, out_ref, full_ref, buf_ref, far_ref, sems, out_sems):
    chans = full_ref.shape[0]
    parts = far_ref.shape[0]
    for step in range(parts // STEP):
        tile_copy(far_hbm, far_ref, sems, step).start()
    gather_lanes(full_ref, (s0, s1, s2, s3), rep_ref[0])

    def copy(step):
        rows = pl.ds(step * STEP, STEP)
        return pltpu.make_async_copy(
            buf_ref.at[rows], out_ref.at[rows, pl.ds(0, 2 * chans)], out_sems.at[step]
        )

    @pl.loop(0, parts // STEP)
    def _(step):
        tile_copy(far_hbm, far_ref, sems, step).wait()
        for item in range(STEP):
            for slot in range(2):
                part = step * STEP + item
                row = rows_ref[slot, part]
                term = dot(full_ref[:, lanes(row, TILE)], far_ref[part, slot], 1, 0)
                buf_ref[part, slot * chans : (slot + 1) * chans, :] = term.astype(BF16)
        copy(step).start()

    for step in range(parts // STEP):
        copy(step).wait()


def near_back_body(rep_ref, cols_ref, *refs):
    scaled, back, outs = refs[0:4], refs[4:8], refs[8:12]
    near_ref, acc_ref, output_ref, full_ref = refs[12:16]
    rep = rep_ref[0]
    reps = 4
    width = outs[0].shape[1]
    gather_lanes(full_ref, scaled, rep)
    gather_lanes(acc_ref, back, rep)
    for k in range(reps):
        output_ref[:, lanes(lax.rem(rep + k, reps), width)] = outs[k][...]

    @pl.loop(0, near_ref.shape[0] // 4)
    def _(step):
        for item in range(4):
            row = step * 4 + item
            for link in range(2):
                term = dot(full_ref[:, lanes(row, TILE)], near_ref[row, link], 1, 0)
                acc_ref[:, lanes(cols_ref[link, row], TILE)] += term


def home_body(send_ref, got_ref, near_acc_hbm, grad_ref, w_self_ref, w_neigh_ref, acc_ref, near_acc_ref, sem):
    chans = acc_ref.shape[0]
    parts = got_ref.shape[0]
    load = pltpu.make_async_copy(near_acc_hbm, near_acc_ref, sem)
    load.start()
    acc_ref[...] = jnp.zeros_like(acc_ref)
    for item in range(parts):
        for slot in range(2):
            block = send_ref[slot, item]
            acc_ref[:, lanes(block, TILE)] += got_ref[item, slot * chans : (slot + 1) * chans, :].astype(F32)
        both = got_ref[item, 2 * chans : 2 * chans + 8, :].astype(F32)
        weight_ref = (w_self_ref, w_neigh_ref)[item // (parts // 2)]
        group, half = item % (parts // 2) // 2, item % 2
        weight_ref[4 * group : 4 * group + 4, half * TILE : (half + 1) * TILE] = both[0:4] + both[4:8]
    load.wait()
    grad_ref[...] = (near_acc_ref[...] + acc_ref[...]).astype(BF16)


def local(feats, w_self, w_neigh, local_cols, local_tiles, send_list, remote_rows, remote_tiles, cotangent):
    chans, nodes = feats.shape
    full = w_self.shape[0]
    reps = full // chans
    width = nodes // reps
    parts = remote_tiles.shape[1]
    far_tiles = remote_tiles[0]
    rows = remote_rows[0].T
    sends = send_list[0].T
    cols = local_cols.T
    rep = lax.axis_index("rep").astype(jnp.int32).reshape(1)
    piece = shape((chans, width), BF16)
    piece32 = shape((chans, width), F32)
    sems = pltpu.SemaphoreType.DMA((parts // STEP,))
    sem = pltpu.SemaphoreType.DMA(())
    tile_buf = pltpu.VMEM(far_tiles.shape, BF16)
    wide32 = pltpu.VMEM((chans, nodes), F32)

    def shift(value, by):
        return lax.ppermute(value, "rep", [(i, (i + by) % reps) for i in range(reps)])

    def exchange(pieces, sign=1):
        return [pieces[0]] + [shift(pieces[k], (sign * k) % reps) for k in range(1, reps)]

    with jax.named_scope("pick"):
        outgoing = call(
            pick_body, (sends,), (feats,), in_hbm((parts, 2 * chans, TILE), BF16),
            [pltpu.VMEM((chans, nodes), BF16), pltpu.VMEM((parts, 2 * chans, TILE), BF16), sems, sem], 2.0, (0,), (0,),
        )
    incoming = lax.all_to_all(outgoing, "dom", split_axis=0, concat_axis=0, tiled=True)

    with jax.named_scope("chunks"):
        pieces = call(chunk_body, (rep,), (feats, cotangent), [piece] * (2 * reps))
    feats_in = exchange(pieces[:reps])
    cot_in = exchange(pieces[reps:])
    weights_in = exchange([jnp.stack([w_self.T, w_neigh.T])] * reps)
    with jax.named_scope("near"):
        near_acc, div, turned = call(
            near_body, (cols, rows), (feats, local_tiles, far_tiles),
            [shape((chans, nodes), F32), shape((8, nodes), F32), in_hbm(far_tiles.shape, BF16)],
            [tile_buf, sems], 8.0, (), (2,),
        )
    incoming, feats_in, cot_in, weights_in, near_acc, div, turned = lax.optimization_barrier(
        (incoming, feats_in, cot_in, weights_in, near_acc, div, turned)
    )
    with jax.named_scope("far"):
        agg = call(
            far_body, (rep, rows), (incoming, turned, near_acc, div), [piece] * reps,
            [wide32, wide32, tile_buf, pltpu.VMEM((8, nodes), F32), sems, sem, sem], 6.0, (1, 2, 3),
        )
    agg_in = exchange(agg)

    with jax.named_scope("dense"):
        dense = call(
            dense_body, (rep,), (*agg_in, *feats_in, *cot_in, *weights_in, div),
            [shape((chans, width + 2 * full), BF16)] * reps
            + [in_hbm((chans, width), BF16)] * reps
            + [in_hbm((full, width), BF16)],
            [
                pltpu.VMEM((full, width), F32), pltpu.VMEM((full, width), BF16), pltpu.VMEM((full, width), BF16),
                pltpu.VMEM((full, width), BF16), pltpu.VMEM((reps, chans, width), BF16), pltpu.VMEM((full, full), F32),
                pltpu.SemaphoreType.DMA((reps,)), sem,
            ],
            3.0, (), range(reps, 2 * reps + 1),
        )
    scaled, out_pieces, grad_pre = dense[:reps], dense[reps : 2 * reps], dense[2 * reps]
    scaled_in = exchange(scaled)
    with jax.named_scope("slices"):
        slices = call(slice_body, (), scaled_in, shape((parts, 4, TILE), F32), (), 0.5)
    slices_in = lax.all_to_all(slices, "dom", split_axis=0, concat_axis=0, tiled=True)
    with jax.named_scope("far_back"):
        far_back = call(
            far_back_body, (rep, rows), (*scaled_in, far_tiles), in_hbm((parts, 2 * chans + 8, TILE), BF16),
            [
                pltpu.VMEM((chans, nodes), BF16), pltpu.VMEM((parts, 2 * chans, TILE), BF16), tile_buf, sems, sems,
            ],
            2.0, (reps,), (0,),
        )
    with jax.named_scope("slice_send"):
        sending = pl.pallas_call(
            slice_send_body,
            grid=(1,),
            in_specs=[IN_VMEM, IN_HBM],
            out_shape=in_hbm(far_back.shape, BF16),
            out_specs=pl.BlockSpec((parts, 8, TILE), lambda i: (0, 2 * chans // 8, 0)),
            input_output_aliases={1: 0},
            compiler_params=pltpu.CompilerParams(vmem_limit_bytes=VMEM_BYTES),
        )(slices_in, pinned(far_back))
    returned = lax.all_to_all(sending, "dom", split_axis=0, concat_axis=0, tiled=True)

    with jax.named_scope("back"):
        back_self = call(
            back_body, (rep,), (*weights_in, grad_pre), [piece32] * reps, [pltpu.VMEM((full, width), F32)], 1.0
        )
    back_in = exchange(back_self)
    out_in = exchange(out_pieces, -1)
    with jax.named_scope("near_back"):
        near_back, output = call(
            near_back_body, (rep, cols), (*scaled_in, *back_in, *out_in, local_tiles),
            [shape((chans, nodes), F32), shape((chans, nodes), BF16)], [pltpu.VMEM((chans, nodes), BF16)], 2.0,
        )
    with jax.named_scope("home"):
        grad_feats, wg_self, wg_neigh = call(
            home_body, (sends,), (returned, near_back),
            [shape((chans, nodes), BF16), shape((chans, full), F32), shape((chans, full), F32)],
            [wide32, wide32, sem], 3.0, (1,),
        )
    return output, grad_feats, wg_self.T, wg_neigh.T


def solution(mesh):
    placed = (
        P("rep", "dom"),
        P(None, "rep"),
        P(None, "rep"),
        P("dom", None),
        P("dom", None, None, None),
        P("dom", None, None),
        P("dom", None, None),
        P("dom", None, None, None, None),
        P("rep", "dom"),
    )
    return jax.shard_map(
        local,
        mesh=mesh,
        in_specs=placed,
        out_specs=(P("rep", "dom"), P("rep", "dom"), P(None, "rep"), P(None, "rep")),
        check_vma=False,
    )
```

```python
import jax
import jax.numpy as jnp
from jax import lax
from jax.experimental import pallas as pl
from jax.experimental.pallas import tpu as pltpu
from jax.sharding import PartitionSpec as P

TILE = 128
STEP = 8
VMEM_BYTES = 12 * 1024 * 1024
F32 = jnp.float32
BF16 = jnp.bfloat16
IN_VMEM = pl.BlockSpec(memory_space=pltpu.VMEM)
IN_SMEM = pl.BlockSpec(memory_space=pltpu.SMEM)
IN_HBM = pl.BlockSpec(memory_space=pltpu.HBM)


def lanes(index, width):
    return pl.ds(pl.multiple_of(index * width, width), width)


def call(body, scalars, args, out_shape, scratch=(), micros=1.0, hbm=(), hbm_out=()):
    many = isinstance(out_shape, list)
    out_specs = [IN_HBM if i in hbm_out else IN_VMEM for i in range(len(out_shape) if many else 1)]
    out_specs = out_specs if many else out_specs[0]
    args = [pinned(arg) if i in hbm else arg for i, arg in enumerate(args)]
    return pl.pallas_call(
        body,
        in_specs=[IN_SMEM] * len(scalars) + [IN_HBM if i in hbm else IN_VMEM for i in range(len(args))],
        out_shape=out_shape,
        out_specs=out_specs,
        scratch_shapes=scratch,
        compiler_params=pltpu.CompilerParams(vmem_limit_bytes=VMEM_BYTES),
        cost_estimate=pl.CostEstimate(flops=int(micros * 1.1e9), bytes_accessed=1 << 16, transcendentals=0),
    )(*scalars, *args)


def shape(dims, kind):
    return jax.ShapeDtypeStruct(dims, kind)


def in_hbm(dims, kind):
    return pltpu.HBM(dims, kind)


def pinned(value):
    return pltpu.with_memory_space_constraint(value, pltpu.HBM)


def dot(left, right, left_dim, right_dim):
    return lax.dot_general(left, right, (((left_dim,), (right_dim,)), ((), ())), preferred_element_type=F32)


def pick_body(send_ref, feats_hbm, out_ref, feats_ref, buf_ref, sems, feats_sem):
    chans = feats_ref.shape[0]
    load = pltpu.make_async_copy(feats_hbm, feats_ref, feats_sem)
    load.start()
    load.wait()
    parts = buf_ref.shape[0]
    for step in range(parts // STEP):
        for item in range(step * STEP, (step + 1) * STEP):
            for slot in range(2):
                block = send_ref[slot, item]
                buf_ref[item, slot * chans : (slot + 1) * chans, :] = feats_ref[:, lanes(block, TILE)]
        rows = pl.ds(step * STEP, STEP)
        pltpu.make_async_copy(buf_ref.at[rows], out_ref.at[rows], sems.at[step]).start()
    for step in range(parts // STEP):
        rows = pl.ds(step * STEP, STEP)
        pltpu.make_async_copy(buf_ref.at[rows], out_ref.at[rows], sems.at[step]).wait()


def tile_copy(far_hbm, far_ref, sems, step):
    rows = pl.ds(step * STEP, STEP)
    return pltpu.make_async_copy(far_hbm.at[rows], far_ref.at[rows], sems.at[step])


def chunk_body(rep_ref, feats_ref, cot_ref, *outs):
    reps = len(outs) // 2
    width = outs[0].shape[1]
    for k in range(reps):
        chunk = lax.rem(rep_ref[0] + k, reps)
        outs[k][...] = feats_ref[:, lanes(chunk, width)]
        outs[reps + k][...] = cot_ref[:, lanes(chunk, width)]


def near_body(cols_ref, rows_ref, feats_ref, near_ref, far_ref, acc_ref, div_ref, turned_hbm, turned_ref, sems):
    ones = jnp.ones((8, TILE), BF16)
    div_ref[...] = jnp.ones_like(div_ref)

    @pl.loop(0, near_ref.shape[0] // 4)
    def _(step):
        for item in range(4):
            row = step * 4 + item
            total = None
            sums = None
            for link in range(2):
                tile = near_ref[row, link]
                term = dot(feats_ref[:, lanes(cols_ref[link, row], TILE)], tile, 1, 1)
                part = dot(ones, tile, 1, 1)
                total = term if total is None else total + term
                sums = part if sums is None else sums + part
            acc_ref[:, lanes(row, TILE)] = total
            div_ref[:, lanes(row, TILE)] += sums

    @pl.loop(0, far_ref.shape[0] // STEP)
    def _(step):
        for item in range(STEP):
            for slot in range(2):
                part = step * STEP + item
                row = rows_ref[slot, part]
                turned = far_ref[part, slot].T
                turned_ref[part, slot] = turned
                div_ref[:, lanes(row, TILE)] += dot(ones, turned, 1, 0)
        tile_copy(turned_ref, turned_hbm, sems, step).start()

    for step in range(far_ref.shape[0] // STEP):
        tile_copy(turned_ref, turned_hbm, sems, step).wait()


def far_body(rep_ref, rows_ref, got_ref, far_hbm, near_acc_hbm, div_hbm, *rest):
    outs = rest[:4]
    acc_ref, near_acc_ref, far_ref, div_ref, sems, acc_sem, div_sem = rest[4:]
    reps = len(outs)
    chans = acc_ref.shape[0]
    width = outs[0].shape[1]
    load_acc = pltpu.make_async_copy(near_acc_hbm, near_acc_ref, acc_sem)
    load_div = pltpu.make_async_copy(div_hbm, div_ref, div_sem)
    for step in range(far_ref.shape[0] // STEP):
        tile_copy(far_hbm, far_ref, sems, step).start()
    load_acc.start()
    load_div.start()
    acc_ref[...] = jnp.zeros_like(acc_ref)

    @pl.loop(0, far_ref.shape[0] // STEP)
    def _(step):
        tile_copy(far_hbm, far_ref, sems, step).wait()
        for item in range(STEP):
            for slot in range(2):
                part = step * STEP + item
                row = rows_ref[slot, part]
                block = got_ref[part, slot * chans : (slot + 1) * chans, :]
                acc_ref[:, lanes(row, TILE)] += dot(block, far_ref[part, slot], 1, 0)

    load_acc.wait()
    load_div.wait()
    for k in range(reps):
        where = lanes(lax.rem(rep_ref[0] + k, reps), width)
        outs[k][...] = ((near_acc_ref[:, where] + acc_ref[:, where]) / div_ref[0:1, where]).astype(BF16)


def gather_rows(ref, pieces, rep):
    reps = len(pieces)
    rows = pieces[0].shape[0]
    for k in range(reps):
        source = lax.rem(rep + reps - k, reps)
        ref[lanes(source, rows), :] = pieces[k][...]


def dense_body(rep_ref, *refs):
    agg, feats, cot, wts = refs[0:4], refs[4:8], refs[8:12], refs[12:16]
    div_ref = refs[16]
    scaled_out, out_out, grad_hbm, slices_hbm = refs[17:21], refs[21:25], refs[25], refs[26]
    back_ref, full_feats, full_agg, grad_ref, out_buf, prod_ref, slices_ref = refs[27:34]
    out_sems, grad_sem, slices_sem = refs[34:37]
    rep = rep_ref[0]
    reps = 4
    rows, width = agg[0].shape
    gather_rows(full_feats, feats, rep)
    gather_rows(full_agg, agg, rep)
    copies = []

    def leave(source, target, sem):
        copies.append(pltpu.make_async_copy(source, target, sem))
        copies[-1].start()

    for k in range(reps):
        preact = dot(wts[k][0], full_feats[...], 1, 0) + dot(wts[k][1], full_agg[...], 1, 0)
        gate = jax.nn.sigmoid(preact)
        slope = gate * (1.0 + preact * (1.0 - gate))
        grad_ref[k * rows : (k + 1) * rows, :] = (cot[k][...].astype(F32) * slope).astype(BF16)
        out_buf[k] = (preact * gate).astype(BF16)
        leave(out_buf.at[k], out_out[k], out_sems.at[k])
    leave(grad_ref, grad_hbm, grad_sem)
    for which, full in ((0, full_feats), (1, full_agg)):
        prod_ref[...] = dot(grad_ref[...], full[...], 1, 1)
        wide = prod_ref.shape[1]
        for part in range(slices_ref.shape[0]):
            for k in range(reps):
                start = k * rows + 8 * part
                slices_ref[part, 8 * k : 8 * k + 8, which * wide : (which + 1) * wide] = prod_ref[
                    start : start + 8, :
                ].astype(BF16)
    leave(slices_ref, slices_hbm, slices_sem)
    w_neigh = jnp.concatenate([wts[k][1] for k in range(reps)], axis=0)
    back_ref[...] = dot(w_neigh, grad_ref[...], 0, 0)
    div = div_ref[0:1, lanes(rep, width)]
    for k in range(reps):
        target = lax.rem(rep + k, reps)
        scaled_out[k][...] = (back_ref[lanes(target, rows), :] / div).astype(BF16)
    for copy in copies:
        copy.wait()


def back_body(rep_ref, *refs):
    wts, grad_ref, back_out, back_ref = refs[0:4], refs[4], refs[5:9], refs[9]
    rep = rep_ref[0]
    reps = 4
    rows = back_out[0].shape[0]
    w_self = jnp.concatenate([wts[k][0] for k in range(reps)], axis=0)
    back_ref[...] = dot(w_self, grad_ref[...], 0, 0)
    for k in range(reps):
        target = lax.rem(rep + k, reps)
        back_out[k][...] = back_ref[lanes(target, rows), :]


def slice_sum_body(got_ref, *outs):
    total = jnp.sum(got_ref[...].astype(F32), axis=0)
    for k in range(len(outs)):
        outs[k][...] = total[8 * k : 8 * k + 8, :]


def add_body(*refs):
    total = refs[0][...]
    for ref in refs[1:-1]:
        total = total + ref[...]
    refs[-1][...] = total


def stack_body(*refs):
    rows = refs[0].shape[0]
    for k, ref in enumerate(refs[:-1]):
        refs[-1][rows * k : rows * (k + 1), :] = ref[...]


def join_body(place_ref, mine_ref, own_ref, other_ref, w_self_ref, w_neigh_ref):
    full = w_self_ref.shape[1]
    core = lax.rem(place_ref[1], 2)
    place = lax.rem(lax.div(place_ref[1], 2), 8)
    sign = 1 - 2 * core

    def put(place, piece):
        rows = lanes(place, 8)
        w_self_ref[rows, :] = piece[:, :full]
        w_neigh_ref[rows, :] = piece[:, full:]

    put(place, mine_ref[...])
    for k in range(1, 5):
        rows = slice(8 * (k - 1), 8 * k)
        put(lax.rem(place + 8 - sign * k, 8), own_ref[rows, :])
        put(lax.rem(place + 8 + sign * k, 8), other_ref[rows, :])


def gather_lanes(ref, pieces, rep):
    reps = len(pieces)
    width = pieces[0].shape[1]
    for k in range(reps):
        source = lax.rem(rep + reps - k, reps)
        ref[:, lanes(source, width)] = pieces[k][...]


def far_back_body(rep_ref, rows_ref, s0, s1, s2, s3, far_hbm, out_ref, full_ref, buf_ref, far_ref, sems, out_sems):
    chans = full_ref.shape[0]
    parts = far_ref.shape[0]
    for step in range(parts // STEP):
        tile_copy(far_hbm, far_ref, sems, step).start()
    gather_lanes(full_ref, (s0, s1, s2, s3), rep_ref[0])

    def copy(step):
        rows = pl.ds(step * STEP, STEP)
        return pltpu.make_async_copy(
            buf_ref.at[rows], out_ref.at[rows], out_sems.at[step]
        )

    @pl.loop(0, parts // STEP)
    def _(step):
        tile_copy(far_hbm, far_ref, sems, step).wait()
        for item in range(STEP):
            for slot in range(2):
                part = step * STEP + item
                row = rows_ref[slot, part]
                term = dot(full_ref[:, lanes(row, TILE)], far_ref[part, slot], 1, 0)
                buf_ref[part, slot * chans : (slot + 1) * chans, :] = term.astype(BF16)
        copy(step).start()

    for step in range(parts // STEP):
        copy(step).wait()


def near_back_body(rep_ref, cols_ref, *refs):
    scaled, back, outs = refs[0:4], refs[4:8], refs[8:12]
    near_ref, acc_ref, output_ref, full_ref = refs[12:16]
    rep = rep_ref[0]
    reps = 4
    width = scaled[0].shape[1]
    gather_lanes(full_ref, scaled, rep)
    gather_lanes(acc_ref, back, rep)
    for k in range(reps):
        output_ref[:, lanes(lax.rem(rep + k, reps), width)] = outs[k][...]

    @pl.loop(0, near_ref.shape[0] // 4)
    def _(step):
        for item in range(4):
            row = step * 4 + item
            for link in range(2):
                term = dot(full_ref[:, lanes(row, TILE)], near_ref[row, link], 1, 0)
                acc_ref[:, lanes(cols_ref[link, row], TILE)] += term


def home_body(send_ref, got_ref, near_acc_hbm, grad_ref, acc_ref, near_acc_ref, sem):
    chans = acc_ref.shape[0]
    parts = got_ref.shape[0]
    load = pltpu.make_async_copy(near_acc_hbm, near_acc_ref, sem)
    load.start()
    acc_ref[...] = jnp.zeros_like(acc_ref)
    for item in range(parts):
        for slot in range(2):
            block = send_ref[slot, item]
            acc_ref[:, lanes(block, TILE)] += got_ref[item, slot * chans : (slot + 1) * chans, :].astype(F32)
    load.wait()
    grad_ref[...] = (near_acc_ref[...] + acc_ref[...]).astype(BF16)


def local(feats, w_self, w_neigh, local_cols, local_tiles, send_list, remote_rows, remote_tiles, cotangent):
    chans, nodes = feats.shape
    full = w_self.shape[0]
    reps = full // chans
    width = nodes // reps
    parts = remote_tiles.shape[1]
    far_tiles = remote_tiles[0]
    rows = remote_rows[0].T
    sends = send_list[0].T
    cols = local_cols.T
    rep = jnp.stack([lax.axis_index("rep"), lax.axis_index("dom")]).astype(jnp.int32)
    piece = shape((chans, width), BF16)
    piece32 = shape((chans, width), F32)
    sems = pltpu.SemaphoreType.DMA((parts // STEP,))
    sem = pltpu.SemaphoreType.DMA(())
    tile_buf = pltpu.VMEM(far_tiles.shape, BF16)
    wide32 = pltpu.VMEM((chans, nodes), F32)

    def shift(value, by):
        return lax.ppermute(value, "rep", [(i, (i + by) % reps) for i in range(reps)])

    def move(value, dy, dz, dc, turn=False):
        pairs = [
            ((y * 8 + z) * 2 + c, ((y + dy) % 4 * 8 + (z + (-dz if turn and c else dz)) % 8) * 2 + (c + dc) % 2)
            for y in range(4)
            for z in range(8)
            for c in range(2)
        ]
        return lax.ppermute(value, "dom", pairs)

    z_groups = [[(y * 8 + z) * 2 + c for z in range(8)] for y in range(4) for c in range(2)]
    def exchange(pieces, sign=1):
        return [pieces[0]] + [shift(pieces[k], (sign * k) % reps) for k in range(1, reps)]

    with jax.named_scope("pick"):
        outgoing = call(
            pick_body, (sends,), (feats,), in_hbm((parts, 2 * chans, TILE), BF16),
            [pltpu.VMEM((chans, nodes), BF16), pltpu.VMEM((parts, 2 * chans, TILE), BF16), sems, sem], 2.0, (0,), (0,),
        )
    incoming = lax.all_to_all(outgoing, "dom", split_axis=0, concat_axis=0, tiled=True)

    with jax.named_scope("chunks"):
        pieces = call(chunk_body, (rep,), (feats, cotangent), [piece] * (2 * reps))
    feats_in = exchange(pieces[:reps])
    cot_in = exchange(pieces[reps:])
    weights_in = exchange([jnp.stack([w_self.T, w_neigh.T])] * reps)
    with jax.named_scope("near"):
        near_acc, div, turned = call(
            near_body, (cols, rows), (feats, local_tiles, far_tiles),
            [shape((chans, nodes), F32), shape((8, nodes), F32), in_hbm(far_tiles.shape, BF16)],
            [tile_buf, sems], 8.0, (), (2,),
        )
    incoming, feats_in, cot_in, weights_in, near_acc, div, turned = lax.optimization_barrier(
        (incoming, feats_in, cot_in, weights_in, near_acc, div, turned)
    )
    with jax.named_scope("far"):
        agg = call(
            far_body, (rep, rows), (incoming, turned, near_acc, div), [piece] * reps,
            [wide32, wide32, tile_buf, pltpu.VMEM((8, nodes), F32), sems, sem, sem], 6.0, (1, 2, 3),
        )
    agg_in = exchange(agg)

    with jax.named_scope("dense"):
        dense = call(
            dense_body, (rep,), (*agg_in, *feats_in, *cot_in, *weights_in, div),
            [piece] * reps
            + [in_hbm((chans, width), BF16)] * reps
            + [in_hbm((full, width), BF16), in_hbm((8, 8 * reps, 2 * full), BF16)],
            [
                pltpu.VMEM((full, width), F32), pltpu.VMEM((full, width), BF16), pltpu.VMEM((full, width), BF16),
                pltpu.VMEM((full, width), BF16), pltpu.VMEM((reps, chans, width), BF16), pltpu.VMEM((full, full), F32),
                pltpu.VMEM((8, 8 * reps, 2 * full), BF16), pltpu.SemaphoreType.DMA((reps,)), sem, sem,
            ],
            3.0, (), range(reps, 2 * reps + 2),
        )
    scaled, out_pieces, grad_pre, slices = dense[:reps], dense[reps : 2 * reps], dense[2 * reps], dense[2 * reps + 1]
    scaled_in = exchange(scaled)
    slices_in = lax.all_to_all(slices, "dom", 0, 0, axis_index_groups=z_groups, tiled=True)
    with jax.named_scope("far_back"):
        far_back = call(
            far_back_body, (rep, rows), (*scaled_in, far_tiles), in_hbm((parts, 2 * chans, TILE), BF16),
            [
                pltpu.VMEM((chans, nodes), BF16), pltpu.VMEM((parts, 2 * chans, TILE), BF16), tile_buf, sems, sems,
            ],
            2.0, (reps,), (0,),
        )
    slices_in, far_back = lax.optimization_barrier((slices_in, far_back))
    returned = lax.all_to_all(far_back, "dom", split_axis=0, concat_axis=0, tiled=True)

    with jax.named_scope("slice_sums"):
        slice_shape = shape((8, 2 * full), F32)
        sums = call(slice_sum_body, (), (slices_in,), [slice_shape] * reps)
        total = call(add_body, (), exchange(sums, -1), slice_shape)
        total = call(add_body, (), (total, move(total, 0, 0, 1)), slice_shape)
        total = call(add_body, (), (total, *[move(total, dy, 0, 0) for dy in range(1, 4)]), slice_shape)
    with jax.named_scope("back"):
        back_self = call(
            back_body, (rep,), (*weights_in, grad_pre), [piece32] * reps, [pltpu.VMEM((full, width), F32)], 1.0
        )
    back_in = exchange(back_self)
    out_in = exchange(out_pieces, -1)
    with jax.named_scope("near_back"):
        near_back, output = call(
            near_back_body, (rep, cols), (*scaled_in, *back_in, *out_in, local_tiles),
            [shape((chans, nodes), F32), shape((chans, nodes), BF16)], [pltpu.VMEM((chans, nodes), BF16)], 2.0,
        )
    total, near_back, output = lax.optimization_barrier((total, near_back, output))
    with jax.named_scope("spread"):
        own = call(
            stack_body, (), [move(total, 0, dz, 0, True) for dz in range(1, 5)], shape((32, 2 * full), F32), (), 0.5
        )
        other = move(own, 0, 0, 1)
    with jax.named_scope("home"):
        grad_feats = call(
            home_body, (sends,), (returned, near_back), shape((chans, nodes), BF16), [wide32, wide32, sem], 3.0, (1,)
        )
    with jax.named_scope("join"):
        other, grad_feats = lax.optimization_barrier((other, grad_feats))
        wg_self, wg_neigh = call(join_body, (rep,), (total, own, other), [shape((chans, full), F32)] * 2)
    return output, grad_feats, wg_self.T, wg_neigh.T


def solution(mesh):
    placed = (
        P("rep", "dom"),
        P(None, "rep"),
        P(None, "rep"),
        P("dom", None),
        P("dom", None, None, None),
        P("dom", None, None),
        P("dom", None, None),
        P("dom", None, None, None, None),
        P("rep", "dom"),
    )
    return jax.shard_map(
        local,
        mesh=mesh,
        in_specs=placed,
        out_specs=(P("rep", "dom"), P("rep", "dom"), P(None, "rep"), P(None, "rep")),
        check_vma=False,
    )
```

```python
import jax
import jax.numpy as jnp
from jax import lax
from jax.experimental import pallas as pl
from jax.experimental.pallas import tpu as pltpu
from jax.sharding import PartitionSpec as P

TILE = 128
STEP = 8
VMEM_BYTES = 12 * 1024 * 1024
F32 = jnp.float32
BF16 = jnp.bfloat16
IN_VMEM = pl.BlockSpec(memory_space=pltpu.VMEM)
IN_SMEM = pl.BlockSpec(memory_space=pltpu.SMEM)
IN_HBM = pl.BlockSpec(memory_space=pltpu.HBM)


def lanes(index, width):
    return pl.ds(pl.multiple_of(index * width, width), width)


def call(body, scalars, args, out_shape, scratch=(), micros=1.0, hbm=(), hbm_out=()):
    many = isinstance(out_shape, list)
    out_specs = [IN_HBM if i in hbm_out else IN_VMEM for i in range(len(out_shape) if many else 1)]
    out_specs = out_specs if many else out_specs[0]
    args = [pinned(arg) if i in hbm else arg for i, arg in enumerate(args)]
    return pl.pallas_call(
        body,
        in_specs=[IN_SMEM] * len(scalars) + [IN_HBM if i in hbm else IN_VMEM for i in range(len(args))],
        out_shape=out_shape,
        out_specs=out_specs,
        scratch_shapes=scratch,
        compiler_params=pltpu.CompilerParams(vmem_limit_bytes=VMEM_BYTES),
        cost_estimate=pl.CostEstimate(flops=int(micros * 1.1e9), bytes_accessed=1 << 16, transcendentals=0),
    )(*scalars, *args)


def shape(dims, kind):
    return jax.ShapeDtypeStruct(dims, kind)


def in_hbm(dims, kind):
    return pltpu.HBM(dims, kind)


def pinned(value):
    return pltpu.with_memory_space_constraint(value, pltpu.HBM)


def dot(left, right, left_dim, right_dim):
    return lax.dot_general(left, right, (((left_dim,), (right_dim,)), ((), ())), preferred_element_type=F32)


def pick_body(send_ref, feats_hbm, out_ref, feats_ref, buf_ref, sems, feats_sem):
    chans = feats_ref.shape[0]
    load = pltpu.make_async_copy(feats_hbm, feats_ref, feats_sem)
    load.start()
    load.wait()
    parts = buf_ref.shape[0]
    for step in range(parts // STEP):
        for item in range(step * STEP, (step + 1) * STEP):
            for slot in range(2):
                block = send_ref[slot, item]
                buf_ref[item, slot * chans : (slot + 1) * chans, :] = feats_ref[:, lanes(block, TILE)]
        rows = pl.ds(step * STEP, STEP)
        pltpu.make_async_copy(buf_ref.at[rows], out_ref.at[rows], sems.at[step]).start()
    for step in range(parts // STEP):
        rows = pl.ds(step * STEP, STEP)
        pltpu.make_async_copy(buf_ref.at[rows], out_ref.at[rows], sems.at[step]).wait()


def tile_copy(far_hbm, far_ref, sems, step):
    rows = pl.ds(step * STEP, STEP)
    return pltpu.make_async_copy(far_hbm.at[rows], far_ref.at[rows], sems.at[step])


def chunk_body(rep_ref, feats_ref, cot_ref, *outs):
    reps = len(outs) // 2
    width = outs[0].shape[1]
    for k in range(reps):
        chunk = lax.rem(rep_ref[0] + k, reps)
        outs[k][...] = feats_ref[:, lanes(chunk, width)]
        outs[reps + k][...] = cot_ref[:, lanes(chunk, width)]


def near_body(cols_ref, rows_ref, feats_ref, near_ref, far_ref, acc_ref, div_ref, turned_hbm, turned_ref, sems):
    ones = jnp.ones((8, TILE), BF16)
    div_ref[...] = jnp.ones_like(div_ref)

    @pl.loop(0, near_ref.shape[0] // 4)
    def _(step):
        for item in range(4):
            row = step * 4 + item
            total = None
            sums = None
            for link in range(2):
                tile = near_ref[row, link]
                term = dot(feats_ref[:, lanes(cols_ref[link, row], TILE)], tile, 1, 1)
                part = dot(ones, tile, 1, 1)
                total = term if total is None else total + term
                sums = part if sums is None else sums + part
            acc_ref[:, lanes(row, TILE)] = total
            div_ref[:, lanes(row, TILE)] += sums

    @pl.loop(0, far_ref.shape[0] // STEP)
    def _(step):
        for item in range(STEP):
            for slot in range(2):
                part = step * STEP + item
                row = rows_ref[slot, part]
                turned = far_ref[part, slot].T
                turned_ref[part, slot] = turned
                div_ref[:, lanes(row, TILE)] += dot(ones, turned, 1, 0)
        tile_copy(turned_ref, turned_hbm, sems, step).start()

    for step in range(far_ref.shape[0] // STEP):
        tile_copy(turned_ref, turned_hbm, sems, step).wait()


def far_body(rep_ref, rows_ref, got_ref, far_hbm, near_acc_hbm, div_hbm, *rest):
    outs = rest[:4]
    acc_ref, near_acc_ref, far_ref, div_ref, sems, acc_sem, div_sem = rest[4:]
    reps = len(outs)
    chans = acc_ref.shape[0]
    width = outs[0].shape[1]
    load_acc = pltpu.make_async_copy(near_acc_hbm, near_acc_ref, acc_sem)
    load_div = pltpu.make_async_copy(div_hbm, div_ref, div_sem)
    for step in range(far_ref.shape[0] // STEP):
        tile_copy(far_hbm, far_ref, sems, step).start()
    load_acc.start()
    load_div.start()
    acc_ref[...] = jnp.zeros_like(acc_ref)

    @pl.loop(0, far_ref.shape[0] // STEP)
    def _(step):
        tile_copy(far_hbm, far_ref, sems, step).wait()
        for item in range(STEP):
            for slot in range(2):
                part = step * STEP + item
                row = rows_ref[slot, part]
                block = got_ref[part, slot * chans : (slot + 1) * chans, :]
                acc_ref[:, lanes(row, TILE)] += dot(block, far_ref[part, slot], 1, 0)

    load_acc.wait()
    load_div.wait()
    for k in range(reps):
        where = lanes(lax.rem(rep_ref[0] + k, reps), width)
        outs[k][...] = ((near_acc_ref[:, where] + acc_ref[:, where]) / div_ref[0:1, where]).astype(BF16)


def gather_rows(ref, pieces, rep):
    reps = len(pieces)
    rows = pieces[0].shape[0]
    for k in range(reps):
        source = lax.rem(rep + reps - k, reps)
        ref[lanes(source, rows), :] = pieces[k][...]


def dense_body(rep_ref, *refs):
    agg, feats, cot, wts = refs[0:4], refs[4:8], refs[8:12], refs[12:16]
    div_ref = refs[16]
    scaled_out, out_out, grad_hbm, slices_out = refs[17:21], refs[21:25], refs[25], refs[26:30]
    back_ref, full_feats, full_agg, grad_ref, out_buf, prod_ref, kept_ref = refs[30:37]
    out_sems, grad_sem, kept_sem = refs[37:40]
    low = lax.rem(lax.div(rep_ref[1], 2), 4)
    rep = rep_ref[0]
    reps = 4
    rows, width = agg[0].shape
    gather_rows(full_feats, feats, rep)
    gather_rows(full_agg, agg, rep)
    copies = []

    def leave(source, target, sem):
        copies.append(pltpu.make_async_copy(source, target, sem))
        copies[-1].start()

    for k in range(reps):
        preact = dot(wts[k][0], full_feats[...], 1, 0) + dot(wts[k][1], full_agg[...], 1, 0)
        gate = jax.nn.sigmoid(preact)
        slope = gate * (1.0 + preact * (1.0 - gate))
        grad_ref[k * rows : (k + 1) * rows, :] = (cot[k][...].astype(F32) * slope).astype(BF16)
        out_buf[k] = (preact * gate).astype(BF16)
        leave(out_buf.at[k], out_out[k], out_sems.at[k])
    leave(grad_ref, grad_hbm, grad_sem)
    for which, full in ((0, full_feats), (1, full_agg)):
        prod_ref[...] = dot(grad_ref[...], full[...], 1, 1)
        wide = prod_ref.shape[1]
        for part in range(4):
            target = lax.rem(low + part, 4)
            slice_ref = slices_out[part] if part else kept_ref
            for k in range(reps):
                start = pl.multiple_of(k * rows + 16 * target, 16)
                slice_ref[16 * k : 16 * k + 16, which * wide : (which + 1) * wide] = prod_ref[
                    pl.ds(start, 16), :
                ].astype(BF16)
    leave(kept_ref, slices_out[0], kept_sem)
    w_neigh = jnp.concatenate([wts[k][1] for k in range(reps)], axis=0)
    back_ref[...] = dot(w_neigh, grad_ref[...], 0, 0)
    div = div_ref[0:1, lanes(rep, width)]
    for k in range(reps):
        target = lax.rem(rep + k, reps)
        scaled_out[k][...] = (back_ref[lanes(target, rows), :] / div).astype(BF16)
    for copy in copies:
        copy.wait()


def back_body(rep_ref, *refs):
    wts, grad_ref, back_out, back_ref = refs[0:4], refs[4], refs[5:9], refs[9]
    rep = rep_ref[0]
    reps = 4
    rows = back_out[0].shape[0]
    w_self = jnp.concatenate([wts[k][0] for k in range(reps)], axis=0)
    back_ref[...] = dot(w_self, grad_ref[...], 0, 0)
    for k in range(reps):
        target = lax.rem(rep + k, reps)
        back_out[k][...] = back_ref[lanes(target, rows), :]


def slice_sum_body(*refs):
    pieces, outs = refs[:4], refs[4:]
    total = pieces[0][...].astype(F32)
    for piece in pieces[1:]:
        total = total + piece[...].astype(F32)
    for k in range(len(outs)):
        outs[k][...] = total[16 * k : 16 * k + 16, :]


def add_body(*refs):
    total = refs[0][...]
    for ref in refs[1:-1]:
        total = total + ref[...]
    refs[-1][...] = total.astype(refs[-1].dtype)


def stack_body(*refs):
    rows = refs[0].shape[0]
    for k, ref in enumerate(refs[:-1]):
        refs[-1][rows * k : rows * (k + 1), :] = ref[...]


def join_body(place_ref, mine_ref, own_ref, other_ref, w_self_ref, w_neigh_ref, parts_ref):
    full = w_self_ref.shape[1]
    core = lax.rem(place_ref[1], 2)
    place = lax.rem(lax.div(place_ref[1], 2), 8)
    sign = 1 - 2 * core
    parts_ref[place] = mine_ref[...].astype(F32)
    for k in range(1, 5):
        rows = slice(16 * (k - 1), 16 * k)
        parts_ref[lax.rem(place + 8 - sign * k, 8)] = own_ref[rows, :].astype(F32)
        parts_ref[lax.rem(place + 8 + sign * k, 8)] = other_ref[rows, :].astype(F32)
    for low in range(4):
        total = parts_ref[low] + parts_ref[low + 4]
        w_self_ref[16 * low : 16 * low + 16, :] = total[:, :full]
        w_neigh_ref[16 * low : 16 * low + 16, :] = total[:, full:]


def gather_lanes(ref, pieces, rep):
    reps = len(pieces)
    width = pieces[0].shape[1]
    for k in range(reps):
        source = lax.rem(rep + reps - k, reps)
        ref[:, lanes(source, width)] = pieces[k][...]


def far_back_body(rep_ref, rows_ref, s0, s1, s2, s3, far_hbm, out_ref, full_ref, buf_ref, far_ref, sems, out_sems):
    chans = full_ref.shape[0]
    parts = far_ref.shape[0]
    for step in range(parts // STEP):
        tile_copy(far_hbm, far_ref, sems, step).start()
    gather_lanes(full_ref, (s0, s1, s2, s3), rep_ref[0])

    def copy(step):
        rows = pl.ds(step * STEP, STEP)
        return pltpu.make_async_copy(
            buf_ref.at[rows], out_ref.at[rows], out_sems.at[step]
        )

    @pl.loop(0, parts // STEP)
    def _(step):
        tile_copy(far_hbm, far_ref, sems, step).wait()
        for item in range(STEP):
            for slot in range(2):
                part = step * STEP + item
                row = rows_ref[slot, part]
                term = dot(full_ref[:, lanes(row, TILE)], far_ref[part, slot], 1, 0)
                buf_ref[part, slot * chans : (slot + 1) * chans, :] = term.astype(BF16)
        copy(step).start()

    for step in range(parts // STEP):
        copy(step).wait()


def near_back_body(rep_ref, cols_ref, *refs):
    scaled, back, outs = refs[0:4], refs[4:8], refs[8:12]
    near_ref, acc_ref, output_ref, full_ref = refs[12:16]
    rep = rep_ref[0]
    reps = 4
    width = scaled[0].shape[1]
    gather_lanes(full_ref, scaled, rep)
    gather_lanes(acc_ref, back, rep)
    for k in range(reps):
        output_ref[:, lanes(lax.rem(rep + k, reps), width)] = outs[k][...]

    @pl.loop(0, near_ref.shape[0] // 4)
    def _(step):
        for item in range(4):
            row = step * 4 + item
            for link in range(2):
                term = dot(full_ref[:, lanes(row, TILE)], near_ref[row, link], 1, 0)
                acc_ref[:, lanes(cols_ref[link, row], TILE)] += term


def home_body(send_ref, got_ref, near_acc_hbm, grad_ref, acc_ref, near_acc_ref, sem):
    chans = acc_ref.shape[0]
    parts = got_ref.shape[0]
    load = pltpu.make_async_copy(near_acc_hbm, near_acc_ref, sem)
    load.start()
    acc_ref[...] = jnp.zeros_like(acc_ref)
    for item in range(parts):
        for slot in range(2):
            block = send_ref[slot, item]
            acc_ref[:, lanes(block, TILE)] += got_ref[item, slot * chans : (slot + 1) * chans, :].astype(F32)
    load.wait()
    grad_ref[...] = (near_acc_ref[...] + acc_ref[...]).astype(BF16)


def local(feats, w_self, w_neigh, local_cols, local_tiles, send_list, remote_rows, remote_tiles, cotangent):
    chans, nodes = feats.shape
    full = w_self.shape[0]
    reps = full // chans
    width = nodes // reps
    parts = remote_tiles.shape[1]
    far_tiles = remote_tiles[0]
    rows = remote_rows[0].T
    sends = pinned(send_list[0].T)
    cols = local_cols.T
    rep = jnp.stack([lax.axis_index("rep"), lax.axis_index("dom")]).astype(jnp.int32)
    piece = shape((chans, width), BF16)
    piece32 = shape((chans, width), F32)
    sems = pltpu.SemaphoreType.DMA((parts // STEP,))
    sem = pltpu.SemaphoreType.DMA(())
    tile_buf = pltpu.VMEM(far_tiles.shape, BF16)
    wide32 = pltpu.VMEM((chans, nodes), F32)

    def shift(value, by):
        return lax.ppermute(value, "rep", [(i, (i + by) % reps) for i in range(reps)])

    def move(value, dy, dz, dc, turn=False):
        pairs = [
            ((y * 8 + z) * 2 + c, ((y + dy) % 4 * 8 + (z + (-dz if turn and c else dz)) % 8) * 2 + (c + dc) % 2)
            for y in range(4)
            for z in range(8)
            for c in range(2)
        ]
        return lax.ppermute(value, "dom", pairs)

    def move_low(value, k):
        pairs = [
            ((y * 8 + z) * 2 + c, (y * 8 + z // 4 * 4 + (z + k) % 4) * 2 + c)
            for y in range(4)
            for z in range(8)
            for c in range(2)
        ]
        return lax.ppermute(value, "dom", pairs)

    def exchange(pieces, sign=1):
        return [pieces[0]] + [shift(pieces[k], (sign * k) % reps) for k in range(1, reps)]

    with jax.named_scope("pick"):
        outgoing = call(
            pick_body, (sends,), (feats,), in_hbm((parts, 2 * chans, TILE), BF16),
            [pltpu.VMEM((chans, nodes), BF16), pltpu.VMEM((parts, 2 * chans, TILE), BF16), sems, sem], 2.0, (0,), (0,),
        )
    incoming = lax.all_to_all(outgoing, "dom", split_axis=0, concat_axis=0, tiled=True)

    with jax.named_scope("chunks"):
        pieces = call(chunk_body, (rep,), (feats, cotangent), [piece] * (2 * reps))
    feats_in = exchange(pieces[:reps])
    cot_in = exchange(pieces[reps:])
    weights_in = exchange([jnp.stack([w_self.T, w_neigh.T])] * reps)
    with jax.named_scope("near"):
        near_acc, div, turned = call(
            near_body, (cols, rows), (feats, local_tiles, far_tiles),
            [shape((chans, nodes), F32), shape((8, nodes), F32), in_hbm(far_tiles.shape, BF16)],
            [tile_buf, sems], 8.0, (), (2,),
        )
    incoming, feats_in, cot_in, weights_in, near_acc, div, turned = lax.optimization_barrier(
        (incoming, feats_in, cot_in, weights_in, near_acc, div, turned)
    )
    with jax.named_scope("far"):
        agg = call(
            far_body, (rep, rows), (incoming, turned, near_acc, div), [piece] * reps,
            [wide32, wide32, tile_buf, pltpu.VMEM((8, nodes), F32), sems, sem, sem], 6.0, (1, 2, 3),
        )
    agg_in = exchange(agg)

    with jax.named_scope("dense"):
        dense = call(
            dense_body, (rep,), (*agg_in, *feats_in, *cot_in, *weights_in, div),
            [piece] * reps
            + [in_hbm((chans, width), BF16)] * reps
            + [in_hbm((full, width), BF16), in_hbm((16 * reps, 2 * full), BF16)]
            + [shape((16 * reps, 2 * full), BF16)] * 3,
            [
                pltpu.VMEM((full, width), F32), pltpu.VMEM((full, width), BF16), pltpu.VMEM((full, width), BF16),
                pltpu.VMEM((full, width), BF16), pltpu.VMEM((reps, chans, width), BF16), pltpu.VMEM((full, full), F32),
                pltpu.VMEM((16 * reps, 2 * full), BF16), pltpu.SemaphoreType.DMA((reps,)), sem, sem,
            ],
            3.0, (), range(reps, 2 * reps + 2),
        )
    scaled, out_pieces, grad_pre, slices = dense[:reps], dense[reps : 2 * reps], dense[2 * reps], dense[2 * reps + 1 :]
    scaled_in = exchange(scaled)
    slices_in = [slices[0]] + [move_low(slices[k], k) for k in range(1, 4)]
    with jax.named_scope("far_back"):
        far_back = call(
            far_back_body, (rep, rows), (*scaled_in, far_tiles), in_hbm((parts, 2 * chans, TILE), BF16),
            [
                pltpu.VMEM((chans, nodes), BF16), pltpu.VMEM((parts, 2 * chans, TILE), BF16), tile_buf, sems, sems,
            ],
            5.0, (reps,), (0,),
        )
    slices_in, far_back = lax.optimization_barrier((slices_in, far_back))
    returned = lax.all_to_all(far_back, "dom", split_axis=0, concat_axis=0, tiled=True)

    with jax.named_scope("slice_sums"):
        slice_shape = shape((16, 2 * full), F32)
        sums = call(slice_sum_body, (), slices_in, [slice_shape] * reps)
        total = call(add_body, (), exchange(sums, -1), slice_shape)
        total = call(add_body, (), (total, move(total, 0, 0, 1)), slice_shape)
        others = [move(total, dy, 0, 0) for dy in range(1, 4)]
        total = call(add_body, (), (total, *others), shape((16, 2 * full), BF16))
    with jax.named_scope("back"):
        back_self = call(
            back_body, (rep,), (*weights_in, grad_pre), [piece32] * reps, [pltpu.VMEM((full, width), F32)], 1.0
        )
    back_in = exchange(back_self)
    out_in = exchange(out_pieces, -1)
    with jax.named_scope("near_back"):
        near_back, output = call(
            near_back_body, (rep, cols), (*scaled_in, *back_in, *out_in, local_tiles),
            [shape((chans, nodes), F32), shape((chans, nodes), BF16)], [pltpu.VMEM((chans, nodes), BF16)], 2.0,
        )
    total, near_back, output = lax.optimization_barrier((total, near_back, output))
    with jax.named_scope("spread"):
        own = call(
            stack_body, (), [move(total, 0, dz, 0, True) for dz in range(1, 5)], shape((64, 2 * full), BF16), (), 0.5
        )
        other = move(own, 0, 0, 1)
    with jax.named_scope("home"):
        grad_feats = call(
            home_body, (sends,), (returned, near_back), shape((chans, nodes), BF16), [wide32, wide32, sem], 3.0, (1,)
        )
    with jax.named_scope("join"):
        other, grad_feats = lax.optimization_barrier((other, grad_feats))
        wg_self, wg_neigh = call(
            join_body, (rep,), (total, own, other), [shape((chans, full), F32)] * 2, [pltpu.VMEM((8, 16, 2 * full), F32)]
        )
    return output, grad_feats, wg_self.T, wg_neigh.T


def solution(mesh):
    placed = (
        P("rep", "dom"),
        P(None, "rep"),
        P(None, "rep"),
        P("dom", None),
        P("dom", None, None, None),
        P("dom", None, None),
        P("dom", None, None),
        P("dom", None, None, None, None),
        P("rep", "dom"),
    )
    return jax.shard_map(
        local,
        mesh=mesh,
        in_specs=placed,
        out_specs=(P("rep", "dom"), P("rep", "dom"), P(None, "rep"), P(None, "rep")),
        check_vma=False,
    )
```

```python
import jax
import jax.numpy as jnp
from jax import lax
from jax.experimental import pallas as pl
from jax.experimental.pallas import tpu as pltpu
from jax.sharding import PartitionSpec as P

TILE = 128
STEP = 8
VMEM_BYTES = 12 * 1024 * 1024
F32 = jnp.float32
BF16 = jnp.bfloat16
IN_VMEM = pl.BlockSpec(memory_space=pltpu.VMEM)
IN_SMEM = pl.BlockSpec(memory_space=pltpu.SMEM)
IN_HBM = pl.BlockSpec(memory_space=pltpu.HBM)


def lanes(index, width):
    return pl.ds(pl.multiple_of(index * width, width), width)


def call(body, scalars, args, out_shape, scratch=(), micros=1.0, hbm=(), hbm_out=()):
    many = isinstance(out_shape, list)
    out_specs = [IN_HBM if i in hbm_out else IN_VMEM for i in range(len(out_shape) if many else 1)]
    out_specs = out_specs if many else out_specs[0]
    args = [pinned(arg) if i in hbm else arg for i, arg in enumerate(args)]
    return pl.pallas_call(
        body,
        in_specs=[IN_SMEM] * len(scalars) + [IN_HBM if i in hbm else IN_VMEM for i in range(len(args))],
        out_shape=out_shape,
        out_specs=out_specs,
        scratch_shapes=scratch,
        compiler_params=pltpu.CompilerParams(vmem_limit_bytes=VMEM_BYTES),
        cost_estimate=pl.CostEstimate(flops=int(micros * 1.1e9), bytes_accessed=1 << 16, transcendentals=0),
    )(*scalars, *args)


def shape(dims, kind):
    return jax.ShapeDtypeStruct(dims, kind)


def in_hbm(dims, kind):
    return pltpu.HBM(dims, kind)


def pinned(value):
    return pltpu.with_memory_space_constraint(value, pltpu.HBM)


def dot(left, right, left_dim, right_dim):
    return lax.dot_general(left, right, (((left_dim,), (right_dim,)), ((), ())), preferred_element_type=F32)


def pick_body(send_ref, feats_hbm, out_ref, feats_ref, buf_ref, sems, feats_sem):
    chans = feats_ref.shape[0]
    load = pltpu.make_async_copy(feats_hbm, feats_ref, feats_sem)
    load.start()
    load.wait()
    parts = buf_ref.shape[0]
    for step in range(parts // STEP):
        for item in range(step * STEP, (step + 1) * STEP):
            for slot in range(2):
                block = send_ref[slot, item]
                buf_ref[item, slot * chans : (slot + 1) * chans, :] = feats_ref[:, lanes(block, TILE)]
        rows = pl.ds(step * STEP, STEP)
        pltpu.make_async_copy(buf_ref.at[rows], out_ref.at[rows], sems.at[step]).start()
    for step in range(parts // STEP):
        rows = pl.ds(step * STEP, STEP)
        pltpu.make_async_copy(buf_ref.at[rows], out_ref.at[rows], sems.at[step]).wait()


def tile_copy(far_hbm, far_ref, sems, step):
    rows = pl.ds(step * STEP, STEP)
    return pltpu.make_async_copy(far_hbm.at[rows], far_ref.at[rows], sems.at[step])


def chunk_body(rep_ref, feats_ref, cot_ref, *outs):
    reps = len(outs) // 2
    width = outs[0].shape[1]
    for k in range(reps):
        chunk = lax.rem(rep_ref[0] + k, reps)
        outs[k][...] = feats_ref[:, lanes(chunk, width)]
        outs[reps + k][...] = cot_ref[:, lanes(chunk, width)]


def near_body(cols_ref, rows_ref, feats_ref, near_ref, far_ref, acc_ref, div_ref, turned_hbm, turned_ref, sems):
    ones = jnp.ones((8, TILE), BF16)
    div_ref[...] = jnp.ones_like(div_ref)

    @pl.loop(0, near_ref.shape[0] // 4)
    def _(step):
        for item in range(4):
            row = step * 4 + item
            total = None
            sums = None
            for link in range(2):
                tile = near_ref[row, link]
                term = dot(feats_ref[:, lanes(cols_ref[link, row], TILE)], tile, 1, 1)
                part = dot(ones, tile, 1, 1)
                total = term if total is None else total + term
                sums = part if sums is None else sums + part
            acc_ref[:, lanes(row, TILE)] = total
            div_ref[:, lanes(row, TILE)] += sums

    @pl.loop(0, far_ref.shape[0] // STEP)
    def _(step):
        for item in range(STEP):
            for slot in range(2):
                part = step * STEP + item
                row = rows_ref[slot, part]
                turned = far_ref[part, slot].T
                turned_ref[part, slot] = turned
                div_ref[:, lanes(row, TILE)] += dot(ones, turned, 1, 0)
        tile_copy(turned_ref, turned_hbm, sems, step).start()

    for step in range(far_ref.shape[0] // STEP):
        tile_copy(turned_ref, turned_hbm, sems, step).wait()


def far_body(rep_ref, rows_ref, got_ref, far_hbm, near_acc_hbm, div_hbm, *rest):
    outs = rest[:4]
    acc_ref, near_acc_ref, far_ref, div_ref, sems, acc_sem, div_sem = rest[4:]
    reps = len(outs)
    chans = acc_ref.shape[0]
    width = outs[0].shape[1]
    load_acc = pltpu.make_async_copy(near_acc_hbm, near_acc_ref, acc_sem)
    load_div = pltpu.make_async_copy(div_hbm, div_ref, div_sem)
    for step in range(far_ref.shape[0] // STEP):
        tile_copy(far_hbm, far_ref, sems, step).start()
    load_acc.start()
    load_div.start()
    acc_ref[...] = jnp.zeros_like(acc_ref)

    @pl.loop(0, far_ref.shape[0] // STEP)
    def _(step):
        tile_copy(far_hbm, far_ref, sems, step).wait()
        for item in range(STEP):
            for slot in range(2):
                part = step * STEP + item
                row = rows_ref[slot, part]
                block = got_ref[part, slot * chans : (slot + 1) * chans, :]
                acc_ref[:, lanes(row, TILE)] += dot(block, far_ref[part, slot], 1, 0)

    load_acc.wait()
    load_div.wait()
    for k in range(reps):
        where = lanes(lax.rem(rep_ref[0] + k, reps), width)
        outs[k][...] = ((near_acc_ref[:, where] + acc_ref[:, where]) / div_ref[0:1, where]).astype(BF16)


def gather_rows(ref, pieces, rep):
    reps = len(pieces)
    rows = pieces[0].shape[0]
    for k in range(reps):
        source = lax.rem(rep + reps - k, reps)
        ref[lanes(source, rows), :] = pieces[k][...]


def dense_body(rep_ref, *refs):
    agg, feats, cot, wts = refs[0:4], refs[4:8], refs[8:12], refs[12:16]
    div_ref = refs[16]
    scaled_out, out_out, grad_out = refs[17:21], refs[21:25], refs[25]
    back_ref, full_feats, full_agg, grad_ref, out_buf, out_sems = refs[26:32]
    rep = rep_ref[0]
    reps = 4
    rows, width = agg[0].shape
    gather_rows(full_feats, feats, rep)
    gather_rows(full_agg, agg, rep)
    copies = []

    def leave(source, target, sem):
        copies.append(pltpu.make_async_copy(source, target, sem))
        copies[-1].start()

    for k in range(reps):
        preact = dot(wts[k][0], full_feats[...], 1, 0) + dot(wts[k][1], full_agg[...], 1, 0)
        gate = jax.nn.sigmoid(preact)
        slope = gate * (1.0 + preact * (1.0 - gate))
        grad_ref[k * rows : (k + 1) * rows, :] = (cot[k][...].astype(F32) * slope).astype(BF16)
        out_buf[k] = (preact * gate).astype(BF16)
        leave(out_buf.at[k], out_out[k], out_sems.at[k])
    grad_out[...] = grad_ref[...]
    w_neigh = jnp.concatenate([wts[k][1] for k in range(reps)], axis=0)
    back_ref[...] = dot(w_neigh, grad_ref[...], 0, 0)
    div = div_ref[0:1, lanes(rep, width)]
    for k in range(reps):
        target = lax.rem(rep + k, reps)
        scaled_out[k][...] = (back_ref[lanes(target, rows), :] / div).astype(BF16)
    for copy in copies:
        copy.wait()


def weight_body(rep_ref, *refs):
    agg, feats, grad_ref = refs[0:4], refs[4:8], refs[8]
    grad_hbm, slices_out = refs[9], refs[10:14]
    full, prod_ref, kept_ref, grad_sem, kept_sem = refs[14:19]
    rep = rep_ref[0]
    low = lax.rem(lax.div(rep_ref[1], 2), 4)
    reps = 4
    rows = agg[0].shape[0]
    wide = prod_ref.shape[1]
    save = pltpu.make_async_copy(grad_ref, grad_hbm, grad_sem)
    save.start()
    for which, pieces in ((0, feats), (1, agg)):
        gather_rows(full, pieces, rep)
        prod_ref[...] = dot(grad_ref[...], full[...], 1, 1)
        for part in range(4):
            target = lax.rem(low + part, 4)
            slice_ref = slices_out[part] if part else kept_ref
            for k in range(reps):
                start = pl.multiple_of(k * rows + 16 * target, 16)
                slice_ref[16 * k : 16 * k + 16, which * wide : (which + 1) * wide] = prod_ref[
                    pl.ds(start, 16), :
                ].astype(BF16)
    keep = pltpu.make_async_copy(kept_ref, slices_out[0], kept_sem)
    keep.start()
    save.wait()
    keep.wait()


def back_body(rep_ref, *refs):
    wts, grad_ref, back_out, back_ref = refs[0:4], refs[4], refs[5:9], refs[9]
    rep = rep_ref[0]
    reps = 4
    rows = back_out[0].shape[0]
    w_self = jnp.concatenate([wts[k][0] for k in range(reps)], axis=0)
    back_ref[...] = dot(w_self, grad_ref[...], 0, 0)
    for k in range(reps):
        target = lax.rem(rep + k, reps)
        back_out[k][...] = back_ref[lanes(target, rows), :]


def slice_sum_body(*refs):
    pieces, outs = refs[:4], refs[4:]
    total = pieces[0][...].astype(F32)
    for piece in pieces[1:]:
        total = total + piece[...].astype(F32)
    for k in range(len(outs)):
        outs[k][...] = total[16 * k : 16 * k + 16, :]


def add_body(*refs):
    total = refs[0][...]
    for ref in refs[1:-1]:
        total = total + ref[...]
    refs[-1][...] = total.astype(refs[-1].dtype)


def stack_body(*refs):
    rows = refs[0].shape[0]
    for k, ref in enumerate(refs[:-1]):
        refs[-1][rows * k : rows * (k + 1), :] = ref[...]


def join_body(place_ref, mine_ref, own_ref, other_ref, w_self_ref, w_neigh_ref, parts_ref):
    full = w_self_ref.shape[1]
    core = lax.rem(place_ref[1], 2)
    place = lax.rem(lax.div(place_ref[1], 2), 8)
    sign = 1 - 2 * core
    parts_ref[place] = mine_ref[...].astype(F32)
    for k in range(1, 5):
        rows = slice(16 * (k - 1), 16 * k)
        parts_ref[lax.rem(place + 8 - sign * k, 8)] = own_ref[rows, :].astype(F32)
        parts_ref[lax.rem(place + 8 + sign * k, 8)] = other_ref[rows, :].astype(F32)
    for low in range(4):
        total = parts_ref[low] + parts_ref[low + 4]
        w_self_ref[16 * low : 16 * low + 16, :] = total[:, :full]
        w_neigh_ref[16 * low : 16 * low + 16, :] = total[:, full:]


def gather_lanes(ref, pieces, rep):
    reps = len(pieces)
    width = pieces[0].shape[1]
    for k in range(reps):
        source = lax.rem(rep + reps - k, reps)
        ref[:, lanes(source, width)] = pieces[k][...]


def far_back_body(rep_ref, rows_ref, s0, s1, s2, s3, far_hbm, out_ref, full_ref, buf_ref, far_ref, sems, out_sems):
    chans = full_ref.shape[0]
    parts = far_ref.shape[0]
    for step in range(parts // STEP):
        tile_copy(far_hbm, far_ref, sems, step).start()
    gather_lanes(full_ref, (s0, s1, s2, s3), rep_ref[0])

    def copy(step):
        rows = pl.ds(step * STEP, STEP)
        return pltpu.make_async_copy(
            buf_ref.at[rows], out_ref.at[rows], out_sems.at[step]
        )

    @pl.loop(0, parts // STEP)
    def _(step):
        tile_copy(far_hbm, far_ref, sems, step).wait()
        for item in range(STEP):
            for slot in range(2):
                part = step * STEP + item
                row = rows_ref[slot, part]
                term = dot(full_ref[:, lanes(row, TILE)], far_ref[part, slot], 1, 0)
                buf_ref[part, slot * chans : (slot + 1) * chans, :] = term.astype(BF16)
        copy(step).start()

    for step in range(parts // STEP):
        copy(step).wait()


def near_back_body(rep_ref, cols_ref, *refs):
    scaled, back, outs = refs[0:4], refs[4:8], refs[8:12]
    near_ref, acc_ref, output_ref, full_ref = refs[12:16]
    rep = rep_ref[0]
    reps = 4
    width = scaled[0].shape[1]
    gather_lanes(full_ref, scaled, rep)
    gather_lanes(acc_ref, back, rep)
    for k in range(reps):
        output_ref[:, lanes(lax.rem(rep + k, reps), width)] = outs[k][...]

    @pl.loop(0, near_ref.shape[0] // 4)
    def _(step):
        for item in range(4):
            row = step * 4 + item
            for link in range(2):
                term = dot(full_ref[:, lanes(row, TILE)], near_ref[row, link], 1, 0)
                acc_ref[:, lanes(cols_ref[link, row], TILE)] += term


def home_body(send_ref, got_ref, near_acc_hbm, grad_ref, acc_ref, near_acc_ref, sem):
    chans = acc_ref.shape[0]
    parts = got_ref.shape[0]
    load = pltpu.make_async_copy(near_acc_hbm, near_acc_ref, sem)
    load.start()
    acc_ref[...] = jnp.zeros_like(acc_ref)
    for item in range(parts):
        for slot in range(2):
            block = send_ref[slot, item]
            acc_ref[:, lanes(block, TILE)] += got_ref[item, slot * chans : (slot + 1) * chans, :].astype(F32)
    load.wait()
    grad_ref[...] = (near_acc_ref[...] + acc_ref[...]).astype(BF16)


def local(feats, w_self, w_neigh, local_cols, local_tiles, send_list, remote_rows, remote_tiles, cotangent):
    chans, nodes = feats.shape
    full = w_self.shape[0]
    reps = full // chans
    width = nodes // reps
    parts = remote_tiles.shape[1]
    far_tiles = remote_tiles[0]
    rows = remote_rows[0].T
    sends = pinned(send_list[0].T)
    cols = local_cols.T
    rep = jnp.stack([lax.axis_index("rep"), lax.axis_index("dom")]).astype(jnp.int32)
    piece = shape((chans, width), BF16)
    piece32 = shape((chans, width), F32)
    sems = pltpu.SemaphoreType.DMA((parts // STEP,))
    sem = pltpu.SemaphoreType.DMA(())
    tile_buf = pltpu.VMEM(far_tiles.shape, BF16)
    wide32 = pltpu.VMEM((chans, nodes), F32)

    def shift(value, by):
        return lax.ppermute(value, "rep", [(i, (i + by) % reps) for i in range(reps)])

    def move(value, dy, dz, dc, turn=False):
        pairs = [
            ((y * 8 + z) * 2 + c, ((y + dy) % 4 * 8 + (z + (-dz if turn and c else dz)) % 8) * 2 + (c + dc) % 2)
            for y in range(4)
            for z in range(8)
            for c in range(2)
        ]
        return lax.ppermute(value, "dom", pairs)

    def move_low(value, k):
        pairs = [
            ((y * 8 + z) * 2 + c, (y * 8 + z // 4 * 4 + (z + k) % 4) * 2 + c)
            for y in range(4)
            for z in range(8)
            for c in range(2)
        ]
        return lax.ppermute(value, "dom", pairs)

    def exchange(pieces, sign=1):
        return [pieces[0]] + [shift(pieces[k], (sign * k) % reps) for k in range(1, reps)]

    with jax.named_scope("pick"):
        outgoing = call(
            pick_body, (sends,), (feats,), in_hbm((parts, 2 * chans, TILE), BF16),
            [pltpu.VMEM((chans, nodes), BF16), pltpu.VMEM((parts, 2 * chans, TILE), BF16), sems, sem], 2.0, (0,), (0,),
        )
    incoming = lax.all_to_all(outgoing, "dom", split_axis=0, concat_axis=0, tiled=True)

    with jax.named_scope("chunks"):
        pieces = call(chunk_body, (rep,), (feats, cotangent), [piece] * (2 * reps))
    feats_in = exchange(pieces[:reps])
    cot_in = exchange(pieces[reps:])
    weights_in = exchange([jnp.stack([w_self.T, w_neigh.T])] * reps)
    with jax.named_scope("near"):
        near_acc, div, turned = call(
            near_body, (cols, rows), (feats, local_tiles, far_tiles),
            [shape((chans, nodes), F32), shape((8, nodes), F32), in_hbm(far_tiles.shape, BF16)],
            [tile_buf, sems], 8.0, (), (2,),
        )
    incoming, feats_in, cot_in, weights_in, near_acc, div, turned = lax.optimization_barrier(
        (incoming, feats_in, cot_in, weights_in, near_acc, div, turned)
    )
    with jax.named_scope("far"):
        agg = call(
            far_body, (rep, rows), (incoming, turned, near_acc, div), [piece] * reps,
            [wide32, wide32, tile_buf, pltpu.VMEM((8, nodes), F32), sems, sem, sem], 6.0, (1, 2, 3),
        )
    agg_in = exchange(agg)

    with jax.named_scope("dense"):
        dense = call(
            dense_body, (rep,), (*agg_in, *feats_in, *cot_in, *weights_in, div),
            [piece] * reps
            + [in_hbm((chans, width), BF16)] * reps
            + [shape((full, width), BF16)],
            [
                pltpu.VMEM((full, width), F32), pltpu.VMEM((full, width), BF16), pltpu.VMEM((full, width), BF16),
                pltpu.VMEM((full, width), BF16), pltpu.VMEM((reps, chans, width), BF16), pltpu.SemaphoreType.DMA((reps,)),
            ],
            2.0, (), range(reps, 2 * reps),
        )
    scaled, out_pieces, grad = dense[:reps], dense[reps : 2 * reps], dense[2 * reps]
    scaled_in = exchange(scaled)
    with jax.named_scope("weights"):
        grad_pre, *slices = call(
            weight_body, (rep,), (*agg_in, *feats_in, grad),
            [in_hbm((full, width), BF16), in_hbm((16 * reps, 2 * full), BF16)]
            + [shape((16 * reps, 2 * full), BF16)] * 3,
            [
                pltpu.VMEM((full, width), BF16), pltpu.VMEM((full, full), F32), pltpu.VMEM((16 * reps, 2 * full), BF16),
                sem, sem,
            ],
            2.0, (), (0, 1),
        )
    slices_in = [slices[0]] + [move_low(slices[k], k) for k in range(1, 4)]
    with jax.named_scope("far_back"):
        far_back = call(
            far_back_body, (rep, rows), (*scaled_in, far_tiles), in_hbm((parts, 2 * chans, TILE), BF16),
            [
                pltpu.VMEM((chans, nodes), BF16), pltpu.VMEM((parts, 2 * chans, TILE), BF16), tile_buf, sems, sems,
            ],
            5.0, (reps,), (0,),
        )
    slices_in, far_back = lax.optimization_barrier((slices_in, far_back))
    returned = lax.all_to_all(far_back, "dom", split_axis=0, concat_axis=0, tiled=True)

    with jax.named_scope("slice_sums"):
        slice_shape = shape((16, 2 * full), F32)
        sums = call(slice_sum_body, (), slices_in, [slice_shape] * reps)
        total = call(add_body, (), exchange(sums, -1), slice_shape)
        total = call(add_body, (), (total, move(total, 0, 0, 1)), slice_shape)
        others = [move(total, dy, 0, 0) for dy in range(1, 4)]
        total = call(add_body, (), (total, *others), shape((16, 2 * full), BF16))
    with jax.named_scope("back"):
        back_self = call(
            back_body, (rep,), (*weights_in, grad_pre), [piece32] * reps, [pltpu.VMEM((full, width), F32)], 1.0
        )
    back_in = exchange(back_self)
    out_in = exchange(out_pieces, -1)
    with jax.named_scope("near_back"):
        near_back, output = call(
            near_back_body, (rep, cols), (*scaled_in, *back_in, *out_in, local_tiles),
            [shape((chans, nodes), F32), shape((chans, nodes), BF16)], [pltpu.VMEM((chans, nodes), BF16)], 2.0,
        )
    total, near_back, output = lax.optimization_barrier((total, near_back, output))
    with jax.named_scope("spread"):
        own = call(
            stack_body, (), [move(total, 0, dz, 0, True) for dz in range(1, 5)], shape((64, 2 * full), BF16), (), 0.5
        )
        other = move(own, 0, 0, 1)
    with jax.named_scope("home"):
        grad_feats = call(
            home_body, (sends,), (returned, near_back), shape((chans, nodes), BF16), [wide32, wide32, sem], 3.0, (1,)
        )
    with jax.named_scope("join"):
        other, grad_feats = lax.optimization_barrier((other, grad_feats))
        wg_self, wg_neigh = call(
            join_body, (rep,), (total, own, other), [shape((chans, full), F32)] * 2, [pltpu.VMEM((8, 16, 2 * full), F32)]
        )
    return output, grad_feats, wg_self.T, wg_neigh.T


def solution(mesh):
    placed = (
        P("rep", "dom"),
        P(None, "rep"),
        P(None, "rep"),
        P("dom", None),
        P("dom", None, None, None),
        P("dom", None, None),
        P("dom", None, None),
        P("dom", None, None, None, None),
        P("rep", "dom"),
    )
    return jax.shard_map(
        local,
        mesh=mesh,
        in_specs=placed,
        out_specs=(P("rep", "dom"), P("rep", "dom"), P(None, "rep"), P(None, "rep")),
        check_vma=False,
    )
```

```python
import jax
import jax.numpy as jnp
from jax import lax
from jax.experimental import pallas as pl
from jax.experimental.pallas import tpu as pltpu
from jax.sharding import PartitionSpec as P

TILE = 128
STEP = 4
VMEM_BYTES = 12 * 1024 * 1024
F32 = jnp.float32
BF16 = jnp.bfloat16
IN_VMEM = pl.BlockSpec(memory_space=pltpu.VMEM)
IN_SMEM = pl.BlockSpec(memory_space=pltpu.SMEM)
IN_HBM = pl.BlockSpec(memory_space=pltpu.HBM)


def lanes(index, width):
    return pl.ds(pl.multiple_of(index * width, width), width)


def call(body, scalars, args, out_shape, scratch=(), micros=1.0, hbm=(), hbm_out=()):
    many = isinstance(out_shape, list)
    out_specs = [IN_HBM if i in hbm_out else IN_VMEM for i in range(len(out_shape) if many else 1)]
    out_specs = out_specs if many else out_specs[0]
    args = [pinned(arg) if i in hbm else arg for i, arg in enumerate(args)]
    return pl.pallas_call(
        body,
        in_specs=[IN_SMEM] * len(scalars) + [IN_HBM if i in hbm else IN_VMEM for i in range(len(args))],
        out_shape=out_shape,
        out_specs=out_specs,
        scratch_shapes=scratch,
        compiler_params=pltpu.CompilerParams(vmem_limit_bytes=VMEM_BYTES),
        cost_estimate=pl.CostEstimate(flops=int(micros * 1.1e9), bytes_accessed=1 << 16, transcendentals=0),
    )(*scalars, *args)


def shape(dims, kind):
    return jax.ShapeDtypeStruct(dims, kind)


def in_hbm(dims, kind):
    return pltpu.HBM(dims, kind)


def pinned(value):
    return pltpu.with_memory_space_constraint(value, pltpu.HBM)


def dot(left, right, left_dim, right_dim):
    return lax.dot_general(left, right, (((left_dim,), (right_dim,)), ((), ())), preferred_element_type=F32)


def pick_body(send_ref, feats_hbm, out_ref, feats_ref, buf_ref, sems, feats_sem):
    chans = feats_ref.shape[0]
    load = pltpu.make_async_copy(feats_hbm, feats_ref, feats_sem)
    load.start()
    load.wait()
    parts = buf_ref.shape[0]
    for step in range(parts // STEP):
        for item in range(step * STEP, (step + 1) * STEP):
            for slot in range(2):
                block = send_ref[slot, item]
                buf_ref[item, slot * chans : (slot + 1) * chans, :] = feats_ref[:, lanes(block, TILE)]
        rows = pl.ds(step * STEP, STEP)
        pltpu.make_async_copy(buf_ref.at[rows], out_ref.at[rows], sems.at[step]).start()
    for step in range(parts // STEP):
        rows = pl.ds(step * STEP, STEP)
        pltpu.make_async_copy(buf_ref.at[rows], out_ref.at[rows], sems.at[step]).wait()


def tile_copy(far_hbm, far_ref, sems, step):
    rows = pl.ds(step * STEP, STEP)
    return pltpu.make_async_copy(far_hbm.at[rows], far_ref.at[rows], sems.at[step])


def chunk_body(rep_ref, feats_ref, cot_ref, *outs):
    reps = len(outs) // 2
    width = outs[0].shape[1]
    for k in range(reps):
        chunk = lax.rem(rep_ref[0] + k, reps)
        outs[k][...] = feats_ref[:, lanes(chunk, width)]
        outs[reps + k][...] = cot_ref[:, lanes(chunk, width)]


def near_body(cols_ref, rows_ref, feats_ref, near_ref, far_ref, acc_ref, div_ref, turned_hbm, turned_ref, sems):
    ones = jnp.ones((8, TILE), BF16)
    div_ref[...] = jnp.ones_like(div_ref)

    @pl.loop(0, near_ref.shape[0] // 4)
    def _(step):
        for item in range(4):
            row = step * 4 + item
            total = None
            sums = None
            for link in range(2):
                tile = near_ref[row, link]
                term = dot(feats_ref[:, lanes(cols_ref[link, row], TILE)], tile, 1, 1)
                part = dot(ones, tile, 1, 1)
                total = term if total is None else total + term
                sums = part if sums is None else sums + part
            acc_ref[:, lanes(row, TILE)] = total
            div_ref[:, lanes(row, TILE)] += sums

    @pl.loop(0, far_ref.shape[0] // STEP)
    def _(step):
        for item in range(STEP):
            for slot in range(2):
                part = step * STEP + item
                row = rows_ref[slot, part]
                turned = far_ref[part, slot].T
                turned_ref[part, slot] = turned
                div_ref[:, lanes(row, TILE)] += dot(ones, turned, 1, 0)
        tile_copy(turned_ref, turned_hbm, sems, step).start()

    for step in range(far_ref.shape[0] // STEP):
        tile_copy(turned_ref, turned_hbm, sems, step).wait()


def far_body(rep_ref, rows_ref, got_ref, far_hbm, near_acc_hbm, div_hbm, *rest):
    outs = rest[:4]
    acc_ref, near_acc_ref, far_ref, div_ref, sems, acc_sem, div_sem = rest[4:]
    reps = len(outs)
    chans = acc_ref.shape[0]
    width = outs[0].shape[1]
    load_acc = pltpu.make_async_copy(near_acc_hbm, near_acc_ref, acc_sem)
    load_div = pltpu.make_async_copy(div_hbm, div_ref, div_sem)
    for step in range(far_ref.shape[0] // STEP):
        tile_copy(far_hbm, far_ref, sems, step).start()
    load_acc.start()
    load_div.start()
    acc_ref[...] = jnp.zeros_like(acc_ref)

    @pl.loop(0, far_ref.shape[0] // STEP)
    def _(step):
        tile_copy(far_hbm, far_ref, sems, step).wait()
        for item in range(STEP):
            for slot in range(2):
                part = step * STEP + item
                row = rows_ref[slot, part]
                block = got_ref[part, slot * chans : (slot + 1) * chans, :]
                acc_ref[:, lanes(row, TILE)] += dot(block, far_ref[part, slot], 1, 0)

    load_acc.wait()
    load_div.wait()
    for k in range(reps):
        where = lanes(lax.rem(rep_ref[0] + k, reps), width)
        outs[k][...] = ((near_acc_ref[:, where] + acc_ref[:, where]) / div_ref[0:1, where]).astype(BF16)


def gather_rows(ref, pieces, rep):
    reps = len(pieces)
    rows = pieces[0].shape[0]
    for k in range(reps):
        source = lax.rem(rep + reps - k, reps)
        ref[lanes(source, rows), :] = pieces[k][...]


def dense_body(rep_ref, *refs):
    agg, feats, cot, wts = refs[0:4], refs[4:8], refs[8:12], refs[12:16]
    div_ref = refs[16]
    scaled_out, out_out, grad_hbm, slices_out = refs[17:21], refs[21:25], refs[25], refs[26:30]
    back_ref, full_feats, full_agg, grad_ref, out_buf, prod_ref, kept_ref = refs[30:37]
    out_sems, grad_sem, kept_sem = refs[37:40]
    low = lax.rem(lax.div(rep_ref[1], 2), 4)
    rep = rep_ref[0]
    reps = 4
    rows, width = agg[0].shape
    gather_rows(full_feats, feats, rep)
    gather_rows(full_agg, agg, rep)
    copies = []

    def leave(source, target, sem):
        copies.append(pltpu.make_async_copy(source, target, sem))
        copies[-1].start()

    for k in range(reps):
        preact = dot(wts[k][0], full_feats[...], 1, 0) + dot(wts[k][1], full_agg[...], 1, 0)
        gate = jax.nn.sigmoid(preact)
        slope = gate * (1.0 + preact * (1.0 - gate))
        grad_ref[k * rows : (k + 1) * rows, :] = (cot[k][...].astype(F32) * slope).astype(BF16)
        out_buf[k] = (preact * gate).astype(BF16)
        leave(out_buf.at[k], out_out[k], out_sems.at[k])
    leave(grad_ref, grad_hbm, grad_sem)
    for which, full in ((0, full_feats), (1, full_agg)):
        prod_ref[...] = dot(grad_ref[...], full[...], 1, 1)
        wide = prod_ref.shape[1]
        for part in range(4):
            target = lax.rem(low + part, 4)
            slice_ref = slices_out[part] if part else kept_ref
            for k in range(reps):
                start = pl.multiple_of(k * rows + 16 * target, 16)
                slice_ref[16 * k : 16 * k + 16, which * wide : (which + 1) * wide] = prod_ref[
                    pl.ds(start, 16), :
                ].astype(BF16)
    leave(kept_ref, slices_out[0], kept_sem)
    w_neigh = jnp.concatenate([wts[k][1] for k in range(reps)], axis=0)
    back_ref[...] = dot(w_neigh, grad_ref[...], 0, 0)
    div = div_ref[0:1, lanes(rep, width)]
    for k in range(reps):
        target = lax.rem(rep + k, reps)
        scaled_out[k][...] = (back_ref[lanes(target, rows), :] / div).astype(BF16)
    for copy in copies:
        copy.wait()


def back_body(rep_ref, *refs):
    wts, grad_ref, back_out, back_ref = refs[0:4], refs[4], refs[5:9], refs[9]
    rep = rep_ref[0]
    reps = 4
    rows = back_out[0].shape[0]
    w_self = jnp.concatenate([wts[k][0] for k in range(reps)], axis=0)
    back_ref[...] = dot(w_self, grad_ref[...], 0, 0)
    for k in range(reps):
        target = lax.rem(rep + k, reps)
        back_out[k][...] = back_ref[lanes(target, rows), :]


def slice_sum_body(*refs):
    pieces, outs = refs[:4], refs[4:]
    total = pieces[0][...].astype(F32)
    for piece in pieces[1:]:
        total = total + piece[...].astype(F32)
    for k in range(len(outs)):
        outs[k][...] = total[16 * k : 16 * k + 16, :]


def add_body(*refs):
    total = refs[0][...]
    for ref in refs[1:-1]:
        total = total + ref[...]
    refs[-1][...] = total.astype(refs[-1].dtype)


def stack_body(*refs):
    rows = refs[0].shape[0]
    for k, ref in enumerate(refs[:-1]):
        refs[-1][rows * k : rows * (k + 1), :] = ref[...]


def join_body(place_ref, mine_ref, own_ref, other_ref, w_self_ref, w_neigh_ref, parts_ref):
    full = w_self_ref.shape[1]
    core = lax.rem(place_ref[1], 2)
    place = lax.rem(lax.div(place_ref[1], 2), 8)
    sign = 1 - 2 * core
    parts_ref[place] = mine_ref[...].astype(F32)
    for k in range(1, 5):
        rows = slice(16 * (k - 1), 16 * k)
        parts_ref[lax.rem(place + 8 - sign * k, 8)] = own_ref[rows, :].astype(F32)
        parts_ref[lax.rem(place + 8 + sign * k, 8)] = other_ref[rows, :].astype(F32)
    for low in range(4):
        total = parts_ref[low] + parts_ref[low + 4]
        w_self_ref[16 * low : 16 * low + 16, :] = total[:, :full]
        w_neigh_ref[16 * low : 16 * low + 16, :] = total[:, full:]


def gather_lanes(ref, pieces, rep):
    reps = len(pieces)
    width = pieces[0].shape[1]
    for k in range(reps):
        source = lax.rem(rep + reps - k, reps)
        ref[:, lanes(source, width)] = pieces[k][...]


def far_back_body(rep_ref, rows_ref, s0, s1, s2, s3, far_hbm, out_ref, full_ref, buf_ref, far_ref, sems, out_sems):
    chans = full_ref.shape[0]
    parts = far_ref.shape[0]
    for step in range(parts // STEP):
        tile_copy(far_hbm, far_ref, sems, step).start()
    gather_lanes(full_ref, (s0, s1, s2, s3), rep_ref[0])

    def copy(step):
        rows = pl.ds(step * STEP, STEP)
        return pltpu.make_async_copy(
            buf_ref.at[rows], out_ref.at[rows], out_sems.at[step]
        )

    @pl.loop(0, parts // STEP)
    def _(step):
        tile_copy(far_hbm, far_ref, sems, step).wait()
        for item in range(STEP):
            for slot in range(2):
                part = step * STEP + item
                row = rows_ref[slot, part]
                term = dot(full_ref[:, lanes(row, TILE)], far_ref[part, slot], 1, 0)
                buf_ref[part, slot * chans : (slot + 1) * chans, :] = term.astype(BF16)
        copy(step).start()

    for step in range(parts // STEP):
        copy(step).wait()


def near_back_body(rep_ref, cols_ref, *refs):
    scaled, back, outs = refs[0:4], refs[4:8], refs[8:12]
    near_ref, acc_ref, output_ref, full_ref = refs[12:16]
    rep = rep_ref[0]
    reps = 4
    width = scaled[0].shape[1]
    gather_lanes(full_ref, scaled, rep)
    gather_lanes(acc_ref, back, rep)
    for k in range(reps):
        output_ref[:, lanes(lax.rem(rep + k, reps), width)] = outs[k][...]

    @pl.loop(0, near_ref.shape[0] // 4)
    def _(step):
        for item in range(4):
            row = step * 4 + item
            for link in range(2):
                term = dot(full_ref[:, lanes(row, TILE)], near_ref[row, link], 1, 0)
                acc_ref[:, lanes(cols_ref[link, row], TILE)] += term


def home_body(send_ref, got_ref, near_acc_hbm, grad_hbm, acc_ref, near_acc_ref, grad_ref, sem, sems):
    chans = acc_ref.shape[0]
    parts = got_ref.shape[0]
    load = pltpu.make_async_copy(near_acc_hbm, near_acc_ref, sem)
    load.start()
    acc_ref[...] = jnp.zeros_like(acc_ref)
    for item in range(parts):
        for slot in range(2):
            block = send_ref[slot, item]
            acc_ref[:, lanes(block, TILE)] += got_ref[item, slot * chans : (slot + 1) * chans, :].astype(F32)
    load.wait()
    rows = chans // 4
    copies = []
    for piece in range(4):
        where = slice(piece * rows, (piece + 1) * rows)
        grad_ref[where, :] = (near_acc_ref[where, :] + acc_ref[where, :]).astype(BF16)
        copies.append(pltpu.make_async_copy(grad_ref.at[where], grad_hbm.at[where], sems.at[piece]))
        copies[-1].start()
    for copy in copies:
        copy.wait()


def local(feats, w_self, w_neigh, local_cols, local_tiles, send_list, remote_rows, remote_tiles, cotangent):
    chans, nodes = feats.shape
    full = w_self.shape[0]
    reps = full // chans
    width = nodes // reps
    parts = remote_tiles.shape[1]
    far_tiles = remote_tiles[0]
    rows = remote_rows[0].T
    sends = pinned(send_list[0].T)
    cols = local_cols.T
    rep = jnp.stack([lax.axis_index("rep"), lax.axis_index("dom")]).astype(jnp.int32)
    piece = shape((chans, width), BF16)
    piece32 = shape((chans, width), F32)
    sems = pltpu.SemaphoreType.DMA((parts // STEP,))
    sem = pltpu.SemaphoreType.DMA(())
    tile_buf = pltpu.VMEM(far_tiles.shape, BF16)
    wide32 = pltpu.VMEM((chans, nodes), F32)

    def shift(value, by):
        return lax.ppermute(value, "rep", [(i, (i + by) % reps) for i in range(reps)])

    def move(value, dy, dz, dc, turn=False):
        pairs = [
            ((y * 8 + z) * 2 + c, ((y + dy) % 4 * 8 + (z + (-dz if turn and c else dz)) % 8) * 2 + (c + dc) % 2)
            for y in range(4)
            for z in range(8)
            for c in range(2)
        ]
        return lax.ppermute(value, "dom", pairs)

    def move_low(value, k):
        pairs = [
            ((y * 8 + z) * 2 + c, (y * 8 + z // 4 * 4 + (z + k) % 4) * 2 + c)
            for y in range(4)
            for z in range(8)
            for c in range(2)
        ]
        return lax.ppermute(value, "dom", pairs)

    def exchange(pieces, sign=1):
        return [pieces[0]] + [shift(pieces[k], (sign * k) % reps) for k in range(1, reps)]

    with jax.named_scope("pick"):
        outgoing = call(
            pick_body, (sends,), (feats,), in_hbm((parts, 2 * chans, TILE), BF16),
            [pltpu.VMEM((chans, nodes), BF16), pltpu.VMEM((parts, 2 * chans, TILE), BF16), sems, sem], 2.0, (0,), (0,),
        )
    incoming = lax.all_to_all(outgoing, "dom", split_axis=0, concat_axis=0, tiled=True)

    with jax.named_scope("chunks"):
        pieces = call(chunk_body, (rep,), (feats, cotangent), [piece] * (2 * reps))
    feats_in = exchange(pieces[:reps])
    cot_in = exchange(pieces[reps:])
    weights_in = exchange([jnp.stack([w_self.T, w_neigh.T])] * reps)
    with jax.named_scope("near"):
        near_acc, div, turned = call(
            near_body, (cols, rows), (feats, local_tiles, far_tiles),
            [shape((chans, nodes), F32), shape((8, nodes), F32), in_hbm(far_tiles.shape, BF16)],
            [tile_buf, sems], 8.0, (), (2,),
        )
    incoming, feats_in, cot_in, weights_in, near_acc, div, turned = lax.optimization_barrier(
        (incoming, feats_in, cot_in, weights_in, near_acc, div, turned)
    )
    with jax.named_scope("far"):
        agg = call(
            far_body, (rep, rows), (incoming, turned, near_acc, div), [piece] * reps,
            [wide32, wide32, tile_buf, pltpu.VMEM((8, nodes), F32), sems, sem, sem], 6.0, (1, 2, 3),
        )
    agg_in = exchange(agg)

    with jax.named_scope("dense"):
        dense = call(
            dense_body, (rep,), (*agg_in, *feats_in, *cot_in, *weights_in, div),
            [piece] * reps
            + [in_hbm((chans, width), BF16)] * reps
            + [in_hbm((full, width), BF16), in_hbm((16 * reps, 2 * full), BF16)]
            + [shape((16 * reps, 2 * full), BF16)] * 3,
            [
                pltpu.VMEM((full, width), F32), pltpu.VMEM((full, width), BF16), pltpu.VMEM((full, width), BF16),
                pltpu.VMEM((full, width), BF16), pltpu.VMEM((reps, chans, width), BF16), pltpu.VMEM((full, full), F32),
                pltpu.VMEM((16 * reps, 2 * full), BF16), pltpu.SemaphoreType.DMA((reps,)), sem, sem,
            ],
            3.0, (), range(reps, 2 * reps + 2),
        )
    scaled, out_pieces, grad_pre, slices = dense[:reps], dense[reps : 2 * reps], dense[2 * reps], dense[2 * reps + 1 :]
    scaled_in = exchange(scaled)
    slices_in = [slices[0]] + [move_low(slices[k], k) for k in range(1, 4)]
    with jax.named_scope("far_back"):
        far_back = call(
            far_back_body, (rep, rows), (*scaled_in, far_tiles), in_hbm((parts, 2 * chans, TILE), BF16),
            [
                pltpu.VMEM((chans, nodes), BF16), pltpu.VMEM((parts, 2 * chans, TILE), BF16), tile_buf, sems, sems,
            ],
            5.0, (reps,), (0,),
        )
    slices_in, far_back = lax.optimization_barrier((slices_in, far_back))
    returned = lax.all_to_all(far_back, "dom", split_axis=0, concat_axis=0, tiled=True)

    with jax.named_scope("slice_sums"):
        slice_shape = shape((16, 2 * full), F32)
        sums = call(slice_sum_body, (), slices_in, [slice_shape] * reps)
        total = call(add_body, (), exchange(sums, -1), slice_shape)
        total = call(add_body, (), (total, move(total, 0, 0, 1)), slice_shape)
        others = [move(total, dy, 0, 0) for dy in range(1, 4)]
        total = call(add_body, (), (total, *others), shape((16, 2 * full), BF16))
    with jax.named_scope("back"):
        back_self = call(
            back_body, (rep,), (*weights_in, grad_pre), [piece32] * reps, [pltpu.VMEM((full, width), F32)], 1.0
        )
    back_in = exchange(back_self)
    out_in = exchange(out_pieces, -1)
    with jax.named_scope("near_back"):
        near_back, output = call(
            near_back_body, (rep, cols), (*scaled_in, *back_in, *out_in, local_tiles),
            [shape((chans, nodes), F32), shape((chans, nodes), BF16)], [pltpu.VMEM((chans, nodes), BF16)], 2.0,
        )
    total, near_back, output = lax.optimization_barrier((total, near_back, output))
    with jax.named_scope("spread"):
        own = call(
            stack_body, (), [move(total, 0, dz, 0, True) for dz in range(1, 5)], shape((64, 2 * full), BF16), (), 0.5
        )
        other = move(own, 0, 0, 1)
    with jax.named_scope("home"):
        grad_feats = call(
            home_body, (sends,), (returned, near_back), in_hbm((chans, nodes), BF16),
            [wide32, wide32, pltpu.VMEM((chans, nodes), BF16), sem, pltpu.SemaphoreType.DMA((4,))], 3.0, (1,), (0,),
        )
    with jax.named_scope("join"):
        other, grad_feats = lax.optimization_barrier((other, grad_feats))
        wg_self, wg_neigh = call(
            join_body, (rep,), (total, own, other), [shape((chans, full), F32)] * 2, [pltpu.VMEM((8, 16, 2 * full), F32)]
        )
    return output, grad_feats, wg_self.T, wg_neigh.T


def solution(mesh):
    placed = (
        P("rep", "dom"),
        P(None, "rep"),
        P(None, "rep"),
        P("dom", None),
        P("dom", None, None, None),
        P("dom", None, None),
        P("dom", None, None),
        P("dom", None, None, None, None),
        P("rep", "dom"),
    )
    return jax.shard_map(
        local,
        mesh=mesh,
        in_specs=placed,
        out_specs=(P("rep", "dom"), P("rep", "dom"), P(None, "rep"), P(None, "rep")),
        check_vma=False,
    )
```

```python
import jax
import jax.numpy as jnp
from jax import lax
from jax.experimental import pallas as pl
from jax.experimental.pallas import tpu as pltpu
from jax.sharding import PartitionSpec as P

TILE = 128
STEP = 8
VMEM_BYTES = 12 * 1024 * 1024
F32 = jnp.float32
BF16 = jnp.bfloat16
IN_VMEM = pl.BlockSpec(memory_space=pltpu.VMEM)
IN_SMEM = pl.BlockSpec(memory_space=pltpu.SMEM)
IN_HBM = pl.BlockSpec(memory_space=pltpu.HBM)


def lanes(index, width):
    return pl.ds(pl.multiple_of(index * width, width), width)


def call(body, scalars, args, out_shape, scratch=(), micros=1.0, hbm=(), hbm_out=()):
    many = isinstance(out_shape, list)
    out_specs = [IN_HBM if i in hbm_out else IN_VMEM for i in range(len(out_shape) if many else 1)]
    out_specs = out_specs if many else out_specs[0]
    args = [pinned(arg) if i in hbm else arg for i, arg in enumerate(args)]
    return pl.pallas_call(
        body,
        in_specs=[IN_SMEM] * len(scalars) + [IN_HBM if i in hbm else IN_VMEM for i in range(len(args))],
        out_shape=out_shape,
        out_specs=out_specs,
        scratch_shapes=scratch,
        compiler_params=pltpu.CompilerParams(vmem_limit_bytes=VMEM_BYTES),
        cost_estimate=pl.CostEstimate(flops=int(micros * 1.1e9), bytes_accessed=1 << 16, transcendentals=0),
    )(*scalars, *args)


def shape(dims, kind):
    return jax.ShapeDtypeStruct(dims, kind)


def in_hbm(dims, kind):
    return pltpu.HBM(dims, kind)


def pinned(value):
    return pltpu.with_memory_space_constraint(value, pltpu.HBM)


def dot(left, right, left_dim, right_dim):
    return lax.dot_general(left, right, (((left_dim,), (right_dim,)), ((), ())), preferred_element_type=F32)


def pick_body(send_ref, feats_hbm, out_ref, feats_ref, buf_ref, sems, feats_sem):
    chans = feats_ref.shape[0]
    load = pltpu.make_async_copy(feats_hbm, feats_ref, feats_sem)
    load.start()
    load.wait()
    parts = buf_ref.shape[0]
    for step in range(parts // STEP):
        for item in range(step * STEP, (step + 1) * STEP):
            for slot in range(2):
                block = send_ref[slot, item]
                buf_ref[item, slot * chans : (slot + 1) * chans, :] = feats_ref[:, lanes(block, TILE)]
        rows = pl.ds(step * STEP, STEP)
        pltpu.make_async_copy(buf_ref.at[rows], out_ref.at[rows], sems.at[step]).start()
    for step in range(parts // STEP):
        rows = pl.ds(step * STEP, STEP)
        pltpu.make_async_copy(buf_ref.at[rows], out_ref.at[rows], sems.at[step]).wait()


def tile_copy(far_hbm, far_ref, sems, step):
    rows = pl.ds(step * STEP, STEP)
    return pltpu.make_async_copy(far_hbm.at[rows], far_ref.at[rows], sems.at[step])


def runs(parts):
    return [(0, parts // 8), (parts // 8, parts // 8), (parts // 4, parts // 4), (parts // 2, parts // 2)]


def run_copy(far_hbm, far_ref, sems, index):
    rows = pl.ds(*runs(far_ref.shape[0])[index])
    return pltpu.make_async_copy(far_hbm.at[rows], far_ref.at[rows], sems.at[index])


def chunk_body(rep_ref, feats_ref, cot_ref, *outs):
    reps = len(outs) // 2
    width = outs[0].shape[1]
    for k in range(reps):
        chunk = lax.rem(rep_ref[0] + k, reps)
        outs[k][...] = feats_ref[:, lanes(chunk, width)]
        outs[reps + k][...] = cot_ref[:, lanes(chunk, width)]


def near_body(cols_ref, rows_ref, feats_ref, near_ref, far_ref, acc_ref, div_ref, turned_hbm, turned_ref, sems):
    ones = jnp.ones((8, TILE), BF16)
    div_ref[...] = jnp.ones_like(div_ref)

    @pl.loop(0, near_ref.shape[0] // 4)
    def _(step):
        for item in range(4):
            row = step * 4 + item
            total = None
            sums = None
            for link in range(2):
                tile = near_ref[row, link]
                term = dot(feats_ref[:, lanes(cols_ref[link, row], TILE)], tile, 1, 1)
                part = dot(ones, tile, 1, 1)
                total = term if total is None else total + term
                sums = part if sums is None else sums + part
            acc_ref[:, lanes(row, TILE)] = total
            div_ref[:, lanes(row, TILE)] += sums

    @pl.loop(0, far_ref.shape[0] // STEP)
    def _(step):
        for item in range(STEP):
            for slot in range(2):
                part = step * STEP + item
                row = rows_ref[slot, part]
                turned = far_ref[part, slot].T
                turned_ref[part, slot] = turned
                div_ref[:, lanes(row, TILE)] += dot(ones, turned, 1, 0)
        tile_copy(turned_ref, turned_hbm, sems, step).start()

    for step in range(far_ref.shape[0] // STEP):
        tile_copy(turned_ref, turned_hbm, sems, step).wait()


def far_body(rep_ref, rows_ref, got_ref, far_hbm, near_acc_hbm, div_hbm, *rest):
    outs = rest[:4]
    acc_ref, near_acc_ref, far_ref, div_ref, sems, acc_sem, div_sem = rest[4:]
    reps = len(outs)
    chans = acc_ref.shape[0]
    width = outs[0].shape[1]
    load_acc = pltpu.make_async_copy(near_acc_hbm, near_acc_ref, acc_sem)
    load_div = pltpu.make_async_copy(div_hbm, div_ref, div_sem)
    for index in range(4):
        run_copy(far_hbm, far_ref, sems, index).start()
    load_acc.start()
    load_div.start()
    acc_ref[...] = jnp.zeros_like(acc_ref)

    for index, (first, count) in enumerate(runs(far_ref.shape[0])):
        run_copy(far_hbm, far_ref, sems, index).wait()
        for part in range(first, first + count):
            for slot in range(2):
                row = rows_ref[slot, part]
                block = got_ref[part, slot * chans : (slot + 1) * chans, :]
                acc_ref[:, lanes(row, TILE)] += dot(block, far_ref[part, slot], 1, 0)

    load_acc.wait()
    load_div.wait()
    for k in range(reps):
        where = lanes(lax.rem(rep_ref[0] + k, reps), width)
        outs[k][...] = ((near_acc_ref[:, where] + acc_ref[:, where]) / div_ref[0:1, where]).astype(BF16)


def gather_rows(ref, pieces, rep):
    reps = len(pieces)
    rows = pieces[0].shape[0]
    for k in range(reps):
        source = lax.rem(rep + reps - k, reps)
        ref[lanes(source, rows), :] = pieces[k][...]


def dense_body(rep_ref, *refs):
    agg, feats, cot, wts = refs[0:4], refs[4:8], refs[8:12], refs[12:16]
    div_ref = refs[16]
    scaled_out, out_out, grad_hbm, slices_out = refs[17:21], refs[21:25], refs[25], refs[26:30]
    back_ref, full_feats, full_agg, grad_ref, out_buf, prod_ref, kept_ref = refs[30:37]
    out_sems, grad_sem, kept_sem = refs[37:40]
    low = lax.rem(lax.div(rep_ref[1], 2), 4)
    rep = rep_ref[0]
    reps = 4
    rows, width = agg[0].shape
    gather_rows(full_feats, feats, rep)
    gather_rows(full_agg, agg, rep)
    copies = []

    def leave(source, target, sem):
        copies.append(pltpu.make_async_copy(source, target, sem))
        copies[-1].start()

    for k in range(reps):
        preact = dot(wts[k][0], full_feats[...], 1, 0) + dot(wts[k][1], full_agg[...], 1, 0)
        gate = jax.nn.sigmoid(preact)
        slope = gate * (1.0 + preact * (1.0 - gate))
        grad_ref[k * rows : (k + 1) * rows, :] = (cot[k][...].astype(F32) * slope).astype(BF16)
        out_buf[k] = (preact * gate).astype(BF16)
        leave(out_buf.at[k], out_out[k], out_sems.at[k])
    leave(grad_ref, grad_hbm, grad_sem)
    for which, full in ((0, full_feats), (1, full_agg)):
        prod_ref[...] = dot(grad_ref[...], full[...], 1, 1)
        wide = prod_ref.shape[1]
        for part in range(4):
            target = lax.rem(low + part, 4)
            slice_ref = slices_out[part] if part else kept_ref
            for k in range(reps):
                start = pl.multiple_of(k * rows + 16 * target, 16)
                slice_ref[16 * k : 16 * k + 16, which * wide : (which + 1) * wide] = prod_ref[
                    pl.ds(start, 16), :
                ].astype(BF16)
    leave(kept_ref, slices_out[0], kept_sem)
    w_neigh = jnp.concatenate([wts[k][1] for k in range(reps)], axis=0)
    back_ref[...] = dot(w_neigh, grad_ref[...], 0, 0)
    div = div_ref[0:1, lanes(rep, width)]
    for k in range(reps):
        target = lax.rem(rep + k, reps)
        scaled_out[k][...] = (back_ref[lanes(target, rows), :] / div).astype(BF16)
    for copy in copies:
        copy.wait()


def back_body(rep_ref, *refs):
    wts, grad_ref, back_out, back_ref = refs[0:4], refs[4], refs[5:9], refs[9]
    rep = rep_ref[0]
    reps = 4
    rows = back_out[0].shape[0]
    w_self = jnp.concatenate([wts[k][0] for k in range(reps)], axis=0)
    back_ref[...] = dot(w_self, grad_ref[...], 0, 0)
    for k in range(reps):
        target = lax.rem(rep + k, reps)
        back_out[k][...] = back_ref[lanes(target, rows), :]


def slice_sum_body(*refs):
    pieces, outs = refs[:4], refs[4:]
    total = pieces[0][...].astype(F32)
    for piece in pieces[1:]:
        total = total + piece[...].astype(F32)
    for k in range(len(outs)):
        outs[k][...] = total[16 * k : 16 * k + 16, :]


def add_body(*refs):
    total = refs[0][...]
    for ref in refs[1:-1]:
        total = total + ref[...]
    refs[-1][...] = total.astype(refs[-1].dtype)


def stack_body(*refs):
    rows = refs[0].shape[0]
    for k, ref in enumerate(refs[:-1]):
        refs[-1][rows * k : rows * (k + 1), :] = ref[...]


def join_body(place_ref, mine_ref, own_ref, other_ref, w_self_ref, w_neigh_ref, parts_ref):
    full = w_self_ref.shape[1]
    core = lax.rem(place_ref[1], 2)
    place = lax.rem(lax.div(place_ref[1], 2), 8)
    sign = 1 - 2 * core
    parts_ref[place] = mine_ref[...].astype(F32)
    for k in range(1, 5):
        rows = slice(16 * (k - 1), 16 * k)
        parts_ref[lax.rem(place + 8 - sign * k, 8)] = own_ref[rows, :].astype(F32)
        parts_ref[lax.rem(place + 8 + sign * k, 8)] = other_ref[rows, :].astype(F32)
    for low in range(4):
        total = parts_ref[low] + parts_ref[low + 4]
        w_self_ref[16 * low : 16 * low + 16, :] = total[:, :full]
        w_neigh_ref[16 * low : 16 * low + 16, :] = total[:, full:]


def gather_lanes(ref, pieces, rep):
    reps = len(pieces)
    width = pieces[0].shape[1]
    for k in range(reps):
        source = lax.rem(rep + reps - k, reps)
        ref[:, lanes(source, width)] = pieces[k][...]


def far_back_body(rep_ref, rows_ref, s0, s1, s2, s3, far_hbm, out_ref, full_ref, buf_ref, far_ref, sems, out_sems):
    chans = full_ref.shape[0]
    parts = far_ref.shape[0]
    for index in range(4):
        run_copy(far_hbm, far_ref, sems, index).start()
    gather_lanes(full_ref, (s0, s1, s2, s3), rep_ref[0])

    each = parts // 4

    def copy(step):
        rows = pl.ds(step * each, each)
        return pltpu.make_async_copy(buf_ref.at[rows], out_ref.at[rows], out_sems.at[step])

    for index, (first, count) in enumerate(runs(parts)):
        run_copy(far_hbm, far_ref, sems, index).wait()
        for part in range(first, first + count):
            for slot in range(2):
                row = rows_ref[slot, part]
                term = dot(full_ref[:, lanes(row, TILE)], far_ref[part, slot], 1, 0)
                buf_ref[part, slot * chans : (slot + 1) * chans, :] = term.astype(BF16)
            if (part + 1) % each == 0:
                copy(part // each).start()
    for step in range(4):
        copy(step).wait()


def near_back_body(rep_ref, cols_ref, *refs):
    scaled, back, outs = refs[0:4], refs[4:8], refs[8:12]
    near_ref, acc_ref, output_ref, full_ref = refs[12:16]
    rep = rep_ref[0]
    reps = 4
    width = scaled[0].shape[1]
    gather_lanes(full_ref, scaled, rep)
    gather_lanes(acc_ref, back, rep)
    for k in range(reps):
        output_ref[:, lanes(lax.rem(rep + k, reps), width)] = outs[k][...]

    @pl.loop(0, near_ref.shape[0] // 4)
    def _(step):
        for item in range(4):
            row = step * 4 + item
            for link in range(2):
                term = dot(full_ref[:, lanes(row, TILE)], near_ref[row, link], 1, 0)
                acc_ref[:, lanes(cols_ref[link, row], TILE)] += term


def home_body(send_ref, got_ref, near_acc_hbm, grad_ref, acc_ref, near_acc_ref, sem):
    chans = acc_ref.shape[0]
    parts = got_ref.shape[0]
    load = pltpu.make_async_copy(near_acc_hbm, near_acc_ref, sem)
    load.start()
    acc_ref[...] = jnp.zeros_like(acc_ref)
    for item in range(parts):
        for slot in range(2):
            block = send_ref[slot, item]
            acc_ref[:, lanes(block, TILE)] += got_ref[item, slot * chans : (slot + 1) * chans, :].astype(F32)
    load.wait()
    grad_ref[...] = (near_acc_ref[...] + acc_ref[...]).astype(BF16)


def local(feats, w_self, w_neigh, local_cols, local_tiles, send_list, remote_rows, remote_tiles, cotangent):
    chans, nodes = feats.shape
    full = w_self.shape[0]
    reps = full // chans
    width = nodes // reps
    parts = remote_tiles.shape[1]
    far_tiles = remote_tiles[0]
    rows = remote_rows[0].T
    sends = pinned(send_list[0].T)
    cols = local_cols.T
    rep = jnp.stack([lax.axis_index("rep"), lax.axis_index("dom")]).astype(jnp.int32)
    piece = shape((chans, width), BF16)
    piece32 = shape((chans, width), F32)
    sems = pltpu.SemaphoreType.DMA((parts // STEP,))
    sem = pltpu.SemaphoreType.DMA(())
    tile_buf = pltpu.VMEM(far_tiles.shape, BF16)
    wide32 = pltpu.VMEM((chans, nodes), F32)

    def shift(value, by):
        return lax.ppermute(value, "rep", [(i, (i + by) % reps) for i in range(reps)])

    def move(value, dy, dz, dc, turn=False):
        pairs = [
            ((y * 8 + z) * 2 + c, ((y + dy) % 4 * 8 + (z + (-dz if turn and c else dz)) % 8) * 2 + (c + dc) % 2)
            for y in range(4)
            for z in range(8)
            for c in range(2)
        ]
        return lax.ppermute(value, "dom", pairs)

    def move_low(value, k):
        pairs = [
            ((y * 8 + z) * 2 + c, (y * 8 + z // 4 * 4 + (z + k) % 4) * 2 + c)
            for y in range(4)
            for z in range(8)
            for c in range(2)
        ]
        return lax.ppermute(value, "dom", pairs)

    def exchange(pieces, sign=1):
        return [pieces[0]] + [shift(pieces[k], (sign * k) % reps) for k in range(1, reps)]

    with jax.named_scope("pick"):
        outgoing = call(
            pick_body, (sends,), (feats,), in_hbm((parts, 2 * chans, TILE), BF16),
            [pltpu.VMEM((chans, nodes), BF16), pltpu.VMEM((parts, 2 * chans, TILE), BF16), sems, sem], 2.0, (0,), (0,),
        )
    incoming = lax.all_to_all(outgoing, "dom", split_axis=0, concat_axis=0, tiled=True)

    with jax.named_scope("chunks"):
        pieces = call(chunk_body, (rep,), (feats, cotangent), [piece] * (2 * reps))
    feats_in = exchange(pieces[:reps])
    cot_in = exchange(pieces[reps:])
    weights_in = exchange([jnp.stack([w_self.T, w_neigh.T])] * reps)
    with jax.named_scope("near"):
        near_acc, div, turned = call(
            near_body, (cols, rows), (feats, local_tiles, far_tiles),
            [shape((chans, nodes), F32), shape((8, nodes), F32), in_hbm(far_tiles.shape, BF16)],
            [tile_buf, sems], 8.0, (), (2,),
        )
    incoming, feats_in, cot_in, weights_in, near_acc, div, turned = lax.optimization_barrier(
        (incoming, feats_in, cot_in, weights_in, near_acc, div, turned)
    )
    with jax.named_scope("far"):
        agg = call(
            far_body, (rep, rows), (incoming, turned, near_acc, div), [piece] * reps,
            [wide32, wide32, tile_buf, pltpu.VMEM((8, nodes), F32), sems, sem, sem], 6.0, (1, 2, 3),
        )
    agg_in = exchange(agg)

    with jax.named_scope("dense"):
        dense = call(
            dense_body, (rep,), (*agg_in, *feats_in, *cot_in, *weights_in, div),
            [piece] * reps
            + [in_hbm((chans, width), BF16)] * reps
            + [in_hbm((full, width), BF16), in_hbm((16 * reps, 2 * full), BF16)]
            + [shape((16 * reps, 2 * full), BF16)] * 3,
            [
                pltpu.VMEM((full, width), F32), pltpu.VMEM((full, width), BF16), pltpu.VMEM((full, width), BF16),
                pltpu.VMEM((full, width), BF16), pltpu.VMEM((reps, chans, width), BF16), pltpu.VMEM((full, full), F32),
                pltpu.VMEM((16 * reps, 2 * full), BF16), pltpu.SemaphoreType.DMA((reps,)), sem, sem,
            ],
            3.0, (), range(reps, 2 * reps + 2),
        )
    scaled, out_pieces, grad_pre, slices = dense[:reps], dense[reps : 2 * reps], dense[2 * reps], dense[2 * reps + 1 :]
    scaled_in = exchange(scaled)
    slices_in = [slices[0]] + [move_low(slices[k], k) for k in range(1, 4)]
    with jax.named_scope("far_back"):
        far_back = call(
            far_back_body, (rep, rows), (*scaled_in, far_tiles), in_hbm((parts, 2 * chans, TILE), BF16),
            [
                pltpu.VMEM((chans, nodes), BF16), pltpu.VMEM((parts, 2 * chans, TILE), BF16), tile_buf, sems, sems,
            ],
            5.0, (reps,), (0,),
        )
    slices_in, far_back = lax.optimization_barrier((slices_in, far_back))
    returned = lax.all_to_all(far_back, "dom", split_axis=0, concat_axis=0, tiled=True)

    with jax.named_scope("slice_sums"):
        slice_shape = shape((16, 2 * full), F32)
        sums = call(slice_sum_body, (), slices_in, [slice_shape] * reps)
        total = call(add_body, (), exchange(sums, -1), slice_shape)
        total = call(add_body, (), (total, move(total, 0, 0, 1)), slice_shape)
        others = [move(total, dy, 0, 0) for dy in range(1, 4)]
        total = call(add_body, (), (total, *others), shape((16, 2 * full), BF16))
    with jax.named_scope("back"):
        back_self = call(
            back_body, (rep,), (*weights_in, grad_pre), [piece32] * reps, [pltpu.VMEM((full, width), F32)], 1.0
        )
    back_in = exchange(back_self)
    out_in = exchange(out_pieces, -1)
    with jax.named_scope("near_back"):
        near_back, output = call(
            near_back_body, (rep, cols), (*scaled_in, *back_in, *out_in, local_tiles),
            [shape((chans, nodes), F32), shape((chans, nodes), BF16)], [pltpu.VMEM((chans, nodes), BF16)], 2.0,
        )
    total, near_back, output = lax.optimization_barrier((total, near_back, output))
    with jax.named_scope("spread"):
        own = call(
            stack_body, (), [move(total, 0, dz, 0, True) for dz in range(1, 5)], shape((64, 2 * full), BF16), (), 0.5
        )
        other = move(own, 0, 0, 1)
    with jax.named_scope("home"):
        grad_feats = call(
            home_body, (sends,), (returned, near_back), shape((chans, nodes), BF16), [wide32, wide32, sem], 3.0, (1,)
        )
    with jax.named_scope("join"):
        other, grad_feats = lax.optimization_barrier((other, grad_feats))
        wg_self, wg_neigh = call(
            join_body, (rep,), (total, own, other), [shape((chans, full), F32)] * 2, [pltpu.VMEM((8, 16, 2 * full), F32)]
        )
    return output, grad_feats, wg_self.T, wg_neigh.T


def solution(mesh):
    placed = (
        P("rep", "dom"),
        P(None, "rep"),
        P(None, "rep"),
        P("dom", None),
        P("dom", None, None, None),
        P("dom", None, None),
        P("dom", None, None),
        P("dom", None, None, None, None),
        P("rep", "dom"),
    )
    return jax.shard_map(
        local,
        mesh=mesh,
        in_specs=placed,
        out_specs=(P("rep", "dom"), P("rep", "dom"), P(None, "rep"), P(None, "rep")),
        check_vma=False,
    )
```

```python
import jax
import jax.numpy as jnp
from jax import lax
from jax.experimental import pallas as pl
from jax.experimental.pallas import tpu as pltpu
from jax.sharding import PartitionSpec as P

TILE = 128
STEP = 8
VMEM_BYTES = 12 * 1024 * 1024
F32 = jnp.float32
BF16 = jnp.bfloat16
IN_VMEM = pl.BlockSpec(memory_space=pltpu.VMEM)
IN_SMEM = pl.BlockSpec(memory_space=pltpu.SMEM)
IN_HBM = pl.BlockSpec(memory_space=pltpu.HBM)


def lanes(index, width):
    return pl.ds(pl.multiple_of(index * width, width), width)


def call(body, scalars, args, out_shape, scratch=(), micros=1.0, hbm=(), hbm_out=()):
    many = isinstance(out_shape, list)
    out_specs = [IN_HBM if i in hbm_out else IN_VMEM for i in range(len(out_shape) if many else 1)]
    out_specs = out_specs if many else out_specs[0]
    args = [pinned(arg) if i in hbm else arg for i, arg in enumerate(args)]
    return pl.pallas_call(
        body,
        in_specs=[IN_SMEM] * len(scalars) + [IN_HBM if i in hbm else IN_VMEM for i in range(len(args))],
        out_shape=out_shape,
        out_specs=out_specs,
        scratch_shapes=scratch,
        compiler_params=pltpu.CompilerParams(vmem_limit_bytes=VMEM_BYTES),
        cost_estimate=pl.CostEstimate(flops=int(micros * 1.1e9), bytes_accessed=1 << 16, transcendentals=0),
    )(*scalars, *args)


def shape(dims, kind):
    return jax.ShapeDtypeStruct(dims, kind)


def in_hbm(dims, kind):
    return pltpu.HBM(dims, kind)


def pinned(value):
    return pltpu.with_memory_space_constraint(value, pltpu.HBM)


def dot(left, right, left_dim, right_dim):
    return lax.dot_general(left, right, (((left_dim,), (right_dim,)), ((), ())), preferred_element_type=F32)


def pick_body(send_ref, feats_hbm, out_ref, feats_ref, buf_ref, sems, feats_sem):
    chans = feats_ref.shape[0]
    load = pltpu.make_async_copy(feats_hbm, feats_ref, feats_sem)
    load.start()
    load.wait()
    parts = buf_ref.shape[0]
    for step in range(parts // STEP):
        for item in range(step * STEP, (step + 1) * STEP):
            for slot in range(2):
                block = send_ref[slot, item]
                buf_ref[item, slot * chans : (slot + 1) * chans, :] = feats_ref[:, lanes(block, TILE)]
        rows = pl.ds(step * STEP, STEP)
        pltpu.make_async_copy(buf_ref.at[rows], out_ref.at[rows], sems.at[step]).start()
    for step in range(parts // STEP):
        rows = pl.ds(step * STEP, STEP)
        pltpu.make_async_copy(buf_ref.at[rows], out_ref.at[rows], sems.at[step]).wait()


def tile_copy(far_hbm, far_ref, sems, step):
    rows = pl.ds(step * STEP, STEP)
    return pltpu.make_async_copy(far_hbm.at[rows], far_ref.at[rows], sems.at[step])


def runs(parts):
    return [(0, parts // 8), (parts // 8, parts // 8), (parts // 4, parts // 4), (parts // 2, parts // 2)]


def run_copy(far_hbm, far_ref, sems, index):
    rows = pl.ds(*runs(far_ref.shape[0])[index])
    return pltpu.make_async_copy(far_hbm.at[rows], far_ref.at[rows], sems.at[index])


def chunk_body(rep_ref, feats_ref, cot_ref, *outs):
    reps = len(outs) // 2
    width = outs[0].shape[1]
    for k in range(reps):
        chunk = lax.rem(rep_ref[0] + k, reps)
        outs[k][...] = feats_ref[:, lanes(chunk, width)]
        outs[reps + k][...] = cot_ref[:, lanes(chunk, width)]


def near_body(cols_ref, rows_ref, feats_ref, near_ref, far_ref, acc_ref, div_ref, turned_hbm, turned_ref, sems):
    ones = jnp.ones((8, TILE), BF16)
    div_ref[...] = jnp.ones_like(div_ref)

    @pl.loop(0, near_ref.shape[0] // 4)
    def _(step):
        for item in range(4):
            row = step * 4 + item
            total = None
            sums = None
            for link in range(2):
                tile = near_ref[row, link]
                term = dot(feats_ref[:, lanes(cols_ref[link, row], TILE)], tile, 1, 1)
                part = dot(ones, tile, 1, 1)
                total = term if total is None else total + term
                sums = part if sums is None else sums + part
            acc_ref[:, lanes(row, TILE)] = total
            div_ref[:, lanes(row, TILE)] += sums

    @pl.loop(0, far_ref.shape[0] // STEP)
    def _(step):
        for item in range(STEP):
            for slot in range(2):
                part = step * STEP + item
                row = rows_ref[slot, part]
                turned = far_ref[part, slot].T
                turned_ref[part, slot] = turned
                div_ref[:, lanes(row, TILE)] += dot(ones, turned, 1, 0)
        tile_copy(turned_ref, turned_hbm, sems, step).start()

    for step in range(far_ref.shape[0] // STEP):
        tile_copy(turned_ref, turned_hbm, sems, step).wait()


def far_body(rep_ref, rows_ref, got_ref, far_hbm, near_acc_hbm, div_hbm, *rest):
    outs = rest[:4]
    acc_ref, second_ref, near_acc_ref, far_ref, div_ref, sems, acc_sem, div_sem = rest[4:]
    reps = len(outs)
    chans = acc_ref.shape[0]
    width = outs[0].shape[1]
    load_acc = pltpu.make_async_copy(near_acc_hbm, near_acc_ref, acc_sem)
    load_div = pltpu.make_async_copy(div_hbm, div_ref, div_sem)
    for index in range(4):
        run_copy(far_hbm, far_ref, sems, index).start()
    load_acc.start()
    load_div.start()
    acc_ref[...] = jnp.zeros_like(acc_ref)
    second_ref[...] = jnp.zeros_like(second_ref)

    for index, (first, count) in enumerate(runs(far_ref.shape[0])):
        run_copy(far_hbm, far_ref, sems, index).wait()
        for part in range(first, first + count):
            for slot in range(2):
                row = rows_ref[slot, part]
                block = got_ref[part, slot * chans : (slot + 1) * chans, :]
                (acc_ref, second_ref)[slot][:, lanes(row, TILE)] += dot(block, far_ref[part, slot], 1, 0)

    load_acc.wait()
    load_div.wait()
    for k in range(reps):
        where = lanes(lax.rem(rep_ref[0] + k, reps), width)
        total = near_acc_ref[:, where] + (acc_ref[:, where] + second_ref[:, where])
        outs[k][...] = (total / div_ref[0:1, where]).astype(BF16)


def gather_rows(ref, pieces, rep):
    reps = len(pieces)
    rows = pieces[0].shape[0]
    for k in range(reps):
        source = lax.rem(rep + reps - k, reps)
        ref[lanes(source, rows), :] = pieces[k][...]


def dense_body(rep_ref, *refs):
    agg, feats, cot, wts = refs[0:4], refs[4:8], refs[8:12], refs[12:16]
    div_ref = refs[16]
    scaled_out, out_out, grad_hbm, slices_out = refs[17:21], refs[21:25], refs[25], refs[26:30]
    back_ref, full_feats, full_agg, grad_ref, out_buf, prod_ref, kept_ref = refs[30:37]
    out_sems, grad_sem, kept_sem = refs[37:40]
    low = lax.rem(lax.div(rep_ref[1], 2), 4)
    rep = rep_ref[0]
    reps = 4
    rows, width = agg[0].shape
    gather_rows(full_feats, feats, rep)
    gather_rows(full_agg, agg, rep)
    copies = []

    def leave(source, target, sem):
        copies.append(pltpu.make_async_copy(source, target, sem))
        copies[-1].start()

    for k in range(reps):
        preact = dot(wts[k][0], full_feats[...], 1, 0) + dot(wts[k][1], full_agg[...], 1, 0)
        gate = jax.nn.sigmoid(preact)
        slope = gate * (1.0 + preact * (1.0 - gate))
        grad_ref[k * rows : (k + 1) * rows, :] = (cot[k][...].astype(F32) * slope).astype(BF16)
        out_buf[k] = (preact * gate).astype(BF16)
        leave(out_buf.at[k], out_out[k], out_sems.at[k])
    leave(grad_ref, grad_hbm, grad_sem)
    for which, full in ((0, full_feats), (1, full_agg)):
        prod_ref[...] = dot(grad_ref[...], full[...], 1, 1)
        wide = prod_ref.shape[1]
        for part in range(4):
            target = lax.rem(low + part, 4)
            slice_ref = slices_out[part] if part else kept_ref
            for k in range(reps):
                start = pl.multiple_of(k * rows + 16 * target, 16)
                slice_ref[16 * k : 16 * k + 16, which * wide : (which + 1) * wide] = prod_ref[
                    pl.ds(start, 16), :
                ].astype(BF16)
    leave(kept_ref, slices_out[0], kept_sem)
    w_neigh = jnp.concatenate([wts[k][1] for k in range(reps)], axis=0)
    back_ref[...] = dot(w_neigh, grad_ref[...], 0, 0)
    div = div_ref[0:1, lanes(rep, width)]
    for k in range(reps):
        target = lax.rem(rep + k, reps)
        scaled_out[k][...] = (back_ref[lanes(target, rows), :] / div).astype(BF16)
    for copy in copies:
        copy.wait()


def back_body(rep_ref, *refs):
    wts, grad_ref, back_out, back_ref = refs[0:4], refs[4], refs[5:9], refs[9]
    rep = rep_ref[0]
    reps = 4
    rows = back_out[0].shape[0]
    w_self = jnp.concatenate([wts[k][0] for k in range(reps)], axis=0)
    back_ref[...] = dot(w_self, grad_ref[...], 0, 0)
    for k in range(reps):
        target = lax.rem(rep + k, reps)
        back_out[k][...] = back_ref[lanes(target, rows), :]


def slice_sum_body(*refs):
    pieces, outs = refs[:4], refs[4:]
    total = pieces[0][...].astype(F32)
    for piece in pieces[1:]:
        total = total + piece[...].astype(F32)
    for k in range(len(outs)):
        outs[k][...] = total[16 * k : 16 * k + 16, :]


def add_body(*refs):
    total = refs[0][...]
    for ref in refs[1:-1]:
        total = total + ref[...]
    refs[-1][...] = total.astype(refs[-1].dtype)


def stack_body(*refs):
    rows = refs[0].shape[0]
    for k, ref in enumerate(refs[:-1]):
        refs[-1][rows * k : rows * (k + 1), :] = ref[...]


def join_body(place_ref, mine_ref, own_ref, other_ref, w_self_ref, w_neigh_ref, parts_ref):
    full = w_self_ref.shape[1]
    core = lax.rem(place_ref[1], 2)
    place = lax.rem(lax.div(place_ref[1], 2), 8)
    sign = 1 - 2 * core
    parts_ref[place] = mine_ref[...].astype(F32)
    for k in range(1, 5):
        rows = slice(16 * (k - 1), 16 * k)
        parts_ref[lax.rem(place + 8 - sign * k, 8)] = own_ref[rows, :].astype(F32)
        parts_ref[lax.rem(place + 8 + sign * k, 8)] = other_ref[rows, :].astype(F32)
    for low in range(4):
        total = parts_ref[low] + parts_ref[low + 4]
        w_self_ref[16 * low : 16 * low + 16, :] = total[:, :full]
        w_neigh_ref[16 * low : 16 * low + 16, :] = total[:, full:]


def gather_lanes(ref, pieces, rep):
    reps = len(pieces)
    width = pieces[0].shape[1]
    for k in range(reps):
        source = lax.rem(rep + reps - k, reps)
        ref[:, lanes(source, width)] = pieces[k][...]


def far_back_body(rep_ref, rows_ref, s0, s1, s2, s3, far_hbm, out_ref, full_ref, buf_ref, far_ref, sems, out_sems):
    chans = full_ref.shape[0]
    parts = far_ref.shape[0]
    for index in range(4):
        run_copy(far_hbm, far_ref, sems, index).start()
    gather_lanes(full_ref, (s0, s1, s2, s3), rep_ref[0])

    each = parts // 4

    def copy(step):
        rows = pl.ds(step * each, each)
        return pltpu.make_async_copy(buf_ref.at[rows], out_ref.at[rows], out_sems.at[step])

    for index, (first, count) in enumerate(runs(parts)):
        run_copy(far_hbm, far_ref, sems, index).wait()
        for part in range(first, first + count):
            for slot in range(2):
                row = rows_ref[slot, part]
                term = dot(full_ref[:, lanes(row, TILE)], far_ref[part, slot], 1, 0)
                buf_ref[part, slot * chans : (slot + 1) * chans, :] = term.astype(BF16)
            if (part + 1) % each == 0:
                copy(part // each).start()
    for step in range(4):
        copy(step).wait()


def near_back_body(rep_ref, cols_ref, *refs):
    scaled, back, outs = refs[0:4], refs[4:8], refs[8:12]
    near_ref, acc_ref, output_ref, full_ref = refs[12:16]
    rep = rep_ref[0]
    reps = 4
    width = scaled[0].shape[1]
    gather_lanes(full_ref, scaled, rep)
    gather_lanes(acc_ref, back, rep)
    for k in range(reps):
        output_ref[:, lanes(lax.rem(rep + k, reps), width)] = outs[k][...]

    @pl.loop(0, near_ref.shape[0] // 4)
    def _(step):
        for item in range(4):
            row = step * 4 + item
            for link in range(2):
                term = dot(full_ref[:, lanes(row, TILE)], near_ref[row, link], 1, 0)
                acc_ref[:, lanes(cols_ref[link, row], TILE)] += term


def home_body(send_ref, got_ref, near_acc_hbm, grad_ref, acc_ref, second_ref, near_acc_ref, sem):
    chans = acc_ref.shape[0]
    parts = got_ref.shape[0]
    load = pltpu.make_async_copy(near_acc_hbm, near_acc_ref, sem)
    load.start()
    acc_ref[...] = jnp.zeros_like(acc_ref)
    second_ref[...] = jnp.zeros_like(second_ref)
    for item in range(parts):
        for slot in range(2):
            block = send_ref[slot, item]
            target = (acc_ref, second_ref)[slot]
            target[:, lanes(block, TILE)] += got_ref[item, slot * chans : (slot + 1) * chans, :].astype(F32)
    load.wait()
    grad_ref[...] = (near_acc_ref[...] + (acc_ref[...] + second_ref[...])).astype(BF16)


def local(feats, w_self, w_neigh, local_cols, local_tiles, send_list, remote_rows, remote_tiles, cotangent):
    chans, nodes = feats.shape
    full = w_self.shape[0]
    reps = full // chans
    width = nodes // reps
    parts = remote_tiles.shape[1]
    far_tiles = remote_tiles[0]
    rows = remote_rows[0].T
    sends = pinned(send_list[0].T)
    cols = local_cols.T
    rep = jnp.stack([lax.axis_index("rep"), lax.axis_index("dom")]).astype(jnp.int32)
    piece = shape((chans, width), BF16)
    piece32 = shape((chans, width), F32)
    sems = pltpu.SemaphoreType.DMA((parts // STEP,))
    sem = pltpu.SemaphoreType.DMA(())
    tile_buf = pltpu.VMEM(far_tiles.shape, BF16)
    wide32 = pltpu.VMEM((chans, nodes), F32)

    def shift(value, by):
        return lax.ppermute(value, "rep", [(i, (i + by) % reps) for i in range(reps)])

    def move(value, dy, dz, dc, turn=False):
        pairs = [
            ((y * 8 + z) * 2 + c, ((y + dy) % 4 * 8 + (z + (-dz if turn and c else dz)) % 8) * 2 + (c + dc) % 2)
            for y in range(4)
            for z in range(8)
            for c in range(2)
        ]
        return lax.ppermute(value, "dom", pairs)

    def move_low(value, k):
        pairs = [
            ((y * 8 + z) * 2 + c, (y * 8 + z // 4 * 4 + (z + k) % 4) * 2 + c)
            for y in range(4)
            for z in range(8)
            for c in range(2)
        ]
        return lax.ppermute(value, "dom", pairs)

    def exchange(pieces, sign=1):
        return [pieces[0]] + [shift(pieces[k], (sign * k) % reps) for k in range(1, reps)]

    with jax.named_scope("pick"):
        outgoing = call(
            pick_body, (sends,), (feats,), in_hbm((parts, 2 * chans, TILE), BF16),
            [pltpu.VMEM((chans, nodes), BF16), pltpu.VMEM((parts, 2 * chans, TILE), BF16), sems, sem], 2.0, (0,), (0,),
        )
    incoming = lax.all_to_all(outgoing, "dom", split_axis=0, concat_axis=0, tiled=True)

    with jax.named_scope("chunks"):
        pieces = call(chunk_body, (rep,), (feats, cotangent), [piece] * (2 * reps))
    feats_in = exchange(pieces[:reps])
    cot_in = exchange(pieces[reps:])
    weights_in = exchange([jnp.stack([w_self.T, w_neigh.T])] * reps)
    with jax.named_scope("near"):
        near_acc, div, turned = call(
            near_body, (cols, rows), (feats, local_tiles, far_tiles),
            [shape((chans, nodes), F32), shape((8, nodes), F32), in_hbm(far_tiles.shape, BF16)],
            [tile_buf, sems], 8.0, (), (2,),
        )
    incoming, feats_in, cot_in, weights_in, near_acc, div, turned = lax.optimization_barrier(
        (incoming, feats_in, cot_in, weights_in, near_acc, div, turned)
    )
    with jax.named_scope("far"):
        agg = call(
            far_body, (rep, rows), (incoming, turned, near_acc, div), [piece] * reps,
            [wide32, wide32, wide32, tile_buf, pltpu.VMEM((8, nodes), F32), sems, sem, sem], 6.0, (1, 2, 3),
        )
    agg_in = exchange(agg)

    with jax.named_scope("dense"):
        dense = call(
            dense_body, (rep,), (*agg_in, *feats_in, *cot_in, *weights_in, div),
            [piece] * reps
            + [in_hbm((chans, width), BF16)] * reps
            + [in_hbm((full, width), BF16), in_hbm((16 * reps, 2 * full), BF16)]
            + [shape((16 * reps, 2 * full), BF16)] * 3,
            [
                pltpu.VMEM((full, width), F32), pltpu.VMEM((full, width), BF16), pltpu.VMEM((full, width), BF16),
                pltpu.VMEM((full, width), BF16), pltpu.VMEM((reps, chans, width), BF16), pltpu.VMEM((full, full), F32),
                pltpu.VMEM((16 * reps, 2 * full), BF16), pltpu.SemaphoreType.DMA((reps,)), sem, sem,
            ],
            3.0, (), range(reps, 2 * reps + 2),
        )
    scaled, out_pieces, grad_pre, slices = dense[:reps], dense[reps : 2 * reps], dense[2 * reps], dense[2 * reps + 1 :]
    scaled_in = exchange(scaled)
    slices_in = [slices[0]] + [move_low(slices[k], k) for k in range(1, 4)]
    with jax.named_scope("far_back"):
        far_back = call(
            far_back_body, (rep, rows), (*scaled_in, far_tiles), in_hbm((parts, 2 * chans, TILE), BF16),
            [
                pltpu.VMEM((chans, nodes), BF16), pltpu.VMEM((parts, 2 * chans, TILE), BF16), tile_buf, sems, sems,
            ],
            5.0, (reps,), (0,),
        )
    slices_in, far_back = lax.optimization_barrier((slices_in, far_back))
    returned = lax.all_to_all(far_back, "dom", split_axis=0, concat_axis=0, tiled=True)

    with jax.named_scope("slice_sums"):
        slice_shape = shape((16, 2 * full), F32)
        sums = call(slice_sum_body, (), slices_in, [slice_shape] * reps)
        total = call(add_body, (), exchange(sums, -1), slice_shape)
        total = call(add_body, (), (total, move(total, 0, 0, 1)), slice_shape)
        others = [move(total, dy, 0, 0) for dy in range(1, 4)]
        total = call(add_body, (), (total, *others), shape((16, 2 * full), BF16))
    with jax.named_scope("back"):
        back_self = call(
            back_body, (rep,), (*weights_in, grad_pre), [piece32] * reps, [pltpu.VMEM((full, width), F32)], 1.0
        )
    back_in = exchange(back_self)
    out_in = exchange(out_pieces, -1)
    with jax.named_scope("near_back"):
        near_back, output = call(
            near_back_body, (rep, cols), (*scaled_in, *back_in, *out_in, local_tiles),
            [shape((chans, nodes), F32), shape((chans, nodes), BF16)], [pltpu.VMEM((chans, nodes), BF16)], 2.0,
        )
    total, near_back, output = lax.optimization_barrier((total, near_back, output))
    with jax.named_scope("spread"):
        own = call(
            stack_body, (), [move(total, 0, dz, 0, True) for dz in range(1, 5)], shape((64, 2 * full), BF16), (), 0.5
        )
        other = move(own, 0, 0, 1)
    with jax.named_scope("home"):
        grad_feats = call(
            home_body, (sends,), (returned, near_back), shape((chans, nodes), BF16), [wide32, wide32, wide32, sem], 3.0, (1,)
        )
    with jax.named_scope("join"):
        other, grad_feats = lax.optimization_barrier((other, grad_feats))
        wg_self, wg_neigh = call(
            join_body, (rep,), (total, own, other), [shape((chans, full), F32)] * 2, [pltpu.VMEM((8, 16, 2 * full), F32)]
        )
    return output, grad_feats, wg_self.T, wg_neigh.T


def solution(mesh):
    placed = (
        P("rep", "dom"),
        P(None, "rep"),
        P(None, "rep"),
        P("dom", None),
        P("dom", None, None, None),
        P("dom", None, None),
        P("dom", None, None),
        P("dom", None, None, None, None),
        P("rep", "dom"),
    )
    return jax.shard_map(
        local,
        mesh=mesh,
        in_specs=placed,
        out_specs=(P("rep", "dom"), P("rep", "dom"), P(None, "rep"), P(None, "rep")),
        check_vma=False,
    )
```

```python
import jax
import jax.numpy as jnp
from jax import lax
from jax.experimental import pallas as pl
from jax.experimental.pallas import tpu as pltpu
from jax.sharding import PartitionSpec as P

TILE = 128
STEP = 8
VMEM_BYTES = 12 * 1024 * 1024
F32 = jnp.float32
BF16 = jnp.bfloat16
IN_VMEM = pl.BlockSpec(memory_space=pltpu.VMEM)
IN_SMEM = pl.BlockSpec(memory_space=pltpu.SMEM)
IN_HBM = pl.BlockSpec(memory_space=pltpu.HBM)


def lanes(index, width):
    return pl.ds(pl.multiple_of(index * width, width), width)


def call(body, scalars, args, out_shape, scratch=(), micros=1.0, hbm=(), hbm_out=()):
    many = isinstance(out_shape, list)
    out_specs = [IN_HBM if i in hbm_out else IN_VMEM for i in range(len(out_shape) if many else 1)]
    out_specs = out_specs if many else out_specs[0]
    args = [pinned(arg) if i in hbm else arg for i, arg in enumerate(args)]
    return pl.pallas_call(
        body,
        in_specs=[IN_SMEM] * len(scalars) + [IN_HBM if i in hbm else IN_VMEM for i in range(len(args))],
        out_shape=out_shape,
        out_specs=out_specs,
        scratch_shapes=scratch,
        compiler_params=pltpu.CompilerParams(vmem_limit_bytes=VMEM_BYTES),
        cost_estimate=pl.CostEstimate(flops=int(micros * 1.1e9), bytes_accessed=1 << 16, transcendentals=0),
    )(*scalars, *args)


def shape(dims, kind):
    return jax.ShapeDtypeStruct(dims, kind)


def in_hbm(dims, kind):
    return pltpu.HBM(dims, kind)


def pinned(value):
    return pltpu.with_memory_space_constraint(value, pltpu.HBM)


def dot(left, right, left_dim, right_dim):
    return lax.dot_general(left, right, (((left_dim,), (right_dim,)), ((), ())), preferred_element_type=F32)


def pick_body(send_ref, feats_hbm, out_ref, feats_ref, buf_ref, sems, feats_sem):
    chans = feats_ref.shape[0]
    load = pltpu.make_async_copy(feats_hbm, feats_ref, feats_sem)
    load.start()
    load.wait()
    parts = buf_ref.shape[0]
    for step in range(parts // STEP):
        for item in range(step * STEP, (step + 1) * STEP):
            for slot in range(2):
                block = send_ref[slot, item]
                buf_ref[item, slot * chans : (slot + 1) * chans, :] = feats_ref[:, lanes(block, TILE)]
        rows = pl.ds(step * STEP, STEP)
        pltpu.make_async_copy(buf_ref.at[rows], out_ref.at[rows], sems.at[step]).start()
    for step in range(parts // STEP):
        rows = pl.ds(step * STEP, STEP)
        pltpu.make_async_copy(buf_ref.at[rows], out_ref.at[rows], sems.at[step]).wait()


def tile_copy(far_hbm, far_ref, sems, step):
    rows = pl.ds(step * STEP, STEP)
    return pltpu.make_async_copy(far_hbm.at[rows], far_ref.at[rows], sems.at[step])


def runs(parts):
    return [(0, parts // 8), (parts // 8, 3 * parts // 8), (parts // 2, parts // 2)]


def run_copy(far_hbm, far_ref, sems, index):
    rows = pl.ds(*runs(far_ref.shape[0])[index])
    return pltpu.make_async_copy(far_hbm.at[rows], far_ref.at[rows], sems.at[index])


def chunk_body(rep_ref, feats_ref, cot_ref, *outs):
    reps = len(outs) // 2
    width = outs[0].shape[1]
    for k in range(reps):
        chunk = lax.rem(rep_ref[0] + k, reps)
        outs[k][...] = feats_ref[:, lanes(chunk, width)]
        outs[reps + k][...] = cot_ref[:, lanes(chunk, width)]


def near_body(cols_ref, rows_ref, feats_ref, near_ref, far_ref, acc_ref, div_ref, turned_hbm, turned_ref, sems):
    ones = jnp.ones((8, TILE), BF16)
    div_ref[...] = jnp.ones_like(div_ref)

    @pl.loop(0, near_ref.shape[0] // 4)
    def _(step):
        for item in range(4):
            row = step * 4 + item
            total = None
            sums = None
            for link in range(2):
                tile = near_ref[row, link]
                term = dot(feats_ref[:, lanes(cols_ref[link, row], TILE)], tile, 1, 1)
                part = dot(ones, tile, 1, 1)
                total = term if total is None else total + term
                sums = part if sums is None else sums + part
            acc_ref[:, lanes(row, TILE)] = total
            div_ref[:, lanes(row, TILE)] += sums

    @pl.loop(0, far_ref.shape[0] // STEP)
    def _(step):
        for item in range(STEP):
            for slot in range(2):
                part = step * STEP + item
                row = rows_ref[slot, part]
                turned = far_ref[part, slot].T
                turned_ref[part, slot] = turned
                div_ref[:, lanes(row, TILE)] += dot(ones, turned, 1, 0)
        tile_copy(turned_ref, turned_hbm, sems, step).start()

    for step in range(far_ref.shape[0] // STEP):
        tile_copy(turned_ref, turned_hbm, sems, step).wait()


def far_body(rep_ref, rows_ref, got_ref, far_hbm, near_acc_hbm, div_hbm, *rest):
    outs = rest[:4]
    acc_ref, near_acc_ref, far_ref, div_ref, sems, acc_sem, div_sem = rest[4:]
    reps = len(outs)
    chans = acc_ref.shape[0]
    width = outs[0].shape[1]
    load_acc = pltpu.make_async_copy(near_acc_hbm, near_acc_ref, acc_sem)
    load_div = pltpu.make_async_copy(div_hbm, div_ref, div_sem)
    for index in range(3):
        run_copy(far_hbm, far_ref, sems, index).start()
    load_acc.start()
    load_div.start()
    acc_ref[...] = jnp.zeros_like(acc_ref)

    for index, (first, count) in enumerate(runs(far_ref.shape[0])):
        run_copy(far_hbm, far_ref, sems, index).wait()
        for part in range(first, first + count):
            for slot in range(2):
                row = rows_ref[slot, part]
                block = got_ref[part, slot * chans : (slot + 1) * chans, :]
                acc_ref[:, lanes(row, TILE)] += dot(block, far_ref[part, slot], 1, 0)

    load_acc.wait()
    load_div.wait()
    for k in range(reps):
        where = lanes(lax.rem(rep_ref[0] + k, reps), width)
        outs[k][...] = ((near_acc_ref[:, where] + acc_ref[:, where]) / div_ref[0:1, where]).astype(BF16)


def gather_rows(ref, pieces, rep):
    reps = len(pieces)
    rows = pieces[0].shape[0]
    for k in range(reps):
        source = lax.rem(rep + reps - k, reps)
        ref[lanes(source, rows), :] = pieces[k][...]


def dense_body(rep_ref, *refs):
    agg, feats, cot, wts = refs[0:4], refs[4:8], refs[8:12], refs[12:16]
    div_ref = refs[16]
    scaled_out, out_out, grad_hbm, slices_out = refs[17:21], refs[21:25], refs[25], refs[26:30]
    back_ref, full_feats, full_agg, grad_ref, out_buf, prod_ref, kept_ref = refs[30:37]
    out_sems, grad_sem, kept_sem = refs[37:40]
    low = lax.rem(lax.div(rep_ref[1], 2), 4)
    rep = rep_ref[0]
    reps = 4
    rows, width = agg[0].shape
    gather_rows(full_feats, feats, rep)
    gather_rows(full_agg, agg, rep)
    copies = []

    def leave(source, target, sem):
        copies.append(pltpu.make_async_copy(source, target, sem))
        copies[-1].start()

    for k in range(reps):
        preact = dot(wts[k][0], full_feats[...], 1, 0) + dot(wts[k][1], full_agg[...], 1, 0)
        gate = jax.nn.sigmoid(preact)
        slope = gate * (1.0 + preact * (1.0 - gate))
        grad_ref[k * rows : (k + 1) * rows, :] = (cot[k][...].astype(F32) * slope).astype(BF16)
        out_buf[k] = (preact * gate).astype(BF16)
        leave(out_buf.at[k], out_out[k], out_sems.at[k])
    leave(grad_ref, grad_hbm, grad_sem)
    for which, full in ((0, full_feats), (1, full_agg)):
        prod_ref[...] = dot(grad_ref[...], full[...], 1, 1)
        wide = prod_ref.shape[1]
        for part in range(4):
            target = lax.rem(low + part, 4)
            slice_ref = slices_out[part] if part else kept_ref
            for k in range(reps):
                start = pl.multiple_of(k * rows + 16 * target, 16)
                slice_ref[16 * k : 16 * k + 16, which * wide : (which + 1) * wide] = prod_ref[
                    pl.ds(start, 16), :
                ].astype(BF16)
    leave(kept_ref, slices_out[0], kept_sem)
    w_neigh = jnp.concatenate([wts[k][1] for k in range(reps)], axis=0)
    back_ref[...] = dot(w_neigh, grad_ref[...], 0, 0)
    div = div_ref[0:1, lanes(rep, width)]
    for k in range(reps):
        target = lax.rem(rep + k, reps)
        scaled_out[k][...] = (back_ref[lanes(target, rows), :] / div).astype(BF16)
    for copy in copies:
        copy.wait()


def back_body(rep_ref, *refs):
    wts, grad_ref, back_out, back_ref = refs[0:4], refs[4], refs[5:9], refs[9]
    rep = rep_ref[0]
    reps = 4
    rows = back_out[0].shape[0]
    w_self = jnp.concatenate([wts[k][0] for k in range(reps)], axis=0)
    back_ref[...] = dot(w_self, grad_ref[...], 0, 0)
    for k in range(reps):
        target = lax.rem(rep + k, reps)
        back_out[k][...] = back_ref[lanes(target, rows), :]


def slice_sum_body(*refs):
    pieces, outs = refs[:4], refs[4:]
    total = pieces[0][...].astype(F32)
    for piece in pieces[1:]:
        total = total + piece[...].astype(F32)
    for k in range(len(outs)):
        outs[k][...] = total[16 * k : 16 * k + 16, :]


def add_body(*refs):
    total = refs[0][...]
    for ref in refs[1:-1]:
        total = total + ref[...]
    refs[-1][...] = total.astype(refs[-1].dtype)


def stack_body(*refs):
    rows = refs[0].shape[0]
    for k, ref in enumerate(refs[:-1]):
        refs[-1][rows * k : rows * (k + 1), :] = ref[...]


def join_body(place_ref, mine_ref, own_ref, other_ref, w_self_ref, w_neigh_ref, parts_ref):
    full = w_self_ref.shape[1]
    core = lax.rem(place_ref[1], 2)
    place = lax.rem(lax.div(place_ref[1], 2), 8)
    sign = 1 - 2 * core
    parts_ref[place] = mine_ref[...].astype(F32)
    for k in range(1, 5):
        rows = slice(16 * (k - 1), 16 * k)
        parts_ref[lax.rem(place + 8 - sign * k, 8)] = own_ref[rows, :].astype(F32)
        parts_ref[lax.rem(place + 8 + sign * k, 8)] = other_ref[rows, :].astype(F32)
    for low in range(4):
        total = parts_ref[low] + parts_ref[low + 4]
        w_self_ref[16 * low : 16 * low + 16, :] = total[:, :full]
        w_neigh_ref[16 * low : 16 * low + 16, :] = total[:, full:]


def gather_lanes(ref, pieces, rep):
    reps = len(pieces)
    width = pieces[0].shape[1]
    for k in range(reps):
        source = lax.rem(rep + reps - k, reps)
        ref[:, lanes(source, width)] = pieces[k][...]


def far_back_body(rep_ref, rows_ref, s0, s1, s2, s3, far_hbm, out_ref, full_ref, buf_ref, far_ref, sems, out_sems):
    chans = full_ref.shape[0]
    parts = far_ref.shape[0]
    for index in range(3):
        run_copy(far_hbm, far_ref, sems, index).start()
    gather_lanes(full_ref, (s0, s1, s2, s3), rep_ref[0])

    each = parts // 4

    def copy(step):
        rows = pl.ds(step * each, each)
        return pltpu.make_async_copy(buf_ref.at[rows], out_ref.at[rows], out_sems.at[step])

    for index, (first, count) in enumerate(runs(parts)):
        run_copy(far_hbm, far_ref, sems, index).wait()
        for part in range(first, first + count):
            for slot in range(2):
                row = rows_ref[slot, part]
                term = dot(full_ref[:, lanes(row, TILE)], far_ref[part, slot], 1, 0)
                buf_ref[part, slot * chans : (slot + 1) * chans, :] = term.astype(BF16)
            if (part + 1) % each == 0:
                copy(part // each).start()
    for step in range(4):
        copy(step).wait()


def near_back_body(rep_ref, cols_ref, *refs):
    scaled, back, outs = refs[0:4], refs[4:8], refs[8:12]
    near_ref, acc_ref, output_ref, full_ref = refs[12:16]
    rep = rep_ref[0]
    reps = 4
    width = scaled[0].shape[1]
    gather_lanes(full_ref, scaled, rep)
    gather_lanes(acc_ref, back, rep)
    for k in range(reps):
        output_ref[:, lanes(lax.rem(rep + k, reps), width)] = outs[k][...]

    @pl.loop(0, near_ref.shape[0] // 4)
    def _(step):
        for item in range(4):
            row = step * 4 + item
            for link in range(2):
                term = dot(full_ref[:, lanes(row, TILE)], near_ref[row, link], 1, 0)
                acc_ref[:, lanes(cols_ref[link, row], TILE)] += term


def home_body(send_ref, got_ref, near_acc_hbm, grad_ref, acc_ref, near_acc_ref, sem):
    chans = acc_ref.shape[0]
    parts = got_ref.shape[0]
    load = pltpu.make_async_copy(near_acc_hbm, near_acc_ref, sem)
    load.start()
    acc_ref[...] = jnp.zeros_like(acc_ref)
    for item in range(parts):
        for slot in range(2):
            block = send_ref[slot, item]
            acc_ref[:, lanes(block, TILE)] += got_ref[item, slot * chans : (slot + 1) * chans, :].astype(F32)
    load.wait()
    grad_ref[...] = (near_acc_ref[...] + acc_ref[...]).astype(BF16)


def local(feats, w_self, w_neigh, local_cols, local_tiles, send_list, remote_rows, remote_tiles, cotangent):
    chans, nodes = feats.shape
    full = w_self.shape[0]
    reps = full // chans
    width = nodes // reps
    parts = remote_tiles.shape[1]
    far_tiles = remote_tiles[0]
    rows = remote_rows[0].T
    sends = pinned(send_list[0].T)
    cols = local_cols.T
    rep = jnp.stack([lax.axis_index("rep"), lax.axis_index("dom")]).astype(jnp.int32)
    piece = shape((chans, width), BF16)
    piece32 = shape((chans, width), F32)
    sems = pltpu.SemaphoreType.DMA((parts // STEP,))
    sem = pltpu.SemaphoreType.DMA(())
    tile_buf = pltpu.VMEM(far_tiles.shape, BF16)
    wide32 = pltpu.VMEM((chans, nodes), F32)

    def shift(value, by):
        return lax.ppermute(value, "rep", [(i, (i + by) % reps) for i in range(reps)])

    def move(value, dy, dz, dc, turn=False):
        pairs = [
            ((y * 8 + z) * 2 + c, ((y + dy) % 4 * 8 + (z + (-dz if turn and c else dz)) % 8) * 2 + (c + dc) % 2)
            for y in range(4)
            for z in range(8)
            for c in range(2)
        ]
        return lax.ppermute(value, "dom", pairs)

    def move_low(value, k):
        pairs = [
            ((y * 8 + z) * 2 + c, (y * 8 + z // 4 * 4 + (z + k) % 4) * 2 + c)
            for y in range(4)
            for z in range(8)
            for c in range(2)
        ]
        return lax.ppermute(value, "dom", pairs)

    def exchange(pieces, sign=1):
        return [pieces[0]] + [shift(pieces[k], (sign * k) % reps) for k in range(1, reps)]

    with jax.named_scope("pick"):
        outgoing = call(
            pick_body, (sends,), (feats,), in_hbm((parts, 2 * chans, TILE), BF16),
            [pltpu.VMEM((chans, nodes), BF16), pltpu.VMEM((parts, 2 * chans, TILE), BF16), sems, sem], 2.0, (0,), (0,),
        )
    incoming = lax.all_to_all(outgoing, "dom", split_axis=0, concat_axis=0, tiled=True)

    with jax.named_scope("chunks"):
        pieces = call(chunk_body, (rep,), (feats, cotangent), [piece] * (2 * reps))
    feats_in = exchange(pieces[:reps])
    cot_in = exchange(pieces[reps:])
    weights_in = exchange([jnp.stack([w_self.T, w_neigh.T])] * reps)
    with jax.named_scope("near"):
        near_acc, div, turned = call(
            near_body, (cols, rows), (feats, local_tiles, far_tiles),
            [shape((chans, nodes), F32), shape((8, nodes), F32), in_hbm(far_tiles.shape, BF16)],
            [tile_buf, sems], 8.0, (), (2,),
        )
    incoming, feats_in, cot_in, weights_in, near_acc, div, turned = lax.optimization_barrier(
        (incoming, feats_in, cot_in, weights_in, near_acc, div, turned)
    )
    with jax.named_scope("far"):
        agg = call(
            far_body, (rep, rows), (incoming, turned, near_acc, div), [piece] * reps,
            [wide32, wide32, tile_buf, pltpu.VMEM((8, nodes), F32), sems, sem, sem], 6.0, (1, 2, 3),
        )
    agg_in = exchange(agg)

    with jax.named_scope("dense"):
        dense = call(
            dense_body, (rep,), (*agg_in, *feats_in, *cot_in, *weights_in, div),
            [piece] * reps
            + [in_hbm((chans, width), BF16)] * reps
            + [in_hbm((full, width), BF16), in_hbm((16 * reps, 2 * full), BF16)]
            + [shape((16 * reps, 2 * full), BF16)] * 3,
            [
                pltpu.VMEM((full, width), F32), pltpu.VMEM((full, width), BF16), pltpu.VMEM((full, width), BF16),
                pltpu.VMEM((full, width), BF16), pltpu.VMEM((reps, chans, width), BF16), pltpu.VMEM((full, full), F32),
                pltpu.VMEM((16 * reps, 2 * full), BF16), pltpu.SemaphoreType.DMA((reps,)), sem, sem,
            ],
            3.0, (), range(reps, 2 * reps + 2),
        )
    scaled, out_pieces, grad_pre, slices = dense[:reps], dense[reps : 2 * reps], dense[2 * reps], dense[2 * reps + 1 :]
    scaled_in = exchange(scaled)
    slices_in = [slices[0]] + [move_low(slices[k], k) for k in range(1, 4)]
    with jax.named_scope("far_back"):
        far_back = call(
            far_back_body, (rep, rows), (*scaled_in, far_tiles), in_hbm((parts, 2 * chans, TILE), BF16),
            [
                pltpu.VMEM((chans, nodes), BF16), pltpu.VMEM((parts, 2 * chans, TILE), BF16), tile_buf, sems, sems,
            ],
            5.0, (reps,), (0,),
        )
    slices_in, far_back = lax.optimization_barrier((slices_in, far_back))
    returned = lax.all_to_all(far_back, "dom", split_axis=0, concat_axis=0, tiled=True)

    with jax.named_scope("slice_sums"):
        slice_shape = shape((16, 2 * full), F32)
        sums = call(slice_sum_body, (), slices_in, [slice_shape] * reps)
        total = call(add_body, (), exchange(sums, -1), slice_shape)
        total = call(add_body, (), (total, move(total, 0, 0, 1)), slice_shape)
        others = [move(total, dy, 0, 0) for dy in range(1, 4)]
        total = call(add_body, (), (total, *others), shape((16, 2 * full), BF16))
    with jax.named_scope("back"):
        back_self = call(
            back_body, (rep,), (*weights_in, grad_pre), [piece32] * reps, [pltpu.VMEM((full, width), F32)], 1.0
        )
    back_in = exchange(back_self)
    out_in = exchange(out_pieces, -1)
    with jax.named_scope("near_back"):
        near_back, output = call(
            near_back_body, (rep, cols), (*scaled_in, *back_in, *out_in, local_tiles),
            [shape((chans, nodes), F32), shape((chans, nodes), BF16)], [pltpu.VMEM((chans, nodes), BF16)], 2.0,
        )
    total, near_back, output = lax.optimization_barrier((total, near_back, output))
    with jax.named_scope("spread"):
        own = call(
            stack_body, (), [move(total, 0, dz, 0, True) for dz in range(1, 5)], shape((64, 2 * full), BF16), (), 0.5
        )
        other = move(own, 0, 0, 1)
    with jax.named_scope("home"):
        grad_feats = call(
            home_body, (sends,), (returned, near_back), shape((chans, nodes), BF16), [wide32, wide32, sem], 3.0, (1,)
        )
    with jax.named_scope("join"):
        other, grad_feats = lax.optimization_barrier((other, grad_feats))
        wg_self, wg_neigh = call(
            join_body, (rep,), (total, own, other), [shape((chans, full), F32)] * 2, [pltpu.VMEM((8, 16, 2 * full), F32)]
        )
    return output, grad_feats, wg_self.T, wg_neigh.T


def solution(mesh):
    placed = (
        P("rep", "dom"),
        P(None, "rep"),
        P(None, "rep"),
        P("dom", None),
        P("dom", None, None, None),
        P("dom", None, None),
        P("dom", None, None),
        P("dom", None, None, None, None),
        P("rep", "dom"),
    )
    return jax.shard_map(
        local,
        mesh=mesh,
        in_specs=placed,
        out_specs=(P("rep", "dom"), P("rep", "dom"), P(None, "rep"), P(None, "rep")),
        check_vma=False,
    )
```
